32 devices in a mesh: cuts: 2 (over x), region: 16 (over z, y, core).
Axes of the slice: x: 2, y: 2, z: 4, core: 2. Of those that a mesh axis runs over, the one named last changes fastest.
Arguments:
- objects: float32 [2, 2, 4096, 1024], P('cuts', None, 'region'), may hold values from -4 to 4
- probes: bfloat16 [4, 2, 256, 256], replicated, may hold values from -4 to 4
- amplitudes: float32 [64, 256, 256], P('region'), may hold values from 0.2 to 2.5
- prop_phase: float32 [256, 256], replicated, may hold values from -3.140625 to 3.140625
- scan_rows: int32 [64], P('region'), may hold values from -128 to 128, as said below
- scan_cols: int32 [64], P('region'), may hold values from 0 to 768
- probe_choice: int32 [64], P('region'), may hold values from 0 to 3
Outputs:
- gradient: float32 [2, 2, 4096, 1024], P('cuts', None, 'region')
The draws below stay inside these ranges and needn't reach their ends.
Inputs may be any that keep to these rules, and one draw needn't show every extreme that they name: `scan_rows`: in every region, half of the positions start between 64 and 128 rows above the band's first row, and the other half end between 64 and 128 rows below its last row.
All inputs are finite; a program needn't handle non-finite values.
Results may differ from the reference program's by a relative error of at most 0.039.
Values may be sent and summed in bfloat16 or wider, within the bound.
A program may use at most 64 MiB of HBM per device.

```python
import math
import jax
import jax.numpy as jnp
from jax import lax

PATCH = 256
HALO = 128
SLICES = 2
BATCHES = 4
PER_BATCH = 1
PROBES = 4
ROWS = 256
COLS = 1024
POS_DEV = 4
NPOS = 64
NROWS = 4096


def draw_scan_rows(key, part):
    key_order = jax.random.fold_in(key, 11)
    key_upper = jax.random.fold_in(key, 12)
    key_lower = jax.random.fold_in(key, 13)
    regions = NPOS // POS_DEV
    upper_rows = jax.random.randint(key_upper, (regions, POS_DEV), -HALO, -(HALO // 2) + 1, dtype=jnp.int32)
    lower_rows = jax.random.randint(key_lower, (regions, POS_DEV), ROWS - PATCH + HALO // 2, ROWS - PATCH + HALO + 1, dtype=jnp.int32)
    scores = jax.random.randint(key_order, (regions, POS_DEV), 0, 1 << 20, dtype=jnp.int32) * POS_DEV + jnp.arange(POS_DEV, dtype=jnp.int32)[None, :]
    ranking = jnp.argsort(jnp.argsort(scores, axis=1), axis=1)
    return jnp.where(ranking < POS_DEV // 2, upper_rows, lower_rows).astype(jnp.int32).reshape(-1)


def touch_ends(values, key, least, largest):
    dims = values.shape
    index_at = [jax.random.randint(jax.random.fold_in(key, axis), (), 0, dims[axis]) for axis in range(len(dims))]
    values = values.at[tuple(index_at)].set(least)
    longest = dims.index(max(dims))
    index_at[longest] = (index_at[longest] + 1) % dims[longest]
    return values.at[tuple(index_at)].set(largest)


def steps_of(rng, dims, cuts, least, top_value):
    def one(dim, shards_of):
        draws = jax.random.uniform(jax.random.fold_in(jax.random.fold_in(rng, 6), dim), (shards_of,), jnp.float32, least / len(cuts), top_value / len(cuts))
        return jnp.repeat(jnp.exp(draws), dims[dim] // shards_of).reshape((-1,) + (1,) * (len(dims) - dim - 1))

    level = one(*cuts[0])
    for cut in cuts[1:]:
        level = level * one(*cut)
    return level


def gaussian(own_key, shape, width, most, split=(), held_as=jnp.bfloat16):
    drawn = jax.random.normal(own_key, shape, jnp.float32) * width
    if len(split) > 0:
        drawn = steps_of(own_key, shape, split, -0.22, 0.18) * drawn
    return jnp.clip(drawn, min=-most, max=most).astype(held_as)


def setup_inputs(seed: int = 0) -> dict:
    key_list = jax.random.split(jax.random.key(seed), 8)
    objects = gaussian(key_list[0], (SLICES, 2, NROWS, COLS), 0.7, 4.0, ((0, 2), (2, 16)), jnp.float32)
    probes = gaussian(key_list[1], (PROBES, 2, PATCH, PATCH), 0.7, 4.0)
    amplitudes = jnp.clip(jnp.exp(math.log(2.5) - 2.5257286 * jax.random.uniform(key_list[2], (NPOS, PATCH, PATCH), jnp.float32) ** steps_of(key_list[2], (NPOS, PATCH, PATCH), ((0, 16),), -0.2, 0.2)), 0.2, 2.5)
    prop_phase = jnp.clip(jax.random.uniform(key_list[3], (PATCH, PATCH), jnp.float32, -3.140625, 3.140625), -3.140625, 3.140625)
    scan_rows = draw_scan_rows(jax.random.fold_in(key_list[7], 71), 0)
    scan_cols = touch_ends(jax.random.randint(key_list[5], (NPOS,), 0, COLS - PATCH + 1), jax.random.fold_in(key_list[5], 1), 0, COLS - PATCH).astype(jnp.int32)
    probe_choice = touch_ends(jax.random.randint(key_list[6], (NPOS,), 0, PROBES), jax.random.fold_in(key_list[6], 1), 0, PROBES - 1).astype(jnp.int32)
    return {"objects": objects, "probes": probes, "amplitudes": amplitudes, "prop_phase": prop_phase, "scan_rows": scan_rows, "scan_cols": scan_cols, "probe_choice": probe_choice}


modulus_floor = 0.25

def widened(narrow):
    return lax.optimization_barrier(narrow).astype(jnp.float32)

def dft_tables(length, direction):
    indices = jnp.arange(length, dtype=jnp.int32)
    product = indices[:, None] * indices[None, :] % length
    angles = product.astype(jnp.float32) * (2.0 * jnp.pi / length)
    scaling = 1.0 / jnp.sqrt(jnp.float32(length))
    return jnp.stack([jnp.cos(angles) * scaling, direction * jnp.sin(angles) * scaling]).astype(jnp.bfloat16)

def complex_join(part_stack):
    return jnp.stack([part_stack[0, :, 0] - part_stack[1, :, 1], part_stack[0, :, 1] + part_stack[1, :, 0]], axis=1)

def transform(input_field, dft_table):
    wide_table = dft_table.astype(jnp.float32)
    narrow_field = widened(input_field.astype(jnp.bfloat16))
    left_part = jnp.einsum('ajk,nckl->ancjl', wide_table, narrow_field)
    middle = widened(complex_join(left_part).astype(jnp.bfloat16))
    right_part = jnp.einsum('nckl,alm->anckm', middle, wide_table)
    return complex_join(right_part)

def multiply_complex(left_field, right_field):
    real_part = left_field[..., 0, :, :] * right_field[..., 0, :, :] - left_field[..., 1, :, :] * right_field[..., 1, :, :]
    imag_part = left_field[..., 0, :, :] * right_field[..., 1, :, :] + left_field[..., 1, :, :] * right_field[..., 0, :, :]
    return jnp.stack([real_part, imag_part], axis=-3)

def multiply_conjugate(left_field, right_field):
    real_part = left_field[..., 0, :, :] * right_field[..., 0, :, :] + left_field[..., 1, :, :] * right_field[..., 1, :, :]
    imag_part = left_field[..., 0, :, :] * right_field[..., 1, :, :] - left_field[..., 1, :, :] * right_field[..., 0, :, :]
    return jnp.stack([real_part, imag_part], axis=-3)

def propagate(input_field, optics):
    propagator, forward_table, inverse_table = optics
    return transform(multiply_complex(propagator, transform(input_field, forward_table)), inverse_table)

def propagate_adjoint(input_field, optics):
    propagator, forward_table, inverse_table = optics
    return transform(multiply_conjugate(propagator, transform(input_field, forward_table)), inverse_table)

def reference(objects, probes, amplitudes, prop_phase, scan_rows, scan_cols, probe_choice):
    slice_count = objects.shape[0]
    total_rows = objects.shape[2]
    rim_depth = PATCH // 2
    per_region = BATCHES * PER_BATCH
    optics = (jnp.stack([jnp.cos(prop_phase), jnp.sin(prop_phase)]), dft_tables(PATCH, -1.0), dft_tables(PATCH, 1.0))
    zero_index = jnp.zeros((), jnp.int32)
    window_steps = jnp.arange(PATCH, dtype=jnp.int32)

    def visit_position(running, position):
        region = position // per_region
        top_row = (region * ROWS + scan_rows[position]).astype(jnp.int32)
        left_col = scan_cols[position].astype(jnp.int32)
        row_ids = ((top_row + total_rows + window_steps) % total_rows).astype(jnp.int32)
        band_part = jnp.take(objects, row_ids, axis=2)
        window = lax.dynamic_slice(band_part, (zero_index, zero_index, zero_index, left_col), (slice_count, 2, PATCH, PATCH))
        current = probes[probe_choice[position]][None]
        measured = amplitudes[position][None]
        stored = []
        for slice_index in range(slice_count):
            stored.append(current)
            exit_field = multiply_complex(widened(current), window[slice_index][None])
            if slice_index < slice_count - 1:
                current = propagate(exit_field, optics).astype(jnp.bfloat16)
            else:
                far_field = transform(exit_field, optics[1])
                modulus = jnp.sqrt(far_field[:, 0] * far_field[:, 0] + far_field[:, 1] * far_field[:, 1])
                factor = 1.0 - measured / jnp.maximum(modulus, modulus_floor)
                current = transform(far_field * factor[:, None], optics[2]).astype(jnp.bfloat16)
        pieces = [None] * slice_count
        for slice_index in reversed(range(slice_count)):
            arriving = widened(current)
            pieces[slice_index] = multiply_conjugate(widened(stored[slice_index]), arriving)[0]
            if slice_index > 0:
                backward = multiply_conjugate(window[slice_index][None], arriving)
                current = propagate_adjoint(backward, optics).astype(jnp.bfloat16)
        deposit_block = jnp.stack(pieces)
        corner = (zero_index, zero_index, (top_row + rim_depth).astype(jnp.int32), left_col)
        existing = lax.dynamic_slice(running, corner, deposit_block.shape)
        return (lax.dynamic_update_slice(running, existing + deposit_block, corner), None)
    padded_shape = (slice_count, 2, total_rows + 2 * rim_depth, objects.shape[3])
    summed, unused = lax.scan(visit_position, jnp.zeros(padded_shape, jnp.float32), jnp.arange(NPOS, dtype=jnp.int32))
    gradient = summed[:, :, rim_depth:rim_depth + total_rows]
    gradient = gradient.at[:, :, :rim_depth].add(summed[:, :, total_rows + rim_depth:])
    gradient = gradient.at[:, :, total_rows - rim_depth:].add(summed[:, :, :rim_depth])
    return gradient
```

```python
import functools
import jax
import jax.numpy as jnp
import numpy as np
from jax import lax
from jax.experimental import pallas as pl
from jax.experimental.pallas import tpu as pltpu
from jax.sharding import PartitionSpec as P

modulus_floor = 0.25
LANES = 128
SUBLANES = 8
VMEM = pl.BlockSpec(memory_space=pltpu.VMEM)
SMEM = pl.BlockSpec(memory_space=pltpu.SMEM)
LIMIT = pltpu.CompilerParams(vmem_limit_bytes=60000 * 1024)


def dft_blocks(side):
    indices = np.arange(side)
    angles = (indices[:, None] * indices[None, :] % side) * (2.0 * np.pi / side)
    real = np.cos(angles) / np.sqrt(side)
    imag = np.sin(angles) / np.sqrt(side)
    tables = [np.block([[real, imag], [-imag, real]]), np.block([[real, -imag], [imag, real]])]
    return jnp.asarray(np.stack(tables), dtype=jnp.bfloat16)


def split_col(col, cols, side):
    base = jnp.minimum(lax.div(col, LANES), (cols - side) // LANES - 1) * LANES
    return base, col - base


def cut_window(ext, plane, row, col, height, side):
    base, shift = split_col(col, ext.shape[2], side)
    top = lax.div(row, SUBLANES) * SUBLANES
    tall = height + SUBLANES
    block = ext[plane, pl.ds(top, tall), pl.ds(base, side + LANES)]
    block = pltpu.roll(block, lax.rem(tall + top - row, tall), axis=0)[:height]
    back = lax.rem(LANES - shift + LANES, LANES)
    chunks = [
        pltpu.roll(block[:, j : j + LANES], back, axis=1) for j in range(0, side + LANES, LANES)
    ]
    lane = lax.broadcasted_iota(jnp.int32, (height, LANES), 1)
    keep = lane < LANES - shift
    return jnp.concatenate(
        [jnp.where(keep, chunks[j], chunks[j + 1]) for j in range(len(chunks) - 1)], axis=1
    )


def add_window(grad, plane, row, col, field):
    height, side = field.shape
    base, shift = split_col(col, grad.shape[2], side)
    top = lax.div(row, SUBLANES) * SUBLANES
    tall = height + SUBLANES
    field = jnp.concatenate([field, jnp.zeros((SUBLANES, side), field.dtype)], axis=0)
    field = pltpu.roll(field, row - top, axis=0)
    ahead = lax.rem(shift, LANES)
    chunks = [pltpu.roll(field[:, j : j + LANES], ahead, axis=1) for j in range(0, side, LANES)]
    lane = lax.broadcasted_iota(jnp.int32, (tall, LANES), 1)
    keep = lane >= shift
    zero = jnp.zeros((tall, LANES), field.dtype)
    parts = [zero] + chunks + [zero]
    placed = jnp.concatenate(
        [jnp.where(keep, parts[j + 1], parts[j]) for j in range(len(chunks) + 1)], axis=1
    )
    where = (plane, pl.ds(top, tall), pl.ds(base, side + LANES))
    grad[where] = grad[where] + placed


def dot(left, right):
    return jnp.dot(left, right, preferred_element_type=jnp.float32)


def transform(field, tables, which):
    side = field[0].shape[0]
    stacked = jnp.concatenate([field[0].astype(jnp.bfloat16), field[1].astype(jnp.bfloat16)], axis=0)
    middle = dot(tables[which], stacked).astype(jnp.bfloat16)
    beside = jnp.concatenate([middle[:side], middle[side:]], axis=1)
    result = dot(beside, tables[1 - which])
    return result[:, :side], result[:, side:]


def multiply(left, right):
    return left[0] * right[0] - left[1] * right[1], left[0] * right[1] + left[1] * right[0]


def multiply_conjugate(left, right):
    return left[0] * right[0] + left[1] * right[1], left[0] * right[1] - left[1] * right[0]


def narrowed(field):
    return tuple(part.astype(jnp.bfloat16).astype(jnp.float32) for part in field)


def one_position(psi0, object0, object1, measured, wave, tables):
    psi1 = narrowed(
        transform(multiply(wave, transform(multiply(psi0, object0), tables, 0)), tables, 1)
    )
    far = transform(multiply(psi1, object1), tables, 0)
    modulus = jnp.sqrt(far[0] * far[0] + far[1] * far[1])
    factor = 1.0 - measured / jnp.maximum(modulus, modulus_floor)
    g1 = narrowed(transform((far[0] * factor, far[1] * factor), tables, 1))
    d1 = multiply_conjugate(psi1, g1)
    back = transform(multiply_conjugate(object1, g1), tables, 0)
    g0 = narrowed(transform(multiply_conjugate(wave, back), tables, 1))
    return multiply_conjugate(psi0, g0), d1


def wide(ref, *index):
    return ref[index + (0,)].astype(jnp.float32), ref[index + (1,)].astype(jnp.float32)


def find(rows, upper, rank):
    seen = jnp.int32(0)
    chosen = jnp.int32(0)
    for position in range(rows.shape[0]):
        here = jnp.where(rows[position] < 0, 1, 0) == upper
        chosen = jnp.where(jnp.logical_and(here, seen == rank), position, chosen)
        seen = seen + jnp.where(here, 1, 0)
    return chosen


def corner(info, upper, rank):
    position = find(info[0], upper, rank)
    return info[0][position], info[1][position]


class Step:
    def __init__(self, index, region, count, side, band_rows):
        self.index = index
        even = 1 - lax.rem(region, 2)
        self.upper = 1 - even if index == 0 else even
        before = lax.rem(region + count - 1, count)
        after = lax.rem(region + 1, count)
        self.peer = jnp.where(self.upper == 1, before, after)
        half = side // 2
        self.near_low = pl.multiple_of(self.upper * half, half)
        self.far_low = pl.multiple_of((1 - self.upper) * half, half)
        self.peer_upper = 1 - self.upper
        self.peer_offset = (2 * self.peer_upper - 1) * band_rows
        self.peer_far_low = self.near_low
        self.wraps = jnp.logical_and(self.upper == 1, region == 0) | jnp.logical_and(
            self.upper == 0, region == count - 1
        )


def wave_kernel(
    side, count, scans, choice_any, band, probes_any, amps_any, phase_any, tables_any,
    coords, keep, give_in, far_back,
    ext, probes, amps, phase, wave, tables,
    x_send, x_in, far_send, far_in, own, give,
    here, around, choice,
    local_sem, send_sem, recv_sem,
):
    rim = side // 2
    band_rows = band.shape[1]
    c = lax.axis_index("cuts")
    region = lax.axis_index("region")
    other_cut = 1 - c
    steps = [Step(s, region, count, side, band_rows) for s in range(2)]
    loads = [
        pltpu.make_async_copy(source, target, local_sem.at[k])
        for k, (source, target) in enumerate((
            (scans[0], here[0]), (scans[1], here[1]),
            (band, ext.at[:, pl.ds(rim, band_rows)]), (choice_any, choice), (phase_any, phase),
            (tables_any, tables), (probes_any, probes), (amps_any, amps),
        ))
    ]
    for load in loads:
        load.start()
    barrier = pltpu.get_barrier_semaphore()
    peers = [(other_cut, region)] + [(c, step.peer) for step in steps]
    for peer in peers:
        pl.semaphore_signal(barrier, 1, device_id=peer, device_id_type=pl.DeviceIdType.MESH)
    pl.semaphore_wait(barrier, len(peers))
    slots = iter(range(24))

    def remote(source, target, peer):
        slot = next(slots)
        return pltpu.make_async_remote_copy(
            src_ref=source, dst_ref=target,
            send_sem=send_sem.at[slot], recv_sem=recv_sem.at[slot],
            device_id=peer, device_id_type=pl.DeviceIdType.MESH,
        )

    across = (other_cut, region)
    notes = [
        [remote(scans[k], around[s][k], (c, steps[s].peer)) for k in range(2)] for s in range(2)
    ]
    near = [pl.ds(step.near_low, rim) for step in steps]
    far = [pl.ds(step.far_low, rim) for step in steps]
    x_near = [remote(x_send.at[s, :, near[s]], x_in.at[s, :, near[s]], across) for s in range(2)]
    x_far = [remote(x_send.at[s, :, far[s]], x_in.at[s, :, far[s]], across) for s in range(2)]
    halo = [
        [remote(far_send.at[s, j], far_in.at[s, j], (c, steps[s].peer)) for j in range(2)]
        for s in range(2)
    ]
    give_far = [remote(give.at[s, :, far[s]], give_in.at[s, :, far[s]], across) for s in range(2)]
    give_near = [remote(give.at[s, :, near[s]], give_in.at[s, :, near[s]], across) for s in range(2)]
    back_own = [
        remote(keep.at[s, :, far[s]], far_back.at[s, 0], (c, steps[s].peer)) for s in range(2)
    ]
    back_other = [
        remote(give_in.at[s, :, far[s]], far_back.at[s, 1], (c, steps[s].peer)) for s in range(2)
    ]
    for pair in notes:
        for note in pair:
            note.start()
    for load in loads[:3]:
        load.wait()

    ids = lax.broadcasted_iota(jnp.int32, (rim, side), 0)

    def cut_far(s, rank):
        step = steps[s]
        row, col = corner(around[s], step.peer_upper, rank)
        top = row + step.peer_offset + step.peer_far_low + rim
        return [cut_window(ext, plane, top, col, rim, side) for plane in range(2)]

    def mixed(s, rank, j, plane):
        step = steps[s]
        row, col = corner(here, step.upper, rank)
        held = cut_window(ext, plane, row + rim + step.far_low, col, rim, side)
        rows = ids + (row + step.far_low)
        outside = jnp.logical_or(rows < 0, rows >= band_rows)
        return jnp.where(outside, far_in[s, j, plane].astype(jnp.float32), held)

    def near_half(s, rank, plane):
        step = steps[s]
        row, col = corner(here, step.upper, rank)
        return cut_window(ext, plane, row + rim + step.near_low, col, rim, side)

    def send_near(s):
        for plane in range(2):
            x_send[s, plane, near[s]] = near_half(s, other_cut, plane).astype(jnp.bfloat16)
        x_near[s].start()

    def send_halo(s):
        for note in notes[s]:
            note.wait()
        for j, rank in enumerate((other_cut, c)):
            for plane, part in enumerate(cut_far(s, rank)):
                far_send[s, j, plane] = part.astype(jnp.bfloat16)
            halo[s][j].start()

    def send_far(s):
        halo[s][0].wait_recv()
        for plane in range(2):
            x_send[s, plane, far[s]] = mixed(s, other_cut, 0, plane).astype(jnp.bfloat16)
        x_far[s].start()

    def gather_own(s):
        halo[s][1].wait_recv()
        for plane in range(2):
            own[s, plane, near[s]] = near_half(s, c, plane)
            own[s, plane, far[s]] = mixed(s, c, 1, plane)

    send_near(0)
    send_halo(0)
    send_far(0)
    send_near(1)
    send_halo(1)
    for load in loads[3:]:
        load.wait()
    wave[0] = jnp.cos(phase[...])
    wave[1] = jnp.sin(phase[...])
    for k, (s, rank) in enumerate(((0, c), (0, other_cut), (1, c), (1, other_cut))):
        row, col = corner(here, steps[s].upper, rank)
        coords[2 * k] = row
        coords[2 * k + 1] = col
    for k, (s, rank) in enumerate(((0, c), (0, other_cut), (1, c), (1, other_cut))):
        row, col = corner(around[s], steps[s].peer_upper, rank)
        coords[8 + 2 * k] = row + steps[s].peer_offset + steps[s].peer_far_low
        coords[9 + 2 * k] = col
    gather_own(0)
    first = c == 0

    @pl.when(jnp.logical_not(steps[1].wraps))
    def _():
        send_far(1)

    for s in range(2):
        step = steps[s]
        position = find(here[0], step.upper, c)
        psi0 = wide(probes, choice[position])
        x_near[s].wait_recv()
        x_far[s].wait_recv()
        mine = tuple(own[s, plane] for plane in range(2))
        theirs = tuple(x_in[s, plane].astype(jnp.float32) for plane in range(2))
        object0 = tuple(jnp.where(first, x, y) for x, y in zip(mine, theirs))
        object1 = tuple(jnp.where(first, y, x) for x, y in zip(mine, theirs))
        d0, d1 = one_position(psi0, object0, object1, amps[position], (wave[0], wave[1]), tables)
        for plane in range(2):
            give[s, plane] = jnp.where(first, d1[plane], d0[plane]).astype(jnp.bfloat16)
        give_far[s].start()
        give_near[s].start()
        for plane in range(2):
            keep[s, plane] = jnp.where(first, d0[plane], d1[plane]).astype(jnp.bfloat16)
        back_own[s].start()
        if s == 0:

            @pl.when(steps[1].wraps)
            def _():
                send_far(1)

            gather_own(1)
    for s in range(2):
        give_far[s].wait_recv()
        back_other[s].start()
    for copy in x_near + x_far + halo[0] + halo[1] + give_far:
        copy.wait_send()
    for copy in give_near + back_own + back_other:
        copy.wait()


def deposit_kernel(side, coords, keep, give_in, far_back, out, grad, out_sem):
    rim = side // 2
    quarter = side // 4
    band_rows = out.shape[1]
    region = lax.axis_index("region")
    grad[...] = jnp.zeros_like(grad)
    stores = []
    for plane in range(2):
        for s in range(2):
            even = 1 - lax.rem(region, 2)
            upper = 1 - even if s == 0 else even
            low = pl.multiple_of(upper * quarter, quarter)
            rows = pl.ds(low, side - quarter)
            parts = [
                (keep[s, plane, rows], coords[4 * s] + low, coords[4 * s + 1]),
                (give_in[s, plane, rows], coords[4 * s + 2] + low, coords[4 * s + 3]),
                (far_back[s, 0, plane], coords[8 + 4 * s], coords[9 + 4 * s]),
                (far_back[s, 1, plane], coords[10 + 4 * s], coords[11 + 4 * s]),
            ]
            for part, row, col in parts:
                add_window(grad, plane, row + rim, col, part.astype(jnp.float32))
        stores.append(
            pltpu.make_async_copy(
                grad.at[plane, pl.ds(rim, band_rows)], out.at[plane], out_sem.at[plane]
            )
        )
        stores[-1].start()
    for store in stores:
        store.wait()


def shards(objects, probes, amplitudes, prop_phase, scan_rows, scan_cols, probe_choice):
    side = probes.shape[-1]
    rim = side // 2
    count = lax.axis_size("region")
    band = objects[0]
    band_rows, columns = band.shape[1:]
    tables = dft_blocks(side)
    whole = (2, 2, side, side)
    half = (2, 2, 2, rim, side)
    held = lambda shape: jax.ShapeDtypeStruct(shape, jnp.bfloat16)
    slot = lambda shape: pltpu.VMEM(shape, jnp.bfloat16)
    tall = pltpu.VMEM((2, band_rows + 2 * rim + SUBLANES, columns), jnp.float32)
    ANY = pl.BlockSpec(memory_space=pl.ANY)
    scalars = pltpu.SMEM(scan_rows.shape, jnp.int32)
    coords, keep, give_in, far_back = pl.pallas_call(
        functools.partial(wave_kernel, side, count),
        out_shape=(jax.ShapeDtypeStruct((16,), jnp.int32), held(whole), held(whole), held(half)),
        in_specs=[(ANY, ANY)] + [ANY] * 6,
        out_specs=(SMEM, VMEM, VMEM, VMEM),
        scratch_shapes=[
            tall,
            pltpu.VMEM(probes.shape, probes.dtype),
            pltpu.VMEM(amplitudes.shape, amplitudes.dtype),
            pltpu.VMEM(prop_phase.shape, jnp.float32),
            pltpu.VMEM((2,) + prop_phase.shape, jnp.float32),
            pltpu.VMEM(tables.shape, tables.dtype),
            slot(whole), slot(whole), slot(half), slot(half),
            pltpu.VMEM(whole, jnp.float32), slot(whole),
            (scalars,) * 2, ((scalars,) * 2,) * 2, scalars,
            pltpu.SemaphoreType.DMA((8,)),
            pltpu.SemaphoreType.DMA((24,)),
            pltpu.SemaphoreType.DMA((24,)),
        ],
        compiler_params=pltpu.CompilerParams(
            collective_id=0, has_side_effects=True, vmem_limit_bytes=60000 * 1024
        ),
    )((scan_rows, scan_cols), probe_choice, band, probes, amplitudes, prop_phase, tables)
    out = pl.pallas_call(
        functools.partial(deposit_kernel, side),
        out_shape=jax.ShapeDtypeStruct(band.shape, jnp.float32),
        in_specs=[SMEM] + [VMEM] * 3,
        out_specs=ANY,
        scratch_shapes=[tall, pltpu.SemaphoreType.DMA((2,))],
        compiler_params=LIMIT,
    )(coords, keep, give_in, far_back)
    return out[None]


def solution(mesh):
    return jax.shard_map(
        shards,
        mesh=mesh,
        in_specs=(
            P("cuts", None, "region", None),
            P(),
            P("region", None, None),
            P(),
            P("region"),
            P("region"),
            P("region"),
        ),
        out_specs=P("cuts", None, "region", None),
        check_vma=False,
    )
```

```python
import contextlib
import functools
import jax
import jax.numpy as jnp
import numpy as np
from jax import lax
from jax.experimental import pallas as pl
from jax.experimental.pallas import tpu as pltpu
from jax.sharding import PartitionSpec as P

modulus_floor = 0.25
LANES = 128
SUBLANES = 8
VMEM = pl.BlockSpec(memory_space=pltpu.VMEM)
SMEM = pl.BlockSpec(memory_space=pltpu.SMEM)
LIMIT = pltpu.CompilerParams(vmem_limit_bytes=16 * 1024 * 1024)


def mark(name):
    return contextlib.nullcontext()


def dft_blocks(side):
    half = side // 2
    indices = np.arange(side)
    angles = (indices[:, None] * indices[None, :] % side) * (2.0 * np.pi / side)
    real = np.cos(angles) / np.sqrt(side)
    imag = np.sin(angles) / np.sqrt(side)
    tables = []
    for odd in range(2):
        cos, sin = real[:half, odd::2], imag[:half, odd::2]
        tables.append(np.block([[cos.T, sin.T], [-sin.T, cos.T]]))
    for odd in range(2):
        cos, sin = real[:half, odd::2], imag[:half, odd::2]
        tables.append(np.block([[cos, -sin], [sin, cos]]))
    return jnp.asarray(np.stack(tables), dtype=jnp.bfloat16)


def split_col(col, cols, side):
    base = jnp.minimum(lax.div(col, LANES), (cols - side) // LANES - 1) * LANES
    return base, col - base


def cut_window(ext, plane, row, col, height, side):
    base, shift = split_col(col, ext.shape[2], side)
    top = lax.div(row, SUBLANES) * SUBLANES
    tall = height + SUBLANES
    block = ext[plane, pl.ds(top, tall), pl.ds(base, side + LANES)]
    block = pltpu.roll(block, lax.rem(tall + top - row, tall), axis=0)[:height]
    back = lax.rem(LANES - shift + LANES, LANES)
    chunks = [
        pltpu.roll(block[:, j : j + LANES], back, axis=1) for j in range(0, side + LANES, LANES)
    ]
    lane = lax.broadcasted_iota(jnp.int32, (height, LANES), 1)
    keep = lane < LANES - shift
    return jnp.concatenate(
        [jnp.where(keep, chunks[j], chunks[j + 1]) for j in range(len(chunks) - 1)], axis=1
    )


def add_window(grad, plane, row, col, field):
    height, side = field.shape
    base, shift = split_col(col, grad.shape[2], side)
    top = lax.div(row, SUBLANES) * SUBLANES
    tall = height + SUBLANES
    field = jnp.concatenate([field, jnp.zeros((SUBLANES, side), field.dtype)], axis=0)
    field = pltpu.roll(field, row - top, axis=0)
    ahead = lax.rem(shift, LANES)
    chunks = [pltpu.roll(field[:, j : j + LANES], ahead, axis=1) for j in range(0, side, LANES)]
    lane = lax.broadcasted_iota(jnp.int32, (tall, LANES), 1)
    keep = lane >= shift
    zero = jnp.zeros((tall, LANES), field.dtype)
    parts = [zero] + chunks + [zero]
    placed = jnp.concatenate(
        [jnp.where(keep, parts[j + 1], parts[j]) for j in range(len(chunks) + 1)], axis=1
    )
    where = (plane, pl.ds(top, tall), pl.ds(base, side + LANES))
    grad[where] = grad[where] + placed


def dot(left, right):
    return jnp.dot(left, right, preferred_element_type=jnp.float32)


def narrow(left, right, axis):
    return jnp.concatenate([left, right], axis=axis).astype(jnp.bfloat16)


def forward(field, tables):
    half = field[0].shape[0] // 2
    low, high = [part[:half] for part in field], [part[half:] for part in field]
    even = dot(tables[0], narrow(low[0] + high[0], low[1] + high[1], 0))
    odd = dot(tables[1], narrow(low[0] - high[0], low[1] - high[1], 0))
    middle = [
        jnp.concatenate([even[:half], odd[:half]], axis=0),
        jnp.concatenate([even[half:], odd[half:]], axis=0),
    ]
    low, high = [part[:, :half] for part in middle], [part[:, half:] for part in middle]
    even = dot(narrow(low[0] + high[0], low[1] + high[1], 1), tables[2])
    odd = dot(narrow(low[0] - high[0], low[1] - high[1], 1), tables[3])
    return (
        jnp.concatenate([even[:, :half], odd[:, :half]], axis=1),
        jnp.concatenate([even[:, half:], odd[:, half:]], axis=1),
    )


def inverse(field, tables):
    half = field[0].shape[0] // 2
    even = dot(tables[2], narrow(field[0][:half], field[1][:half], 0))
    odd = dot(tables[3], narrow(field[0][half:], field[1][half:], 0))
    total, rest = even + odd, even - odd
    middle = [
        jnp.concatenate([total[:half], rest[:half]], axis=0),
        jnp.concatenate([total[half:], rest[half:]], axis=0),
    ]
    even = dot(narrow(middle[0][:, :half], middle[1][:, :half], 1), tables[0])
    odd = dot(narrow(middle[0][:, half:], middle[1][:, half:], 1), tables[1])
    total, rest = even + odd, even - odd
    return (
        jnp.concatenate([total[:, :half], rest[:, :half]], axis=1),
        jnp.concatenate([total[:, half:], rest[:, half:]], axis=1),
    )


def even_first(rows):
    array = jnp.concatenate(
        [jnp.concatenate([rows(first, k) for k in range(2)], axis=1) for first in range(2)], axis=0
    )
    side = array.shape[1]
    source = lax.broadcasted_iota(jnp.int32, (side, side), 0)
    target = lax.broadcasted_iota(jnp.int32, (side, side), 1)
    wanted = jnp.where(target < side // 2, 2 * target, 2 * target - side + 1)
    pick = jnp.where(source == wanted, 1.0, 0.0).astype(jnp.bfloat16)
    total = None
    for _ in range(3):
        part = array.astype(jnp.bfloat16)
        array = array - part.astype(jnp.float32)
        moved = dot(part, pick)
        total = moved if total is None else total + moved
    return total


def turn(phase):
    x = phase * 0.5
    y = x * x
    sin = np.float32(1.0 / 6227020800.0)
    for factor in (-39916800.0, 362880.0, -5040.0, 120.0, -6.0, 1.0):
        sin = sin * y + np.float32(1.0 / factor)
    sin = sin * x
    cos = np.float32(-1.0 / 87178291200.0)
    for factor in (479001600.0, -3628800.0, 40320.0, -720.0, 24.0, -2.0, 1.0):
        cos = cos * y + np.float32(1.0 / factor)
    return 1.0 - 2.0 * sin * sin, 2.0 * sin * cos


def multiply(left, right):
    return left[0] * right[0] - left[1] * right[1], left[0] * right[1] + left[1] * right[0]


def multiply_conjugate(left, right):
    return left[0] * right[0] + left[1] * right[1], left[0] * right[1] - left[1] * right[0]


def narrowed(field):
    return tuple(part.astype(jnp.bfloat16).astype(jnp.float32) for part in field)


def one_position(psi0, object0, object1, measured, wave, tables):
    psi1 = narrowed(
        inverse(multiply(wave, forward(multiply(psi0, object0), tables)), tables)
    )
    far = forward(multiply(psi1, object1), tables)
    modulus = jnp.sqrt(far[0] * far[0] + far[1] * far[1])
    factor = 1.0 - measured / jnp.maximum(modulus, modulus_floor)
    g1 = narrowed(inverse((far[0] * factor, far[1] * factor), tables))
    d1 = multiply_conjugate(psi1, g1)
    back = forward(multiply_conjugate(object1, g1), tables)
    g0 = narrowed(inverse(multiply_conjugate(wave, back), tables))
    return multiply_conjugate(psi0, g0), d1


def wide(ref, *index):
    return ref[index + (0,)].astype(jnp.float32), ref[index + (1,)].astype(jnp.float32)


def find(rows, upper, rank):
    seen = jnp.int32(0)
    chosen = jnp.int32(0)
    for position in range(rows.shape[0]):
        here = jnp.where(rows[position] < 0, 1, 0) == upper
        chosen = jnp.where(jnp.logical_and(here, seen == rank), position, chosen)
        seen = seen + jnp.where(here, 1, 0)
    return chosen


def corner(info, upper, rank):
    position = find(info[0], upper, rank)
    return info[0][position], info[1][position]


class Step:
    def __init__(self, index, region, count, side, band_rows):
        self.index = index
        even = 1 - lax.rem(region, 2)
        self.upper = 1 - even if index == 0 else even
        before = lax.rem(region + count - 1, count)
        after = lax.rem(region + 1, count)
        self.peer = jnp.where(self.upper == 1, before, after)
        half = side // 2
        self.near_low = pl.multiple_of(self.upper * half, half)
        self.far_low = pl.multiple_of((1 - self.upper) * half, half)
        self.peer_upper = 1 - self.upper
        self.peer_offset = (2 * self.peer_upper - 1) * band_rows
        self.peer_far_low = self.near_low
        self.wraps = jnp.logical_and(self.upper == 1, region == 0) | jnp.logical_and(
            self.upper == 0, region == count - 1
        )


def wave_kernel(
    side, count, scans, choice_any, band, probes_any, amps_any, phase_any, tables_any,
    coords, keep_out, give_in, far_back,
    ext, probes, amps, phase, wave, tables, measured,
    x_send, x_in, far_send, far_in, own, give, keep,
    here, around, choice,
    local_sem, keep_sem, send_sem, recv_sem,
):
    rim = side // 2
    band_rows = band.shape[1]
    c = lax.axis_index("cuts")
    region = lax.axis_index("region")
    other_cut = 1 - c
    steps = [Step(s, region, count, side, band_rows) for s in range(2)]
    loads = [
        pltpu.make_async_copy(source, target, local_sem.at[k])
        for k, (source, target) in enumerate((
            (scans[0], here[0]), (scans[1], here[1]),
            (band, ext.at[:, pl.ds(rim, band_rows)]), (choice_any, choice),
            (tables_any, tables), (probes_any, probes),
            *((phase_any.at[:, pl.ds(k * rim, rim)], phase.at[k]) for k in range(2)),
            *((amps_any.at[:, :, pl.ds(k * rim, rim)], amps.at[k]) for k in range(2)),
        ))
    ]
    for load in loads:
        load.start()
    barrier = pltpu.get_barrier_semaphore()
    peers = [(other_cut, region)] + [(c, step.peer) for step in steps]
    for peer in peers:
        pl.semaphore_signal(barrier, 1, device_id=peer, device_id_type=pl.DeviceIdType.MESH)
    with mark("bar"):
        pl.semaphore_wait(barrier, len(peers))
    slots = iter(range(24))

    def remote(source, target, peer):
        slot = next(slots)
        return pltpu.make_async_remote_copy(
            src_ref=source, dst_ref=target,
            send_sem=send_sem.at[slot], recv_sem=recv_sem.at[slot],
            device_id=peer, device_id_type=pl.DeviceIdType.MESH,
        )

    across = (other_cut, region)
    notes = [
        [remote(scans[k], around[s][k], (c, steps[s].peer)) for k in range(2)] for s in range(2)
    ]
    near = [pl.ds(step.near_low, rim) for step in steps]
    far = [pl.ds(step.far_low, rim) for step in steps]
    x_near = [remote(x_send.at[s, :, near[s]], x_in.at[s, :, near[s]], across) for s in range(2)]
    x_far = [remote(x_send.at[s, :, far[s]], x_in.at[s, :, far[s]], across) for s in range(2)]
    halo = [
        [remote(far_send.at[s, j], far_in.at[s, j], (c, steps[s].peer)) for j in range(2)]
        for s in range(2)
    ]
    give_far = [remote(give.at[s, :, far[s]], give_in.at[s, :, far[s]], across) for s in range(2)]
    give_near = []
    for s in range(2):
        rows = [pl.ds(pl.multiple_of(steps[s].near_low + k * rim // 2, rim // 2), rim // 2) for k in range(2)]
        give_near.append(
            [remote(give.at[s, :, part], give_in.at[s, :, part], across) for part in rows]
        )
    keeps = [pltpu.make_async_copy(keep.at[s], keep_out.at[s], keep_sem.at[s]) for s in range(2)]
    back_own = [
        remote(keep.at[s, :, far[s]], far_back.at[s, 0], (c, steps[s].peer)) for s in range(2)
    ]
    back_other = [
        remote(give_in.at[s, :, far[s]], far_back.at[s, 1], (c, steps[s].peer)) for s in range(2)
    ]
    for pair in notes:
        for note in pair:
            note.start()
    with mark("band"):
        for load in loads[:3]:
            load.wait()

    ids = lax.broadcasted_iota(jnp.int32, (rim, side), 0)

    def cut_far(s, rank):
        step = steps[s]
        row, col = corner(around[s], step.peer_upper, rank)
        top = row + step.peer_offset + step.peer_far_low + rim
        return [cut_window(ext, plane, top, col, rim, side) for plane in range(2)]

    def mixed(s, rank, j, plane):
        step = steps[s]
        row, col = corner(here, step.upper, rank)
        held = cut_window(ext, plane, row + rim + step.far_low, col, rim, side)
        rows = ids + (row + step.far_low)
        outside = jnp.logical_or(rows < 0, rows >= band_rows)
        return jnp.where(outside, far_in[s, j, plane].astype(jnp.float32), held)

    def near_half(s, rank, plane):
        step = steps[s]
        row, col = corner(here, step.upper, rank)
        return cut_window(ext, plane, row + rim + step.near_low, col, rim, side)

    def cut_near(s):
        for plane in range(2):
            x_send[s, plane, near[s]] = near_half(s, other_cut, plane).astype(jnp.bfloat16)

    def cut_halo(s, j):
        for plane, part in enumerate(cut_far(s, (other_cut, c)[j])):
            far_send[s, j, plane] = part.astype(jnp.bfloat16)

    def send_far(s):
        with mark("wh0"):
            halo[s][0].wait_recv()
        for plane in range(2):
            x_send[s, plane, far[s]] = mixed(s, other_cut, 0, plane).astype(jnp.bfloat16)
        x_far[s].start()

    def gather_own(s):
        with mark("wh1"):
            halo[s][1].wait_recv()
        for plane in range(2):
            own[s, plane, near[s]] = near_half(s, c, plane)
            own[s, plane, far[s]] = mixed(s, c, 1, plane)

    with mark("near0"):
        cut_near(0)
        x_near[0].start()
    for s in range(2):
        with mark("wnote"):
            for note in notes[s]:
                note.wait()
        if s == 0:
            for j in range(2):
                cut_halo(0, j)
                halo[0][j].start()
            with mark("far0"):
                send_far(0)
        else:
            cut_halo(1, 0)
            halo[1][0].start()
    with mark("prep"):
        cut_near(1)
        for load in loads[3:]:
            load.wait()
        wave[0], wave[1] = turn(
            even_first(lambda first, k: phase[k, pl.ds(first, rim, stride=2), :])
        )
        gather_own(0)
        for s in range(2):
            position = find(here[0], steps[s].upper, c)
            measured[s] = even_first(
                lambda first, k: amps[k, position, pl.ds(first, rim, stride=2), :]
            )
    for k, (s, rank) in enumerate(((0, c), (0, other_cut), (1, c), (1, other_cut))):
        row, col = corner(here, steps[s].upper, rank)
        coords[2 * k] = row
        coords[2 * k + 1] = col
    for k, (s, rank) in enumerate(((0, c), (0, other_cut), (1, c), (1, other_cut))):
        row, col = corner(around[s], steps[s].peer_upper, rank)
        coords[8 + 2 * k] = row + steps[s].peer_offset + steps[s].peer_far_low
        coords[9 + 2 * k] = col
    first = c == 0
    with mark("wsA"):
        x_near[0].wait_send()
        x_far[0].wait_send()
    x_near[1].start()
    cut_halo(1, 1)
    halo[1][1].start()

    @pl.when(jnp.logical_not(steps[1].wraps))
    def _():
        with mark("far1"):
            send_far(1)

    for s in range(2):
        step = steps[s]
        position = find(here[0], step.upper, c)
        psi0 = wide(probes, choice[position])
        with mark("wx"):
            x_near[s].wait_recv()
            x_far[s].wait_recv()
        mine = tuple(own[s, plane] for plane in range(2))
        theirs = tuple(x_in[s, plane].astype(jnp.float32) for plane in range(2))
        object0 = tuple(jnp.where(first, x, y) for x, y in zip(mine, theirs))
        object1 = tuple(jnp.where(first, y, x) for x, y in zip(mine, theirs))
        with mark("pos"):
            d0, d1 = one_position(psi0, object0, object1, measured[s], (wave[0], wave[1]), tables)
        for plane in range(2):
            give[s, plane] = jnp.where(first, d1[plane], d0[plane]).astype(jnp.bfloat16)
            keep[s, plane] = jnp.where(first, d0[plane], d1[plane]).astype(jnp.bfloat16)
        if s == 0:
            back_own[0].start()
            keeps[0].start()

            @pl.when(steps[1].wraps)
            def _():
                with mark("far1w"):
                    send_far(1)

            with mark("own1"):
                gather_own(1)
            with mark("wsB"):
                x_near[1].wait_send()
                x_far[1].wait_send()
            give_far[0].start()
            give_near[0][0].start()
        else:
            give_far[1].start()
            give_near[0][1].start()
            give_near[1][0].start()
            give_near[1][1].start()
            back_own[1].start()
            keeps[1].start()
    for s in range(2):
        with mark("wgf"):
            give_far[s].wait_recv()
        back_other[s].start()
    for copy in halo[0] + halo[1] + give_far:
        copy.wait_send()
    with mark("wgn"):
        for copy in give_near[0] + give_near[1]:
            copy.wait()
    with mark("wend"):
        for copy in back_own + back_other:
            copy.wait()
    for copy in keeps:
        copy.wait()


def deposit_kernel(side, coords, keep, give_in, far_back, out, grad, out_sem):
    rim = side // 2
    quarter = side // 4
    band_rows = out.shape[1]
    region = lax.axis_index("region")
    grad[...] = jnp.zeros_like(grad)
    stores = []
    for plane in range(2):
        for s in range(2):
            even = 1 - lax.rem(region, 2)
            upper = 1 - even if s == 0 else even
            low = pl.multiple_of(upper * quarter, quarter)
            rows = pl.ds(low, side - quarter)
            parts = [
                (keep[s, plane, rows], coords[4 * s] + low, coords[4 * s + 1]),
                (give_in[s, plane, rows], coords[4 * s + 2] + low, coords[4 * s + 3]),
                (far_back[s, 0, plane], coords[8 + 4 * s], coords[9 + 4 * s]),
                (far_back[s, 1, plane], coords[10 + 4 * s], coords[11 + 4 * s]),
            ]
            for part, row, col in parts:
                add_window(grad, plane, row + rim, col, part.astype(jnp.float32))
        stores.append(
            pltpu.make_async_copy(
                grad.at[plane, pl.ds(rim, band_rows)], out.at[plane], out_sem.at[plane]
            )
        )
        stores[-1].start()
    for store in stores:
        store.wait()


def shards(objects, probes, amplitudes, prop_phase, scan_rows, scan_cols, probe_choice):
    side = probes.shape[-1]
    rim = side // 2
    count = lax.axis_size("region")
    band = objects[0]
    band_rows, columns = band.shape[1:]
    tables = dft_blocks(side)
    whole = (2, 2, side, side)
    half = (2, 2, 2, rim, side)
    held = lambda shape: jax.ShapeDtypeStruct(shape, jnp.bfloat16)
    slot = lambda shape: pltpu.VMEM(shape, jnp.bfloat16)
    tall = pltpu.VMEM((2, band_rows + 2 * rim + SUBLANES, columns), jnp.float32)
    ANY = pl.BlockSpec(memory_space=pl.ANY)
    HBM = pl.BlockSpec(memory_space=pltpu.HBM)
    scalars = pltpu.SMEM(scan_rows.shape, jnp.int32)
    coords, keep, give_in, far_back = pl.pallas_call(
        functools.partial(wave_kernel, side, count),
        out_shape=(jax.ShapeDtypeStruct((16,), jnp.int32), held(whole), held(whole), held(half)),
        in_specs=[(HBM, HBM)] + [HBM] * 6,
        out_specs=(SMEM, ANY, ANY, ANY),
        scratch_shapes=[
            tall,
            pltpu.VMEM(probes.shape, probes.dtype),
            pltpu.VMEM((2,) + amplitudes.shape[:2] + (rim,), jnp.float32),
            pltpu.VMEM((2, side, rim), jnp.float32),
            pltpu.VMEM((2,) + prop_phase.shape, jnp.float32),
            pltpu.VMEM(tables.shape, tables.dtype),
            pltpu.VMEM((2, side, side), jnp.float32),
            slot(whole), slot(whole), slot(half), slot(half),
            pltpu.VMEM(whole, jnp.float32), slot(whole), slot(whole),
            (scalars,) * 2, ((scalars,) * 2,) * 2, scalars,
            pltpu.SemaphoreType.DMA((10,)),
            pltpu.SemaphoreType.DMA((2,)),
            pltpu.SemaphoreType.DMA((24,)),
            pltpu.SemaphoreType.DMA((24,)),
        ],
        compiler_params=pltpu.CompilerParams(
            collective_id=0, has_side_effects=True, vmem_limit_bytes=28 * 1024 * 1024
        ),
    )(*jax.tree.map(lambda x: pltpu.with_memory_space_constraint(x, pltpu.HBM), ((scan_rows, scan_cols), probe_choice, band, probes, amplitudes, prop_phase, tables)))
    out = pl.pallas_call(
        functools.partial(deposit_kernel, side),
        out_shape=jax.ShapeDtypeStruct(band.shape, jnp.float32),
        in_specs=[SMEM] + [VMEM] * 3,
        out_specs=ANY,
        scratch_shapes=[tall, pltpu.SemaphoreType.DMA((2,))],
        compiler_params=LIMIT,
    )(coords, keep, give_in, far_back)
    return out[None]


def solution(mesh):
    return jax.shard_map(
        shards,
        mesh=mesh,
        in_specs=(
            P("cuts", None, "region", None),
            P(),
            P("region", None, None),
            P(),
            P("region"),
            P("region"),
            P("region"),
        ),
        out_specs=P("cuts", None, "region", None),
        check_vma=False,
    )
```

```python
import contextlib
import functools
import jax
import jax.numpy as jnp
import numpy as np
from jax import lax
from jax.experimental import pallas as pl
from jax.experimental.pallas import tpu as pltpu
from jax.sharding import PartitionSpec as P

modulus_floor = 0.25
LANES = 128
SUBLANES = 8
VMEM = pl.BlockSpec(memory_space=pltpu.VMEM)


def mark(name):
    return contextlib.nullcontext()


def dft_blocks(side):
    half = side // 2
    indices = np.arange(side)
    angles = (indices[:, None] * indices[None, :] % side) * (2.0 * np.pi / side)
    real = np.cos(angles) / np.sqrt(side)
    imag = np.sin(angles) / np.sqrt(side)
    tables = []
    for odd in range(2):
        cos, sin = real[:half, odd::2], imag[:half, odd::2]
        tables.append(np.block([[cos.T, sin.T], [-sin.T, cos.T]]))
    for odd in range(2):
        cos, sin = real[:half, odd::2], imag[:half, odd::2]
        tables.append(np.block([[cos, -sin], [sin, cos]]))
    return jnp.asarray(np.stack(tables), dtype=jnp.bfloat16)


def split_col(col, cols, side):
    base = jnp.minimum(lax.div(col, LANES), (cols - side) // LANES - 1) * LANES
    return base, col - base


def cut_window(ext, plane, row, col, height, side):
    base, shift = split_col(col, ext.shape[2], side)
    top = lax.div(row, SUBLANES) * SUBLANES
    tall = height + SUBLANES
    block = ext[plane, pl.ds(top, tall), pl.ds(base, side + LANES)]
    block = pltpu.roll(block, lax.rem(tall + top - row, tall), axis=0)[:height]
    back = lax.rem(LANES - shift + LANES, LANES)
    chunks = [
        pltpu.roll(block[:, j : j + LANES], back, axis=1) for j in range(0, side + LANES, LANES)
    ]
    lane = lax.broadcasted_iota(jnp.int32, (height, LANES), 1)
    keep = lane < LANES - shift
    return jnp.concatenate(
        [jnp.where(keep, chunks[j], chunks[j + 1]) for j in range(len(chunks) - 1)], axis=1
    )


def lay_window(padded, plane, row, col, field):
    height, side = field.shape
    rows = lax.rem(row + 8 * SUBLANES * side, SUBLANES)
    base, shift = col
    tall = height + SUBLANES
    field = jnp.concatenate([field, jnp.zeros((SUBLANES, side), field.dtype)], axis=0)
    field = pltpu.roll(field, rows, axis=0)
    ahead = lax.rem(shift, LANES)
    chunks = [pltpu.roll(field[:, j : j + LANES], ahead, axis=1) for j in range(0, side, LANES)]
    lane = lax.broadcasted_iota(jnp.int32, (tall, LANES), 1)
    keep = lane >= shift
    zero = jnp.zeros((tall, LANES), field.dtype)
    parts = [zero] + chunks + [zero]
    for j in range(len(chunks) + 1):
        padded[plane, j + 1, pl.ds(side // 4, tall)] = jnp.where(keep, parts[j + 1], parts[j])


def add_laid(total, padded, plane, row, col, first, height, side):
    base, _ = col
    shift = side // 4 + 8 * SUBLANES * side
    start = (lax.div(first + shift, SUBLANES) - lax.div(row + 8 * SUBLANES * side, SUBLANES)) * SUBLANES
    count = side // LANES + 1
    for j in range(total.shape[2] // LANES):
        block = j - lax.div(base, LANES)
        inside = jnp.logical_and(block >= 0, block < count)
        source = padded[plane, jnp.where(inside, block + 1, 0), pl.ds(start, height)]
        where = (plane, pl.ds(first, height), pl.ds(j * LANES, LANES))
        total[where] = total[where] + source


def dot(left, right):
    return jnp.dot(left, right, preferred_element_type=jnp.float32)


def narrow(left, right, axis):
    return jnp.concatenate([left, right], axis=axis).astype(jnp.bfloat16)


def forward(field, tables):
    half = field[0].shape[0] // 2
    low, high = [part[:half] for part in field], [part[half:] for part in field]
    even = dot(tables[0], narrow(low[0] + high[0], low[1] + high[1], 0))
    odd = dot(tables[1], narrow(low[0] - high[0], low[1] - high[1], 0))
    middle = [
        jnp.concatenate([even[:half], odd[:half]], axis=0),
        jnp.concatenate([even[half:], odd[half:]], axis=0),
    ]
    low, high = [part[:, :half] for part in middle], [part[:, half:] for part in middle]
    even = dot(narrow(low[0] + high[0], low[1] + high[1], 1), tables[2])
    odd = dot(narrow(low[0] - high[0], low[1] - high[1], 1), tables[3])
    return (
        jnp.concatenate([even[:, :half], odd[:, :half]], axis=1),
        jnp.concatenate([even[:, half:], odd[:, half:]], axis=1),
    )


def inverse(field, tables):
    half = field[0].shape[0] // 2
    even = dot(tables[2], narrow(field[0][:half], field[1][:half], 0))
    odd = dot(tables[3], narrow(field[0][half:], field[1][half:], 0))
    total, rest = even + odd, even - odd
    middle = [
        jnp.concatenate([total[:half], rest[:half]], axis=0),
        jnp.concatenate([total[half:], rest[half:]], axis=0),
    ]
    even = dot(narrow(middle[0][:, :half], middle[1][:, :half], 1), tables[0])
    odd = dot(narrow(middle[0][:, half:], middle[1][:, half:], 1), tables[1])
    total, rest = even + odd, even - odd
    return (
        jnp.concatenate([total[:, :half], rest[:, :half]], axis=1),
        jnp.concatenate([total[:, half:], rest[:, half:]], axis=1),
    )


def even_first(rows):
    array = jnp.concatenate(
        [jnp.concatenate([rows(first, k) for k in range(2)], axis=1) for first in range(2)], axis=0
    )
    side = array.shape[1]
    source = lax.broadcasted_iota(jnp.int32, (side, side), 0)
    target = lax.broadcasted_iota(jnp.int32, (side, side), 1)
    wanted = jnp.where(target < side // 2, 2 * target, 2 * target - side + 1)
    pick = jnp.where(source == wanted, 1.0, 0.0).astype(jnp.bfloat16)
    total = None
    for _ in range(3):
        part = array.astype(jnp.bfloat16)
        array = array - part.astype(jnp.float32)
        moved = dot(part, pick)
        total = moved if total is None else total + moved
    return total


def turn(phase):
    x = phase * 0.5
    y = x * x
    sin = np.float32(1.0 / 6227020800.0)
    for factor in (-39916800.0, 362880.0, -5040.0, 120.0, -6.0, 1.0):
        sin = sin * y + np.float32(1.0 / factor)
    sin = sin * x
    cos = np.float32(-1.0 / 87178291200.0)
    for factor in (479001600.0, -3628800.0, 40320.0, -720.0, 24.0, -2.0, 1.0):
        cos = cos * y + np.float32(1.0 / factor)
    return 1.0 - 2.0 * sin * sin, 2.0 * sin * cos


def multiply(left, right):
    return left[0] * right[0] - left[1] * right[1], left[0] * right[1] + left[1] * right[0]


def multiply_conjugate(left, right):
    return left[0] * right[0] + left[1] * right[1], left[0] * right[1] - left[1] * right[0]


def narrowed(field):
    return tuple(part.astype(jnp.bfloat16).astype(jnp.float32) for part in field)


def one_position(psi0, object0, object1, measured, wave, tables):
    psi1 = narrowed(
        inverse(multiply(wave, forward(multiply(psi0, object0), tables)), tables)
    )
    far = forward(multiply(psi1, object1), tables)
    modulus = jnp.sqrt(far[0] * far[0] + far[1] * far[1])
    factor = 1.0 - measured / jnp.maximum(modulus, modulus_floor)
    g1 = narrowed(inverse((far[0] * factor, far[1] * factor), tables))
    d1 = multiply_conjugate(psi1, g1)
    back = forward(multiply_conjugate(object1, g1), tables)
    g0 = narrowed(inverse(multiply_conjugate(wave, back), tables))
    return multiply_conjugate(psi0, g0), d1


def wide(ref, *index):
    return ref[index + (0,)].astype(jnp.float32), ref[index + (1,)].astype(jnp.float32)


def find(rows, upper, rank):
    seen = jnp.int32(0)
    chosen = jnp.int32(0)
    for position in range(rows.shape[0]):
        here = jnp.where(rows[position] < 0, 1, 0) == upper
        chosen = jnp.where(jnp.logical_and(here, seen == rank), position, chosen)
        seen = seen + jnp.where(here, 1, 0)
    return chosen


def corner(info, upper, rank, side, band_rows):
    position = find(info[0], upper, rank)
    least = jnp.where(upper == 1, -(side // 2), band_rows - side + side // 4)
    row = jnp.minimum(jnp.maximum(info[0][position], least), least + side // 4)
    return row, info[1][position]


class Step:
    def __init__(self, index, region, count, side, band_rows):
        self.index = index
        even = 1 - lax.rem(region, 2)
        self.upper = 1 - even if index == 0 else even
        before = lax.rem(region + count - 1, count)
        after = lax.rem(region + 1, count)
        self.peer = jnp.where(self.upper == 1, before, after)
        half = side // 2
        self.near_low = pl.multiple_of(self.upper * half, half)
        self.far_low = pl.multiple_of((1 - self.upper) * half, half)
        self.peer_upper = 1 - self.upper
        self.peer_offset = (2 * self.peer_upper - 1) * band_rows
        self.peer_far_low = self.near_low


def wave_kernel(
    side, count, scans, choice_any, band, probes_any, amps_any, phase_any, tables_any,
    total,
    ext, probes, amps, phase, wave, tables, measured,
    x_send, x_in, far_send, far_in, own, give, keep, give_in, far_back, strip_send, strip_in,
    near_laid, far_laid, end_laid, here, around, choice,
    local_sem, send_sem, recv_sem,
):
    rim = side // 2
    band_rows = band.shape[1]
    c = lax.axis_index("cuts")
    region = lax.axis_index("region")
    other_cut = 1 - c
    steps = [Step(s, region, count, side, band_rows) for s in range(2)]
    loads = [
        pltpu.make_async_copy(source, target, local_sem.at[k])
        for k, (source, target) in enumerate((
            (scans[0], here[0]), (scans[1], here[1]),
            (band, ext.at[:, pl.ds(rim, band_rows)]), (choice_any, choice),
            (tables_any, tables), (probes_any, probes),
            *((phase_any.at[:, pl.ds(k * rim, rim)], phase.at[k]) for k in range(2)),
            *((amps_any.at[:, :, pl.ds(k * rim, rim)], amps.at[k]) for k in range(2)),
        ))
    ]
    for load in loads:
        load.start()
    barrier = pltpu.get_barrier_semaphore()
    early = region == 0
    late = region == count - 1
    wraps = jnp.logical_or(early, late)
    for peer in ((other_cut, region), (c, steps[0].peer)):
        pl.semaphore_signal(barrier, 1, device_id=peer, device_id_type=pl.DeviceIdType.MESH)

    @pl.when(jnp.logical_not(late))
    def _():
        pl.semaphore_signal(
            barrier, 1, device_id=(c, steps[1].peer), device_id_type=pl.DeviceIdType.MESH
        )

    with mark("bar"):
        pl.semaphore_wait(barrier, jnp.where(early, 2, 3))
    slots = iter(range(40))

    def remote(source, target, peer):
        slot = next(slots)
        return pltpu.make_async_remote_copy(
            src_ref=source, dst_ref=target,
            send_sem=send_sem.at[slot], recv_sem=recv_sem.at[slot],
            device_id=peer, device_id_type=pl.DeviceIdType.MESH,
        )

    across = (other_cut, region)
    notes = [
        [remote(scans[k], around[s][k], (c, steps[s].peer)) for k in range(2)] for s in range(2)
    ]
    near = [pl.ds(step.near_low, rim) for step in steps]
    far = [pl.ds(step.far_low, rim) for step in steps]
    x_near = [remote(x_send.at[s, :, near[s]], x_in.at[s, :, near[s]], across) for s in range(2)]
    x_far = [
        [remote(x_send.at[s, p, far[s]], x_in.at[s, p, far[s]], across) for p in range(2)]
        for s in range(2)
    ]
    halo = [
        [remote(far_send.at[s, j], far_in.at[s, j], (c, steps[s].peer)) for j in range(2)]
        for s in range(2)
    ]
    quarter = side // 4
    give_parts, back_other = [], []
    for s, step in enumerate(steps):
        order = [3 - k + step.upper * (2 * k - 3) for k in range(4)]
        rows = [pl.ds(pl.multiple_of(k * quarter, quarter), quarter) for k in order]
        give_parts.append(
            [remote(give.at[s, :, part], give_in.at[s, :, part], across) for part in rows]
        )
        back_other.append([])
        for part, k in zip(rows[:2], order[:2]):
            start = pl.multiple_of(k * quarter - step.far_low, quarter)
            back_other[s].append(
                remote(
                    give_in.at[s, :, part],
                    far_back.at[s, 1, :, pl.ds(start, quarter)],
                    (c, step.peer),
                )
            )
    back_own = [
        remote(keep.at[s, :, far[s]], far_back.at[s, 0], (c, steps[s].peer)) for s in range(2)
    ]
    strip = [remote(strip_send.at[p], strip_in.at[p], (c, steps[1].peer)) for p in range(2)]
    for note in notes[0]:
        note.start()

    @pl.when(jnp.logical_not(early))
    def _():
        for note in notes[1]:
            note.start()

    with mark("band"):
        for load in loads[:3]:
            load.wait()

    ids = lax.broadcasted_iota(jnp.int32, (rim, side), 0)

    def cut_far(s, rank):
        step = steps[s]
        row, col = corner(around[s], step.peer_upper, rank, side, band_rows)
        top = row + step.peer_offset + step.peer_far_low + rim
        return [cut_window(ext, plane, top, col, rim, side) for plane in range(2)]

    def mixed(s, rank, j, plane):
        step = steps[s]
        row, col = corner(here, step.upper, rank, side, band_rows)
        held = cut_window(ext, plane, row + rim + step.far_low, col, rim, side)
        rows = ids + (row + step.far_low)
        outside = jnp.logical_or(rows < 0, rows >= band_rows)
        if s == 1:
            outside = jnp.logical_and(outside, jnp.logical_not(wraps))
        return jnp.where(outside, far_in[s, j, plane].astype(jnp.float32), held)

    def near_half(s, rank, plane):
        step = steps[s]
        row, col = corner(here, step.upper, rank, side, band_rows)
        return cut_window(ext, plane, row + rim + step.near_low, col, rim, side)

    def cut_near(s):
        for plane in range(2):
            x_send[s, plane, near[s]] = near_half(s, other_cut, plane).astype(jnp.bfloat16)

    def cut_halo(s, j):
        for plane, part in enumerate(cut_far(s, (other_cut, c)[j])):
            far_send[s, j, plane] = part.astype(jnp.bfloat16)

    def send_far(s, plane):
        with mark("far"):
            x_send[s, plane, far[s]] = mixed(s, other_cut, 0, plane).astype(jnp.bfloat16)
            x_far[s][plane].start()

    def send_strip_far(plane):
        with mark("wstrip"):
            strip[plane].wait_recv()
        rows = pl.ds(pl.multiple_of((1 - steps[1].upper) * (rim + band_rows), rim), rim)
        ext[plane, rows] = strip_in[plane].astype(jnp.float32)
        send_far(1, plane)

    def gather_own(s):
        for plane in range(2):
            own[s, plane, near[s]] = near_half(s, c, plane)
            own[s, plane, far[s]] = mixed(s, c, 1, plane)

    def send_strip():
        rows = pl.ds(pl.multiple_of(rim + steps[1].peer_upper * (band_rows - rim), rim), rim)
        for plane in range(2):
            strip_send[plane] = ext[plane, rows].astype(jnp.bfloat16)
            strip[plane].start()

    def add_near(s, rank, source):
        step = steps[s]
        row, col = corner(here, step.upper, rank, side, band_rows)
        low = pl.multiple_of(step.upper * quarter, quarter)
        first = pl.multiple_of((1 - step.upper) * quarter, quarter)
        place = split_col(col, total.shape[2], side)
        for plane in range(2):
            part = source[s, plane, pl.ds(low, side - quarter)].astype(jnp.float32)
            lay_window(near_laid, plane, row + low, place, part)
            add_laid(total, near_laid, plane, row + low, place, first, side - quarter, side)

    def add_far(s, j):
        step = steps[s]
        row, col = corner(around[s], step.peer_upper, (c, other_cut)[j], side, band_rows)
        top = row + step.peer_offset + step.peer_far_low
        first = pl.multiple_of(step.peer_upper * rim, rim)
        place = split_col(col, total.shape[2], side)
        for plane in range(2):
            part = far_back[s, j, plane].astype(jnp.float32)
            lay_window(far_laid, plane, top, place, part)
            add_laid(total, far_laid, plane, top, place, first, rim, side)

    def add_middle(s, rank, source):
        step = steps[s]
        row, col = corner(here, step.upper, rank, side, band_rows)
        first = pl.multiple_of((1 - step.upper) * rim, rim)
        place = split_col(col, total.shape[2], side)
        for plane in range(2):
            part = source[s, plane, pl.ds(quarter, rim)].astype(jnp.float32)
            lay_window(far_laid, plane, row + quarter, place, part)
            add_laid(total, far_laid, plane, row + quarter, place, first, rim, side)

    def add_end(s, rank, source):
        step = steps[s]
        row, col = corner(here, step.upper, rank, side, band_rows)
        low = pl.multiple_of(step.upper * 3 * quarter, quarter)
        place = split_col(col, total.shape[2], side)
        for plane in range(2):
            part = source[s, plane, pl.ds(low, quarter)].astype(jnp.float32)
            lay_window(end_laid, plane, row + low, place, part)
            add_laid(total, end_laid, plane, row + low, place, quarter, rim, side)

    def position_of(s):
        position = find(here[0], steps[s].upper, c)
        psi0 = wide(probes, choice[position])
        with mark("wx"):
            for copy in [x_near[s]] + x_far[s]:
                copy.wait_recv()
        mine = tuple(own[s, plane] for plane in range(2))
        theirs = tuple(x_in[s, plane].astype(jnp.float32) for plane in range(2))
        object0 = tuple(jnp.where(first, x, y) for x, y in zip(mine, theirs))
        object1 = tuple(jnp.where(first, y, x) for x, y in zip(mine, theirs))
        with mark("pos"):
            d0, d1 = one_position(psi0, object0, object1, measured[s], (wave[0], wave[1]), tables)
        for plane in range(2):
            give[s, plane] = jnp.where(first, d1[plane], d0[plane]).astype(jnp.bfloat16)
            keep[s, plane] = jnp.where(first, d0[plane], d1[plane]).astype(jnp.bfloat16)

    first = c == 0
    with mark("near0"):
        cut_near(0)
        x_near[0].start()

    @pl.when(late)
    def _():
        send_strip()

    with mark("wnote"):
        for note in notes[0]:
            note.wait_recv()
    for j in range(2):
        cut_halo(0, j)
        halo[0][j].start()
    with mark("wh0"):
        halo[0][0].wait_recv()
    for plane in range(2):
        send_far(0, plane)

    @pl.when(jnp.logical_not(wraps))
    def _():
        with mark("wnote"):
            for note in notes[1]:
                note.wait_recv()
        cut_halo(1, 0)
        halo[1][0].start()

    with mark("prep"):
        cut_near(1)
        for load in loads[3:]:
            load.wait()
        wave[0], wave[1] = turn(
            even_first(lambda first, k: phase[k, pl.ds(first, rim, stride=2), :])
        )
        halo[0][1].wait_recv()
        gather_own(0)
        for s in range(2):
            position = find(here[0], steps[s].upper, c)
            measured[s] = even_first(
                lambda first, k: amps[k, position, pl.ds(first, rim, stride=2), :]
            )
        near_laid[...] = jnp.zeros_like(near_laid)
        far_laid[...] = jnp.zeros_like(far_laid)
        end_laid[...] = jnp.zeros_like(end_laid)
        total[...] = jnp.zeros_like(total)

    @pl.when(early)
    def _():
        with mark("wnote"):
            for note in notes[1]:
                note.wait_recv()
        send_strip()
        for note in notes[1]:
            note.start()

    with mark("wsA"):
        for copy in [x_near[0]] + x_far[0]:
            copy.wait_send()
    x_near[1].start()

    @pl.when(jnp.logical_not(wraps))
    def _():
        cut_halo(1, 1)
        halo[1][1].start()
        with mark("wh1"):
            halo[1][0].wait_recv()
        for plane in range(2):
            send_far(1, plane)

    @pl.when(wraps)
    def _():
        send_strip_far(0)

    position_of(0)

    @pl.when(wraps)
    def _():
        send_strip_far(1)

    back_own[0].start()

    @pl.when(jnp.logical_not(wraps))
    def _():
        with mark("wh1"):
            halo[1][1].wait_recv()

    with mark("own1"):
        gather_own(1)
    with mark("add"):
        add_near(0, c, keep)
    with mark("wsB"):
        for copy in [x_near[1]] + x_far[1]:
            copy.wait_send()
    for copy in give_parts[0]:
        copy.start()
    position_of(1)
    for copy in give_parts[1][:2]:
        copy.start()
    back_own[1].start()
    with mark("wgf0"):
        for part, back in zip(give_parts[0], back_other[0]):
            part.wait_recv()
            back.start()
    with mark("add"):
        back_own[0].wait_recv()
        add_far(0, 0)
        add_near(1, c, keep)

    @pl.when(late)
    def _():
        for note in notes[1]:
            note.wait_recv()

    with mark("wsC"):
        give_parts[1][0].wait_send()
    for copy in give_parts[1][2:]:
        copy.start()
    with mark("wgf1"):
        for part, back in zip(give_parts[1], back_other[1]):
            part.wait_recv()
            back.start()
    with mark("add"):
        for copy in give_parts[0][2:]:
            copy.wait_recv()
        add_near(0, other_cut, give_in)
    with mark("add"):
        for copy in back_other[0]:
            copy.wait_recv()
        add_far(0, 1)
    with mark("add"):
        back_own[1].wait_recv()
        add_far(1, 0)
    with mark("wgn"):
        give_parts[1][2].wait_recv()
    with mark("add"):
        add_middle(1, other_cut, give_in)
    with mark("wgn"):
        give_parts[1][3].wait_recv()
    with mark("add"):
        add_end(1, other_cut, give_in)
    with mark("wend"):
        for copy in back_other[1]:
            copy.wait_recv()
    with mark("add"):
        add_far(1, 1)

    @pl.when(wraps)
    def _():
        for copy in strip:
            copy.wait_send()

    @pl.when(jnp.logical_not(wraps))
    def _():
        for copy in halo[1]:
            copy.wait_send()

    for copy in notes[0] + notes[1] + halo[0] + give_parts[0] + give_parts[1][1:]:
        copy.wait_send()
    for copy in back_own + back_other[0] + back_other[1]:
        copy.wait_send()


def shards(objects, probes, amplitudes, prop_phase, scan_rows, scan_cols, probe_choice):
    side = probes.shape[-1]
    rim = side // 2
    count = lax.axis_size("region")
    band = objects[0]
    band_rows, columns = band.shape[1:]
    tables = dft_blocks(side)
    whole = (2, 2, side, side)
    half = (2, 2, 2, rim, side)
    slot = lambda shape: pltpu.VMEM(shape, jnp.bfloat16)
    tall = pltpu.VMEM((2, band_rows + 2 * rim + SUBLANES, columns), jnp.float32)
    HBM = pl.BlockSpec(memory_space=pltpu.HBM)
    scalars = pltpu.SMEM(scan_rows.shape, jnp.int32)
    laid = lambda rows: pltpu.VMEM((2, side // LANES + 2, rows, LANES), jnp.float32)
    out = pl.pallas_call(
        functools.partial(wave_kernel, side, count),
        out_shape=jax.ShapeDtypeStruct(band.shape, jnp.float32),
        in_specs=[(HBM, HBM)] + [HBM] * 6,
        out_specs=VMEM,
        scratch_shapes=[
            tall,
            pltpu.VMEM(probes.shape, probes.dtype),
            pltpu.VMEM((2,) + amplitudes.shape[:2] + (rim,), jnp.float32),
            pltpu.VMEM((2, side, rim), jnp.float32),
            pltpu.VMEM((2,) + prop_phase.shape, jnp.float32),
            pltpu.VMEM(tables.shape, tables.dtype),
            pltpu.VMEM((2, side, side), jnp.float32),
            slot(whole), slot(whole), slot(half), slot(half),
            pltpu.VMEM(whole, jnp.float32), slot(whole), slot(whole), slot(whole), slot(half),
            slot((2, rim, columns)), slot((2, rim, columns)),
            laid(side + side // 4), laid(side), laid(side - side // 4),
            (scalars,) * 2, ((scalars,) * 2,) * 2, scalars,
            pltpu.SemaphoreType.DMA((10,)),
            pltpu.SemaphoreType.DMA((40,)),
            pltpu.SemaphoreType.DMA((40,)),
        ],
        compiler_params=pltpu.CompilerParams(
            collective_id=0, has_side_effects=True, vmem_limit_bytes=32 * 1024 * 1024
        ),
    )(*jax.tree.map(
        lambda x: pltpu.with_memory_space_constraint(x, pltpu.HBM),
        ((scan_rows, scan_cols), probe_choice, band, probes, amplitudes, prop_phase, tables),
    ))
    return out[None]


def solution(mesh):
    return jax.shard_map(
        shards,
        mesh=mesh,
        in_specs=(
            P("cuts", None, "region", None),
            P(),
            P("region", None, None),
            P(),
            P("region"),
            P("region"),
            P("region"),
        ),
        out_specs=P("cuts", None, "region", None),
        check_vma=False,
    )
```

```python
import contextlib
import functools
import jax
import jax.numpy as jnp
import numpy as np
from jax import lax
from jax.experimental import pallas as pl
from jax.experimental.pallas import tpu as pltpu
from jax.sharding import PartitionSpec as P

modulus_floor = 0.25
LANES = 128
SUBLANES = 8
VMEM = pl.BlockSpec(memory_space=pltpu.VMEM)


def mark(name):
    return contextlib.nullcontext()


def dft_blocks(side):
    half = side // 2
    indices = np.arange(side)
    angles = (indices[:, None] * indices[None, :] % side) * (2.0 * np.pi / side)
    real = np.cos(angles) / np.sqrt(side)
    imag = np.sin(angles) / np.sqrt(side)
    tables = []
    for odd in range(2):
        cos, sin = real[:half, odd::2], imag[:half, odd::2]
        tables.append(np.block([[cos.T, sin.T], [-sin.T, cos.T]]))
    for odd in range(2):
        cos, sin = real[:half, odd::2], imag[:half, odd::2]
        tables.append(np.block([[cos, -sin], [sin, cos]]))
    return jnp.asarray(np.stack(tables), dtype=jnp.bfloat16)


def split_col(col, cols, side):
    base = jnp.minimum(lax.div(col, LANES), (cols - side) // LANES - 1) * LANES
    return base, col - base


def cut_window(ext, plane, row, col, height, side):
    base, shift = split_col(col, ext.shape[2], side)
    top = lax.div(row, SUBLANES) * SUBLANES
    tall = height + SUBLANES
    block = ext[plane, pl.ds(top, tall), pl.ds(base, side + LANES)]
    block = pltpu.roll(block, lax.rem(tall + top - row, tall), axis=0)[:height]
    back = lax.rem(LANES - shift + LANES, LANES)
    chunks = [
        pltpu.roll(block[:, j : j + LANES], back, axis=1) for j in range(0, side + LANES, LANES)
    ]
    lane = lax.broadcasted_iota(jnp.int32, (height, LANES), 1)
    keep = lane < LANES - shift
    return jnp.concatenate(
        [jnp.where(keep, chunks[j], chunks[j + 1]) for j in range(len(chunks) - 1)], axis=1
    )


def lay_window(padded, plane, row, col, field):
    height, side = field.shape
    rows = lax.rem(row + 8 * SUBLANES * side, SUBLANES)
    base, shift = col
    tall = height + SUBLANES
    field = jnp.concatenate([field, jnp.zeros((SUBLANES, side), field.dtype)], axis=0)
    field = pltpu.roll(field, rows, axis=0)
    ahead = lax.rem(shift, LANES)
    chunks = [pltpu.roll(field[:, j : j + LANES], ahead, axis=1) for j in range(0, side, LANES)]
    lane = lax.broadcasted_iota(jnp.int32, (tall, LANES), 1)
    keep = lane >= shift
    zero = jnp.zeros((tall, LANES), field.dtype)
    parts = [zero] + chunks + [zero]
    for j in range(len(chunks) + 1):
        padded[plane, j + 1, pl.ds(side // 4, tall)] = jnp.where(keep, parts[j + 1], parts[j])


def add_laid(total, padded, plane, row, col, first, height, side):
    base, _ = col
    shift = side // 4 + 8 * SUBLANES * side
    start = (lax.div(first + shift, SUBLANES) - lax.div(row + 8 * SUBLANES * side, SUBLANES)) * SUBLANES
    count = side // LANES + 1
    for j in range(total.shape[2] // LANES):
        block = j - lax.div(base, LANES)
        inside = jnp.logical_and(block >= 0, block < count)
        source = padded[plane, jnp.where(inside, block + 1, 0), pl.ds(start, height)]
        where = (plane, pl.ds(first, height), pl.ds(j * LANES, LANES))
        total[where] = total[where] + source


def dot(left, right):
    return jnp.dot(left, right, preferred_element_type=jnp.float32)


def narrow(left, right, axis):
    return jnp.concatenate([left, right], axis=axis).astype(jnp.bfloat16)


def forward(field, tables):
    half = field[0].shape[0] // 2
    low, high = [part[:half] for part in field], [part[half:] for part in field]
    even = dot(tables[0], narrow(low[0] + high[0], low[1] + high[1], 0))
    odd = dot(tables[1], narrow(low[0] - high[0], low[1] - high[1], 0))
    middle = [
        jnp.concatenate([even[:half], odd[:half]], axis=0),
        jnp.concatenate([even[half:], odd[half:]], axis=0),
    ]
    low, high = [part[:, :half] for part in middle], [part[:, half:] for part in middle]
    even = dot(narrow(low[0] + high[0], low[1] + high[1], 1), tables[2])
    odd = dot(narrow(low[0] - high[0], low[1] - high[1], 1), tables[3])
    return (
        jnp.concatenate([even[:, :half], odd[:, :half]], axis=1),
        jnp.concatenate([even[:, half:], odd[:, half:]], axis=1),
    )


def inverse(field, tables):
    half = field[0].shape[0] // 2
    even = dot(tables[2], narrow(field[0][:half], field[1][:half], 0))
    odd = dot(tables[3], narrow(field[0][half:], field[1][half:], 0))
    total, rest = even + odd, even - odd
    middle = [
        jnp.concatenate([total[:half], rest[:half]], axis=0),
        jnp.concatenate([total[half:], rest[half:]], axis=0),
    ]
    even = dot(narrow(middle[0][:, :half], middle[1][:, :half], 1), tables[0])
    odd = dot(narrow(middle[0][:, half:], middle[1][:, half:], 1), tables[1])
    total, rest = even + odd, even - odd
    return (
        jnp.concatenate([total[:, :half], rest[:, :half]], axis=1),
        jnp.concatenate([total[:, half:], rest[:, half:]], axis=1),
    )


def even_first(rows):
    array = jnp.concatenate(
        [jnp.concatenate([rows(first, k) for k in range(2)], axis=1) for first in range(2)], axis=0
    )
    side = array.shape[1]
    source = lax.broadcasted_iota(jnp.int32, (side, side), 0)
    target = lax.broadcasted_iota(jnp.int32, (side, side), 1)
    wanted = jnp.where(target < side // 2, 2 * target, 2 * target - side + 1)
    pick = jnp.where(source == wanted, 1.0, 0.0).astype(jnp.bfloat16)
    total = None
    for _ in range(3):
        part = array.astype(jnp.bfloat16)
        array = array - part.astype(jnp.float32)
        moved = dot(part, pick)
        total = moved if total is None else total + moved
    return total


def turn(phase):
    x = phase * 0.5
    y = x * x
    sin = np.float32(1.0 / 6227020800.0)
    for factor in (-39916800.0, 362880.0, -5040.0, 120.0, -6.0, 1.0):
        sin = sin * y + np.float32(1.0 / factor)
    sin = sin * x
    cos = np.float32(-1.0 / 87178291200.0)
    for factor in (479001600.0, -3628800.0, 40320.0, -720.0, 24.0, -2.0, 1.0):
        cos = cos * y + np.float32(1.0 / factor)
    return 1.0 - 2.0 * sin * sin, 2.0 * sin * cos


def multiply(left, right):
    return left[0] * right[0] - left[1] * right[1], left[0] * right[1] + left[1] * right[0]


def multiply_conjugate(left, right):
    return left[0] * right[0] + left[1] * right[1], left[0] * right[1] - left[1] * right[0]


def narrowed(field):
    return tuple(part.astype(jnp.bfloat16).astype(jnp.float32) for part in field)


def one_position(psi0, object0, object1, measured, wave, tables):
    psi1 = narrowed(
        inverse(multiply(wave, forward(multiply(psi0, object0), tables)), tables)
    )
    far = forward(multiply(psi1, object1), tables)
    modulus = jnp.sqrt(far[0] * far[0] + far[1] * far[1])
    factor = 1.0 - measured / jnp.maximum(modulus, modulus_floor)
    g1 = narrowed(inverse((far[0] * factor, far[1] * factor), tables))
    d1 = multiply_conjugate(psi1, g1)
    back = forward(multiply_conjugate(object1, g1), tables)
    g0 = narrowed(inverse(multiply_conjugate(wave, back), tables))
    return multiply_conjugate(psi0, g0), d1


def wide(ref, *index):
    return ref[index + (0,)].astype(jnp.float32), ref[index + (1,)].astype(jnp.float32)


def find(rows, upper, rank):
    seen = jnp.int32(0)
    chosen = jnp.int32(0)
    for position in range(rows.shape[0]):
        here = jnp.where(rows[position] < 0, 1, 0) == upper
        chosen = jnp.where(jnp.logical_and(here, seen == rank), position, chosen)
        seen = seen + jnp.where(here, 1, 0)
    return chosen


def corner(info, upper, rank, side, band_rows):
    position = find(info[0], upper, rank)
    least = jnp.where(upper == 1, -(side // 2), band_rows - side + side // 4)
    row = jnp.minimum(jnp.maximum(info[0][position], least), least + side // 4)
    return row, info[1][position]


class Step:
    def __init__(self, index, region, count, side, band_rows):
        self.index = index
        even = 1 - lax.rem(region, 2)
        self.upper = 1 - even if index == 0 else even
        before = lax.rem(region + count - 1, count)
        after = lax.rem(region + 1, count)
        self.peer = jnp.where(self.upper == 1, before, after)
        half = side // 2
        self.near_low = pl.multiple_of(self.upper * half, half)
        self.far_low = pl.multiple_of((1 - self.upper) * half, half)
        self.peer_upper = 1 - self.upper
        self.peer_offset = (2 * self.peer_upper - 1) * band_rows
        self.peer_far_low = self.near_low


def wave_kernel(
    side, count, scans, choice_any, band, probes_any, amps_any, phase_any, tables_any,
    total,
    ext, probes, amps, phase, wave, tables, measured,
    x_send, x_in, far_send, far_in, own, give, keep, give_in, far_back, strip_send, strip_in,
    near_laid, far_laid, end_laid, here, around, choice,
    local_sem, send_sem, recv_sem,
):
    rim = side // 2
    band_rows = band.shape[1]
    c = lax.axis_index("cuts")
    region = lax.axis_index("region")
    other_cut = 1 - c
    steps = [Step(s, region, count, side, band_rows) for s in range(2)]
    loads = [
        pltpu.make_async_copy(source, target, local_sem.at[k])
        for k, (source, target) in enumerate((
            (scans[0], here[0]), (scans[1], here[1]),
            (band, ext.at[:, pl.ds(rim, band_rows)]), (choice_any, choice),
            (tables_any, tables), (probes_any, probes),
            *((phase_any.at[:, pl.ds(k * rim, rim)], phase.at[k]) for k in range(2)),
            *((amps_any.at[:, :, pl.ds(k * rim, rim)], amps.at[k]) for k in range(2)),
        ))
    ]
    for load in loads:
        load.start()
    barrier = pltpu.get_barrier_semaphore()
    early = region == 0
    late = region == count - 1
    for peer in ((other_cut, region), (c, steps[0].peer)):
        pl.semaphore_signal(barrier, 1, device_id=peer, device_id_type=pl.DeviceIdType.MESH)

    @pl.when(jnp.logical_not(late))
    def _():
        pl.semaphore_signal(
            barrier, 1, device_id=(c, steps[1].peer), device_id_type=pl.DeviceIdType.MESH
        )

    with mark("bar"):
        pl.semaphore_wait(barrier, jnp.where(early, 2, 3))
    slots = iter(range(40))

    def remote(source, target, peer):
        slot = next(slots)
        return pltpu.make_async_remote_copy(
            src_ref=source, dst_ref=target,
            send_sem=send_sem.at[slot], recv_sem=recv_sem.at[slot],
            device_id=peer, device_id_type=pl.DeviceIdType.MESH,
        )

    across = (other_cut, region)
    notes = [
        [remote(here[k], around[s][k], (c, steps[s].peer)) for k in range(2)] for s in range(2)
    ]
    near = [pl.ds(step.near_low, rim) for step in steps]
    far = [pl.ds(step.far_low, rim) for step in steps]
    x_near = [remote(x_send.at[s, :, near[s]], x_in.at[s, :, near[s]], across) for s in range(2)]
    x_far = [
        [remote(x_send.at[s, p, far[s]], x_in.at[s, p, far[s]], across) for p in range(2)]
        for s in range(2)
    ]
    halo = [
        [remote(far_send.at[s, j], far_in.at[s, j], (c, steps[s].peer)) for j in range(2)]
        for s in range(2)
    ]
    quarter = side // 4
    give_parts, back_other = [], []
    for s, step in enumerate(steps):
        order = [3 - k + step.upper * (2 * k - 3) for k in range(4)]
        rows = [pl.ds(pl.multiple_of(k * quarter, quarter), quarter) for k in order]
        give_parts.append(
            [remote(give.at[s, :, part], give_in.at[s, :, part], across) for part in rows]
        )
        back_other.append([])
        for part, k in zip(rows[:2], order[:2]):
            start = pl.multiple_of(k * quarter - step.far_low, quarter)
            back_other[s].append(
                remote(
                    give_in.at[s, :, part],
                    far_back.at[s, 1, :, pl.ds(start, quarter)],
                    (c, step.peer),
                )
            )
    back_own = [
        remote(keep.at[s, :, far[s]], far_back.at[s, 0], (c, steps[s].peer)) for s in range(2)
    ]
    strip = [remote(strip_send.at[p], strip_in.at[p], (c, steps[1].peer)) for p in range(2)]
    for load in loads[:2]:
        load.wait()
    for note in notes[0]:
        note.start()

    @pl.when(jnp.logical_not(early))
    def _():
        for note in notes[1]:
            note.start()

    with mark("band"):
        loads[2].wait()

    ids = lax.broadcasted_iota(jnp.int32, (rim, side), 0)

    def cut_far(s, rank):
        step = steps[s]
        row, col = corner(around[s], step.peer_upper, rank, side, band_rows)
        top = row + step.peer_offset + step.peer_far_low + rim
        return [cut_window(ext, plane, top, col, rim, side) for plane in range(2)]

    def mixed(s, rank, j, plane):
        step = steps[s]
        row, col = corner(here, step.upper, rank, side, band_rows)
        held = cut_window(ext, plane, row + rim + step.far_low, col, rim, side)
        rows = ids + (row + step.far_low)
        outside = jnp.logical_or(rows < 0, rows >= band_rows)
        if s == 1:
            outside = jnp.logical_and(outside, jnp.logical_not(early))
        return jnp.where(outside, far_in[s, j, plane].astype(jnp.float32), held)

    def near_half(s, rank, plane):
        step = steps[s]
        row, col = corner(here, step.upper, rank, side, band_rows)
        return cut_window(ext, plane, row + rim + step.near_low, col, rim, side)

    def cut_near(s):
        for plane in range(2):
            x_send[s, plane, near[s]] = near_half(s, other_cut, plane).astype(jnp.bfloat16)

    def cut_halo(s, j):
        for plane, part in enumerate(cut_far(s, (other_cut, c)[j])):
            far_send[s, j, plane] = part.astype(jnp.bfloat16)

    def send_far(s, plane):
        with mark("far"):
            x_send[s, plane, far[s]] = mixed(s, other_cut, 0, plane).astype(jnp.bfloat16)
            x_far[s][plane].start()

    def send_strip_far(plane):
        with mark("wstrip"):
            strip[plane].wait_recv()
        rows = pl.ds(pl.multiple_of((1 - steps[1].upper) * (rim + band_rows), rim), rim)
        ext[plane, rows] = strip_in[plane].astype(jnp.float32)
        send_far(1, plane)

    def gather_own(s):
        for plane in range(2):
            own[s, plane, near[s]] = near_half(s, c, plane)
            own[s, plane, far[s]] = mixed(s, c, 1, plane)

    def send_strip(plane):
        rows = pl.ds(pl.multiple_of(rim + steps[1].peer_upper * (band_rows - rim), rim), rim)
        strip_send[plane] = ext[plane, rows].astype(jnp.bfloat16)
        strip[plane].start()

    def add_near(s, rank, source):
        step = steps[s]
        row, col = corner(here, step.upper, rank, side, band_rows)
        low = pl.multiple_of(step.upper * quarter, quarter)
        first = pl.multiple_of((1 - step.upper) * quarter, quarter)
        place = split_col(col, total.shape[2], side)
        for plane in range(2):
            part = source[s, plane, pl.ds(low, side - quarter)].astype(jnp.float32)
            lay_window(near_laid, plane, row + low, place, part)
            add_laid(total, near_laid, plane, row + low, place, first, side - quarter, side)

    def add_far(s, j):
        step = steps[s]
        row, col = corner(around[s], step.peer_upper, (c, other_cut)[j], side, band_rows)
        top = row + step.peer_offset + step.peer_far_low
        first = pl.multiple_of(step.peer_upper * rim, rim)
        place = split_col(col, total.shape[2], side)
        for plane in range(2):
            part = far_back[s, j, plane].astype(jnp.float32)
            lay_window(far_laid, plane, top, place, part)
            add_laid(total, far_laid, plane, top, place, first, rim, side)

    def add_middle(s, rank, source):
        step = steps[s]
        row, col = corner(here, step.upper, rank, side, band_rows)
        first = pl.multiple_of((1 - step.upper) * rim, rim)
        place = split_col(col, total.shape[2], side)
        for plane in range(2):
            part = source[s, plane, pl.ds(quarter, rim)].astype(jnp.float32)
            lay_window(far_laid, plane, row + quarter, place, part)
            add_laid(total, far_laid, plane, row + quarter, place, first, rim, side)

    def add_end(s, rank, source):
        step = steps[s]
        row, col = corner(here, step.upper, rank, side, band_rows)
        low = pl.multiple_of(step.upper * 3 * quarter, quarter)
        place = split_col(col, total.shape[2], side)
        for plane in range(2):
            part = source[s, plane, pl.ds(low, quarter)].astype(jnp.float32)
            lay_window(end_laid, plane, row + low, place, part)
            add_laid(total, end_laid, plane, row + low, place, quarter, rim, side)

    def position_of(s):
        position = find(here[0], steps[s].upper, c)
        psi0 = wide(probes, choice[position])
        with mark("wx"):
            for copy in [x_near[s]] + x_far[s]:
                copy.wait_recv()
        mine = tuple(own[s, plane] for plane in range(2))
        theirs = tuple(x_in[s, plane].astype(jnp.float32) for plane in range(2))
        object0 = tuple(jnp.where(first, x, y) for x, y in zip(mine, theirs))
        object1 = tuple(jnp.where(first, y, x) for x, y in zip(mine, theirs))
        with mark("pos"):
            d0, d1 = one_position(psi0, object0, object1, measured[s], (wave[0], wave[1]), tables)
        for plane in range(2):
            give[s, plane] = jnp.where(first, d1[plane], d0[plane]).astype(jnp.bfloat16)
            keep[s, plane] = jnp.where(first, d0[plane], d1[plane]).astype(jnp.bfloat16)

    first = c == 0
    with mark("near0"):
        cut_near(0)
        x_near[0].start()

    with mark("wnote"):
        for note in notes[0]:
            note.wait_recv()
    cut_halo(0, 0)
    halo[0][0].start()

    @pl.when(late)
    def _():
        send_strip(0)

    @pl.when(jnp.logical_not(jnp.logical_or(early, late)))
    def _():
        with mark("wnote"):
            for note in notes[1]:
                note.wait_recv()
        cut_halo(1, 0)
        halo[1][0].start()

    with mark("wh0"):
        halo[0][0].wait_recv()
    for plane in range(2):
        send_far(0, plane)
    cut_halo(0, 1)
    halo[0][1].start()
    with mark("prep"):
        cut_near(1)
        for load in loads[3:]:
            load.wait()
        wave[0], wave[1] = turn(
            even_first(lambda first, k: phase[k, pl.ds(first, rim, stride=2), :])
        )

        @pl.when(late)
        def _():
            send_strip(1)

        halo[0][1].wait_recv()
        gather_own(0)
        for s in range(2):
            position = find(here[0], steps[s].upper, c)
            measured[s] = even_first(
                lambda first, k: amps[k, position, pl.ds(first, rim, stride=2), :]
            )
        near_laid[...] = jnp.zeros_like(near_laid)
        far_laid[...] = jnp.zeros_like(far_laid)
        end_laid[...] = jnp.zeros_like(end_laid)
        total[...] = jnp.zeros_like(total)

    @pl.when(early)
    def _():
        with mark("wnote"):
            for note in notes[1]:
                note.wait_recv()
        cut_halo(1, 0)
        halo[1][0].start()
        for note in notes[1]:
            note.start()

    with mark("wsA"):
        x_near[0].wait_send()
        x_far[0][0].wait_send()
    x_near[1].start()

    @pl.when(jnp.logical_not(early))
    def _():
        with mark("wh1"):
            halo[1][0].wait_recv()
        for plane in range(2):
            send_far(1, plane)

    @pl.when(jnp.logical_not(late))
    def _():
        cut_halo(1, 1)
        halo[1][1].start()

    position_of(0)
    back_own[0].start()

    @pl.when(early)
    def _():
        for plane in range(2):
            send_strip_far(plane)

    give_parts[0][0].start()

    @pl.when(early)
    def _():
        give_parts[0][1].start()
        gather_own(1)

    with mark("wsB"):
        for copy in [x_far[0][1], x_near[1]] + x_far[1]:
            copy.wait_send()

    @pl.when(jnp.logical_not(early))
    def _():
        give_parts[0][1].start()

    give_parts[0][2].start()

    @pl.when(jnp.logical_not(early))
    def _():
        with mark("wh1"):
            halo[1][1].wait_recv()
        gather_own(1)

    with mark("add"):
        add_near(0, c, keep)
    position_of(1)
    for copy in give_parts[1][:2]:
        copy.start()

    @pl.when(early)
    def _():
        for copy in give_parts[0][3:] + give_parts[1][2:]:
            copy.start()

    back_own[1].start()
    with mark("wgf0"):
        for part, back in zip(give_parts[0], back_other[0]):
            part.wait_recv()
            back.start()
    with mark("add"):
        back_own[0].wait_recv()
        add_far(0, 0)
        add_near(1, c, keep)

    @pl.when(late)
    def _():
        for note in notes[1]:
            note.wait_recv()

    with mark("wsC"):
        for copy in give_parts[0][:3] + give_parts[1][:2]:
            copy.wait_send()

    @pl.when(jnp.logical_not(early))
    def _():
        for copy in give_parts[0][3:] + give_parts[1][2:]:
            copy.start()

    @pl.when(late)
    def _():
        for copy in strip:
            copy.wait_send()

    @pl.when(jnp.logical_not(late))
    def _():
        for copy in halo[1]:
            copy.wait_send()

    for copy in notes[0] + notes[1] + halo[0] + [back_own[0]]:
        copy.wait_send()
    with mark("wgf1"):
        for part, back in zip(give_parts[1], back_other[1]):
            part.wait_recv()
            back.start()
    with mark("add"):
        for copy in back_other[0]:
            copy.wait_recv()
        add_far(0, 1)
    with mark("add"):
        back_own[1].wait_recv()
        add_far(1, 0)
    for copy in [back_own[1]] + back_other[0]:
        copy.wait_send()
    with mark("wgn0"):
        for copy in give_parts[0][2:]:
            copy.wait_recv()
    with mark("add"):
        add_near(0, other_cut, give_in)
    with mark("wgn"):
        give_parts[1][2].wait_recv()
    with mark("add"):
        add_middle(1, other_cut, give_in)
    with mark("wgn"):
        give_parts[1][3].wait_recv()
    with mark("add"):
        add_end(1, other_cut, give_in)
    for copy in give_parts[0][3:] + give_parts[1][2:] + back_other[1]:
        copy.wait_send()
    with mark("wend"):
        for copy in back_other[1]:
            copy.wait_recv()
    with mark("add"):
        add_far(1, 1)


def shards(objects, probes, amplitudes, prop_phase, scan_rows, scan_cols, probe_choice):
    side = probes.shape[-1]
    rim = side // 2
    count = lax.axis_size("region")
    band = objects[0]
    band_rows, columns = band.shape[1:]
    tables = dft_blocks(side)
    whole = (2, 2, side, side)
    half = (2, 2, 2, rim, side)
    slot = lambda shape: pltpu.VMEM(shape, jnp.bfloat16)
    tall = pltpu.VMEM((2, band_rows + 2 * rim + SUBLANES, columns), jnp.float32)
    HBM = pl.BlockSpec(memory_space=pltpu.HBM)
    scalars = pltpu.SMEM(scan_rows.shape, jnp.int32)
    laid = lambda rows: pltpu.VMEM((2, side // LANES + 2, rows, LANES), jnp.float32)
    out = pl.pallas_call(
        functools.partial(wave_kernel, side, count),
        out_shape=jax.ShapeDtypeStruct(band.shape, jnp.float32),
        in_specs=[(HBM, HBM)] + [HBM] * 6,
        out_specs=VMEM,
        scratch_shapes=[
            tall,
            pltpu.VMEM(probes.shape, probes.dtype),
            pltpu.VMEM((2,) + amplitudes.shape[:2] + (rim,), jnp.float32),
            pltpu.VMEM((2, side, rim), jnp.float32),
            pltpu.VMEM((2,) + prop_phase.shape, jnp.float32),
            pltpu.VMEM(tables.shape, tables.dtype),
            pltpu.VMEM((2, side, side), jnp.float32),
            slot(whole), slot(whole), slot(half), slot(half),
            pltpu.VMEM(whole, jnp.float32), slot(whole), slot(whole), slot(whole), slot(half),
            slot((2, rim, columns)), slot((2, rim, columns)),
            laid(side + side // 4), laid(side), laid(side - side // 4),
            (scalars,) * 2, ((scalars,) * 2,) * 2, scalars,
            pltpu.SemaphoreType.DMA((10,)),
            pltpu.SemaphoreType.DMA((40,)),
            pltpu.SemaphoreType.DMA((40,)),
        ],
        compiler_params=pltpu.CompilerParams(
            collective_id=0, has_side_effects=True, vmem_limit_bytes=32 * 1024 * 1024
        ),
    )(*jax.tree.map(
        lambda x: pltpu.with_memory_space_constraint(x, pltpu.HBM),
        ((scan_rows, scan_cols), probe_choice, band, probes, amplitudes, prop_phase, tables),
    ))
    return out[None]


def solution(mesh):
    return jax.shard_map(
        shards,
        mesh=mesh,
        in_specs=(
            P("cuts", None, "region", None),
            P(),
            P("region", None, None),
            P(),
            P("region"),
            P("region"),
            P("region"),
        ),
        out_specs=P("cuts", None, "region", None),
        check_vma=False,
    )
```

```python
import contextlib
import functools
import jax
import jax.numpy as jnp
import numpy as np
from jax import lax
from jax.experimental import pallas as pl
from jax.experimental.pallas import tpu as pltpu
from jax.sharding import PartitionSpec as P

modulus_floor = 0.25
LANES = 128
SUBLANES = 8
VMEM = pl.BlockSpec(memory_space=pltpu.VMEM)


def mark(name):
    return contextlib.nullcontext()


def dft_blocks(side):
    half = side // 2
    indices = np.arange(side)
    angles = (indices[:, None] * indices[None, :] % side) * (2.0 * np.pi / side)
    real = np.cos(angles) / np.sqrt(side)
    imag = np.sin(angles) / np.sqrt(side)
    tables = []
    for odd in range(2):
        cos, sin = real[:half, odd::2], imag[:half, odd::2]
        tables.append(np.block([[cos.T, sin.T], [-sin.T, cos.T]]))
    for odd in range(2):
        cos, sin = real[:half, odd::2], imag[:half, odd::2]
        tables.append(np.block([[cos, -sin], [sin, cos]]))
    return jnp.asarray(np.stack(tables), dtype=jnp.bfloat16)


def split_col(col, cols, side):
    base = jnp.minimum(lax.div(col, LANES), (cols - side) // LANES - 1) * LANES
    return base, col - base


def cut_window(ext, plane, row, col, height, side):
    base, shift = split_col(col, ext.shape[2], side)
    top = lax.div(row, SUBLANES) * SUBLANES
    tall = height + SUBLANES
    block = ext[plane, pl.ds(top, tall), pl.ds(base, side + LANES)]
    block = pltpu.roll(block, lax.rem(tall + top - row, tall), axis=0)[:height]
    back = lax.rem(LANES - shift + LANES, LANES)
    chunks = [
        pltpu.roll(block[:, j : j + LANES], back, axis=1) for j in range(0, side + LANES, LANES)
    ]
    lane = lax.broadcasted_iota(jnp.int32, (height, LANES), 1)
    keep = lane < LANES - shift
    return jnp.concatenate(
        [jnp.where(keep, chunks[j], chunks[j + 1]) for j in range(len(chunks) - 1)], axis=1
    )


def lay_window(padded, plane, row, col, field):
    height, side = field.shape
    rows = lax.rem(row + 8 * SUBLANES * side, SUBLANES)
    base, shift = col
    tall = height + SUBLANES
    field = jnp.concatenate([field, jnp.zeros((SUBLANES, side), field.dtype)], axis=0)
    field = pltpu.roll(field, rows, axis=0)
    ahead = lax.rem(shift, LANES)
    chunks = [pltpu.roll(field[:, j : j + LANES], ahead, axis=1) for j in range(0, side, LANES)]
    lane = lax.broadcasted_iota(jnp.int32, (tall, LANES), 1)
    keep = lane >= shift
    zero = jnp.zeros((tall, LANES), field.dtype)
    parts = [zero] + chunks + [zero]
    for j in range(len(chunks) + 1):
        padded[plane, j + 1, pl.ds(side // 4, tall)] = jnp.where(keep, parts[j + 1], parts[j])


def add_laid(total, padded, plane, row, col, first, height, side):
    base, _ = col
    shift = side // 4 + 8 * SUBLANES * side
    start = (lax.div(first + shift, SUBLANES) - lax.div(row + 8 * SUBLANES * side, SUBLANES)) * SUBLANES
    count = side // LANES + 1
    for j in range(total.shape[2] // LANES):
        block = j - lax.div(base, LANES)
        inside = jnp.logical_and(block >= 0, block < count)
        source = padded[plane, jnp.where(inside, block + 1, 0), pl.ds(start, height)]
        where = (plane, pl.ds(first, height), pl.ds(j * LANES, LANES))
        total[where] = total[where] + source


def dot(left, right):
    return jnp.dot(left, right, preferred_element_type=jnp.float32)


def narrow(left, right, axis):
    return jnp.concatenate([left, right], axis=axis).astype(jnp.bfloat16)


def forward(field, tables):
    half = field[0].shape[0] // 2
    low, high = [part[:half] for part in field], [part[half:] for part in field]
    even = dot(tables[0], narrow(low[0] + high[0], low[1] + high[1], 0))
    odd = dot(tables[1], narrow(low[0] - high[0], low[1] - high[1], 0))
    middle = [
        jnp.concatenate([even[:half], odd[:half]], axis=0),
        jnp.concatenate([even[half:], odd[half:]], axis=0),
    ]
    low, high = [part[:, :half] for part in middle], [part[:, half:] for part in middle]
    even = dot(narrow(low[0] + high[0], low[1] + high[1], 1), tables[2])
    odd = dot(narrow(low[0] - high[0], low[1] - high[1], 1), tables[3])
    return (
        jnp.concatenate([even[:, :half], odd[:, :half]], axis=1),
        jnp.concatenate([even[:, half:], odd[:, half:]], axis=1),
    )


def inverse(field, tables):
    half = field[0].shape[0] // 2
    even = dot(tables[2], narrow(field[0][:half], field[1][:half], 0))
    odd = dot(tables[3], narrow(field[0][half:], field[1][half:], 0))
    total, rest = even + odd, even - odd
    middle = [
        jnp.concatenate([total[:half], rest[:half]], axis=0),
        jnp.concatenate([total[half:], rest[half:]], axis=0),
    ]
    even = dot(narrow(middle[0][:, :half], middle[1][:, :half], 1), tables[0])
    odd = dot(narrow(middle[0][:, half:], middle[1][:, half:], 1), tables[1])
    total, rest = even + odd, even - odd
    return (
        jnp.concatenate([total[:, :half], rest[:, :half]], axis=1),
        jnp.concatenate([total[:, half:], rest[:, half:]], axis=1),
    )


def even_first(rows):
    array = jnp.concatenate(
        [jnp.concatenate([rows(first, k) for k in range(2)], axis=1) for first in range(2)], axis=0
    )
    side = array.shape[1]
    source = lax.broadcasted_iota(jnp.int32, (side, side), 0)
    target = lax.broadcasted_iota(jnp.int32, (side, side), 1)
    wanted = jnp.where(target < side // 2, 2 * target, 2 * target - side + 1)
    pick = jnp.where(source == wanted, 1.0, 0.0).astype(jnp.bfloat16)
    total = None
    for _ in range(3):
        part = array.astype(jnp.bfloat16)
        array = array - part.astype(jnp.float32)
        moved = dot(part, pick)
        total = moved if total is None else total + moved
    return total


def turn(phase):
    x = phase * 0.5
    y = x * x
    sin = np.float32(1.0 / 6227020800.0)
    for factor in (-39916800.0, 362880.0, -5040.0, 120.0, -6.0, 1.0):
        sin = sin * y + np.float32(1.0 / factor)
    sin = sin * x
    cos = np.float32(-1.0 / 87178291200.0)
    for factor in (479001600.0, -3628800.0, 40320.0, -720.0, 24.0, -2.0, 1.0):
        cos = cos * y + np.float32(1.0 / factor)
    return 1.0 - 2.0 * sin * sin, 2.0 * sin * cos


def multiply(left, right):
    return left[0] * right[0] - left[1] * right[1], left[0] * right[1] + left[1] * right[0]


def multiply_conjugate(left, right):
    return left[0] * right[0] + left[1] * right[1], left[0] * right[1] - left[1] * right[0]


def narrowed(field):
    return tuple(part.astype(jnp.bfloat16).astype(jnp.float32) for part in field)


def one_position(psi0, object0, object1, measured, wave, tables):
    psi1 = narrowed(
        inverse(multiply(wave, forward(multiply(psi0, object0), tables)), tables)
    )
    far = forward(multiply(psi1, object1), tables)
    modulus = jnp.sqrt(far[0] * far[0] + far[1] * far[1])
    factor = 1.0 - measured / jnp.maximum(modulus, modulus_floor)
    g1 = narrowed(inverse((far[0] * factor, far[1] * factor), tables))
    d1 = multiply_conjugate(psi1, g1)
    back = forward(multiply_conjugate(object1, g1), tables)
    g0 = narrowed(inverse(multiply_conjugate(wave, back), tables))
    return multiply_conjugate(psi0, g0), d1


def wide(ref, *index):
    return ref[index + (0,)].astype(jnp.float32), ref[index + (1,)].astype(jnp.float32)


def find(rows, upper, rank):
    seen = jnp.int32(0)
    chosen = jnp.int32(0)
    for position in range(rows.shape[0]):
        here = jnp.where(rows[position] < 0, 1, 0) == upper
        chosen = jnp.where(jnp.logical_and(here, seen == rank), position, chosen)
        seen = seen + jnp.where(here, 1, 0)
    return chosen


def corner(info, upper, rank, side, band_rows):
    position = find(info[0], upper, rank)
    least = jnp.where(upper == 1, -(side // 2), band_rows - side + side // 4)
    row = jnp.minimum(jnp.maximum(info[0][position], least), least + side // 4)
    return row, info[1][position]


class Step:
    def __init__(self, index, region, count, side, band_rows):
        self.index = index
        even = 1 - lax.rem(region, 2)
        self.upper = 1 - even if index == 0 else even
        before = lax.rem(region + count - 1, count)
        after = lax.rem(region + 1, count)
        self.peer = jnp.where(self.upper == 1, before, after)
        half = side // 2
        self.near_low = pl.multiple_of(self.upper * half, half)
        self.far_low = pl.multiple_of((1 - self.upper) * half, half)
        self.peer_upper = 1 - self.upper
        self.peer_offset = (2 * self.peer_upper - 1) * band_rows
        self.peer_far_low = self.near_low


def wave_kernel(
    side, count, scans, choice_any, band, probes_any, amps_any, phase_any, tables_any,
    total,
    ext, probes, amps, phase, wave, tables, measured,
    x_send, x_in, far_send, far_in, own, give, keep, give_in, far_back, strip_send, strip_in,
    near_laid, far_laid, end_laid, here, around, choice,
    local_sem, send_sem, recv_sem,
):
    rim = side // 2
    band_rows = band.shape[1]
    c = lax.axis_index("cuts")
    region = lax.axis_index("region")
    other_cut = 1 - c
    steps = [Step(s, region, count, side, band_rows) for s in range(2)]
    cuts = [(p, k * rim) for p in range(2) for k in range(band_rows // rim)]
    loads = [(scans[0], here[0]), (scans[1], here[1])]
    loads += [
        (band.at[p, pl.ds(low, rim)], ext.at[p, pl.ds(rim + low, rim)]) for p, low in cuts
    ]
    early_loads = len(loads)
    loads += [
        (choice_any, choice), (tables_any, tables), (probes_any, probes),
        *((phase_any.at[:, pl.ds(k * rim, rim)], phase.at[k]) for k in range(2)),
        *((amps_any.at[:, :, pl.ds(k * rim, rim)], amps.at[k]) for k in range(2)),
    ]
    loads = [
        pltpu.make_async_copy(source, target, local_sem.at[k % early_loads if k < 2 * early_loads else k - early_loads])
        for k, (source, target) in enumerate(loads)
    ]
    for load in loads[:early_loads]:
        load.start()
    barrier = pltpu.get_barrier_semaphore()
    early = region == 0
    late = region == count - 1
    for peer in ((other_cut, region), (c, steps[0].peer)):
        pl.semaphore_signal(barrier, 1, device_id=peer, device_id_type=pl.DeviceIdType.MESH)

    @pl.when(jnp.logical_not(late))
    def _():
        pl.semaphore_signal(
            barrier, 1, device_id=(c, steps[1].peer), device_id_type=pl.DeviceIdType.MESH
        )

    with mark("bar"):
        pl.semaphore_wait(barrier, jnp.where(early, 2, 3))
    slots = iter(range(32))

    def remote(source, target, peer, send_slot, recv_slot=None):
        slot = next(slots) if recv_slot is None else recv_slot
        return pltpu.make_async_remote_copy(
            src_ref=source, dst_ref=target,
            send_sem=send_sem.at[send_slot], recv_sem=recv_sem.at[slot],
            device_id=peer, device_id_type=pl.DeviceIdType.MESH,
        )

    across = (other_cut, region)
    halves = [(c, step.peer) for step in steps]
    notes = [[remote(here[k], around[s][k], halves[s], 2 * s + k) for k in range(2)] for s in range(2)]
    near = [pl.ds(step.near_low, rim) for step in steps]
    far = [pl.ds(step.far_low, rim) for step in steps]
    x_near = [remote(x_send.at[s, :, near[s]], x_in.at[s, :, near[s]], across, 4 + 3 * s) for s in range(2)]
    x_far = [
        [remote(x_send.at[s, p, far[s]], x_in.at[s, p, far[s]], across, 5 + 3 * s + p) for p in range(2)]
        for s in range(2)
    ]
    halo = [[remote(far_send.at[0, j], far_in.at[0, j], halves[0], 10 + j) for j in range(2)]]
    halo.append([remote(far_send.at[1, j], far_in.at[1, j], halves[1], 12 + j, 10 + j + 2) for j in range(2)])
    strip = [remote(strip_send.at[p], strip_in.at[p], halves[1], 12 + p, 10 + p + 2) for p in range(2)]
    slots = iter(range(14, 32))
    quarter = side // 4
    rows = []
    for step in steps:
        order = [3 - k + step.upper * (2 * k - 3) for k in range(4)]
        rows.append([pl.ds(pl.multiple_of(k * quarter, quarter), quarter) for k in order])
    give_parts = [
        [
            remote(give.at[0, :, part], give_in.at[0, :, part], across, slot)
            for part, slot in ((far[0], 5), (rows[0][2], 4), (rows[0][3], 6))
        ],
        [
            remote(give.at[1, :, part], give_in.at[1, :, part], across, slot)
            for part, slot in zip(rows[1], (7, 8, 9, 14))
        ],
    ]
    back_other = [[remote(give_in.at[0, :, far[0]], far_back.at[0, 1], halves[0], 0)], []]
    for k in range(2):
        start = pl.multiple_of(jnp.where(steps[1].upper == 1, k, 1 - k) * quarter, quarter)
        back_other[1].append(
            remote(
                give_in.at[1, :, rows[1][k]],
                far_back.at[1, 1, :, pl.ds(start, quarter)],
                halves[1],
                1 + k,
            )
        )
    back_own = [remote(keep.at[s, :, far[s]], far_back.at[s, 0], halves[s], 10 + s) for s in range(2)]
    for load in loads[:2]:
        load.wait()
    for note in notes[0]:
        note.start()

    @pl.when(jnp.logical_not(early))
    def _():
        for note in notes[1]:
            note.start()

    with mark("band"):
        for load in loads[2:early_loads]:
            load.wait()
    for load in loads[early_loads:]:
        load.start()

    ids = lax.broadcasted_iota(jnp.int32, (rim, side), 0)

    def cut_far(s, rank):
        step = steps[s]
        row, col = corner(around[s], step.peer_upper, rank, side, band_rows)
        top = row + step.peer_offset + step.peer_far_low + rim
        return [cut_window(ext, plane, top, col, rim, side) for plane in range(2)]

    def mixed(s, rank, j, plane):
        step = steps[s]
        row, col = corner(here, step.upper, rank, side, band_rows)
        held = cut_window(ext, plane, row + rim + step.far_low, col, rim, side)
        rows = ids + (row + step.far_low)
        outside = jnp.logical_or(rows < 0, rows >= band_rows)
        if s == 1:
            outside = jnp.logical_and(outside, jnp.logical_not(early))
        return jnp.where(outside, far_in[s, j, plane].astype(jnp.float32), held)

    def near_half(s, rank, plane):
        step = steps[s]
        row, col = corner(here, step.upper, rank, side, band_rows)
        return cut_window(ext, plane, row + rim + step.near_low, col, rim, side)

    def cut_near(s):
        for plane in range(2):
            x_send[s, plane, near[s]] = near_half(s, other_cut, plane).astype(jnp.bfloat16)

    def cut_halo(s, j):
        for plane, part in enumerate(cut_far(s, (other_cut, c)[j])):
            far_send[s, j, plane] = part.astype(jnp.bfloat16)

    def send_far(s, plane):
        with mark("far"):
            x_send[s, plane, far[s]] = mixed(s, other_cut, 0, plane).astype(jnp.bfloat16)
            x_far[s][plane].start()

    def send_strip_far(plane):
        with mark("wstrip"):
            strip[plane].wait_recv()
        rows = pl.ds(pl.multiple_of((1 - steps[1].upper) * (rim + band_rows), rim), rim)
        ext[plane, rows] = strip_in[plane].astype(jnp.float32)
        send_far(1, plane)

    def gather_own(s):
        for plane in range(2):
            own[s, plane, near[s]] = near_half(s, c, plane)
            own[s, plane, far[s]] = mixed(s, c, 1, plane)

    def send_strip(plane):
        rows = pl.ds(pl.multiple_of(rim + steps[1].peer_upper * (band_rows - rim), rim), rim)
        strip_send[plane] = ext[plane, rows].astype(jnp.bfloat16)
        strip[plane].start()

    def add_near(s, rank, source):
        step = steps[s]
        row, col = corner(here, step.upper, rank, side, band_rows)
        low = pl.multiple_of(step.upper * quarter, quarter)
        first = pl.multiple_of((1 - step.upper) * quarter, quarter)
        place = split_col(col, total.shape[2], side)
        for plane in range(2):
            part = source[s, plane, pl.ds(low, side - quarter)].astype(jnp.float32)
            lay_window(near_laid, plane, row + low, place, part)
            add_laid(total, near_laid, plane, row + low, place, first, side - quarter, side)

    def add_far(s, j, planes=(0, 1)):
        step = steps[s]
        row, col = corner(around[s], step.peer_upper, (c, other_cut)[j], side, band_rows)
        top = row + step.peer_offset + step.peer_far_low
        first = pl.multiple_of(step.peer_upper * rim, rim)
        place = split_col(col, total.shape[2], side)
        for plane in planes:
            part = far_back[s, j, plane].astype(jnp.float32)
            lay_window(far_laid, plane, top, place, part)
            add_laid(total, far_laid, plane, top, place, first, rim, side)

    def add_middle(s, rank, source):
        step = steps[s]
        row, col = corner(here, step.upper, rank, side, band_rows)
        first = pl.multiple_of((1 - step.upper) * rim, rim)
        place = split_col(col, total.shape[2], side)
        for plane in range(2):
            part = source[s, plane, pl.ds(quarter, rim)].astype(jnp.float32)
            lay_window(far_laid, plane, row + quarter, place, part)
            add_laid(total, far_laid, plane, row + quarter, place, first, rim, side)

    def add_end(s, rank, source, planes=(0, 1)):
        step = steps[s]
        row, col = corner(here, step.upper, rank, side, band_rows)
        low = pl.multiple_of(step.upper * 3 * quarter, quarter)
        place = split_col(col, total.shape[2], side)
        for plane in planes:
            part = source[s, plane, pl.ds(low, quarter)].astype(jnp.float32)
            lay_window(end_laid, plane, row + low, place, part)
            add_laid(total, end_laid, plane, row + low, place, quarter, rim, side)

    def position_of(s):
        position = find(here[0], steps[s].upper, c)
        psi0 = wide(probes, choice[position])
        with mark("wx"):
            for copy in [x_near[s]] + x_far[s]:
                copy.wait_recv()
        mine = tuple(own[s, plane] for plane in range(2))
        theirs = tuple(x_in[s, plane].astype(jnp.float32) for plane in range(2))
        object0 = tuple(jnp.where(first, x, y) for x, y in zip(mine, theirs))
        object1 = tuple(jnp.where(first, y, x) for x, y in zip(mine, theirs))
        with mark("pos"):
            d0, d1 = one_position(psi0, object0, object1, measured[s], (wave[0], wave[1]), tables)
        for plane in range(2):
            give[s, plane] = jnp.where(first, d1[plane], d0[plane]).astype(jnp.bfloat16)
            keep[s, plane] = jnp.where(first, d0[plane], d1[plane]).astype(jnp.bfloat16)

    first = c == 0
    with mark("near0"):
        cut_near(0)
        x_near[0].start()

    with mark("wnote"):
        for note in notes[0]:
            note.wait_recv()
    cut_halo(0, 0)
    halo[0][0].start()

    @pl.when(late)
    def _():
        send_strip(0)

    @pl.when(jnp.logical_not(jnp.logical_or(early, late)))
    def _():
        with mark("wnote"):
            for note in notes[1]:
                note.wait_recv()
        cut_halo(1, 0)
        halo[1][0].start()

    with mark("wh0"):
        halo[0][0].wait_recv()
    for plane in range(2):
        send_far(0, plane)
    cut_halo(0, 1)
    halo[0][1].start()
    with mark("prep"):
        cut_near(1)
        for load in loads[early_loads:]:
            load.wait()
        wave[0], wave[1] = turn(
            even_first(lambda first, k: phase[k, pl.ds(first, rim, stride=2), :])
        )

        @pl.when(late)
        def _():
            send_strip(1)

        halo[0][1].wait_recv()
        gather_own(0)
        for s in range(2):
            position = find(here[0], steps[s].upper, c)
            measured[s] = even_first(
                lambda first, k: amps[k, position, pl.ds(first, rim, stride=2), :]
            )
        near_laid[...] = jnp.zeros_like(near_laid)
        far_laid[...] = jnp.zeros_like(far_laid)
        end_laid[...] = jnp.zeros_like(end_laid)
        total[...] = jnp.zeros_like(total)

    @pl.when(early)
    def _():
        with mark("wnote"):
            for note in notes[1]:
                note.wait_recv()
        cut_halo(1, 0)
        halo[1][0].start()
        for note in notes[1]:
            note.start()

    with mark("wsA"):
        x_near[0].wait_send()
        x_far[0][0].wait_send()
    x_near[1].start()

    @pl.when(jnp.logical_not(early))
    def _():
        with mark("wh1"):
            halo[1][0].wait_recv()
        for plane in range(2):
            send_far(1, plane)

    @pl.when(jnp.logical_not(late))
    def _():
        cut_halo(1, 1)
        halo[1][1].start()

    for copy in notes[0] + notes[1] + halo[0]:
        copy.wait_send()
    position_of(0)
    back_own[0].start()

    @pl.when(early)
    def _():
        for plane in range(2):
            send_strip_far(plane)

    give_parts[0][1].start()

    @pl.when(early)
    def _():
        give_parts[0][0].start()
        gather_own(1)

    with mark("wsB"):
        for copy in [x_far[0][1], x_near[1]] + x_far[1]:
            copy.wait_send()

    @pl.when(jnp.logical_not(early))
    def _():
        give_parts[0][0].start()
        with mark("wh1"):
            halo[1][1].wait_recv()
        gather_own(1)

    with mark("add"):
        add_near(0, c, keep)
    position_of(1)
    for copy in give_parts[1][:2]:
        copy.start()

    @pl.when(early)
    def _():
        for copy in give_parts[0][2:] + give_parts[1][2:]:
            copy.start()

    back_own[1].start()
    with mark("wgf0"):
        for part, back in zip(give_parts[0], back_other[0]):
            part.wait_recv()
            back.start()
    with mark("add"):
        back_own[0].wait_recv()
        add_far(0, 0)
        add_near(1, c, keep)

    @pl.when(late)
    def _():
        for note in notes[1]:
            note.wait_recv()

    with mark("wsC"):
        for copy in give_parts[0][:2] + give_parts[1][:2]:
            copy.wait_send()

    @pl.when(jnp.logical_not(early))
    def _():
        for copy in give_parts[0][2:] + give_parts[1][2:]:
            copy.start()

    @pl.when(late)
    def _():
        for copy in strip:
            copy.wait_send()

    @pl.when(jnp.logical_not(late))
    def _():
        for copy in halo[1]:
            copy.wait_send()

    back_own[0].wait_send()
    with mark("wgf1"):
        for part, back in zip(give_parts[1], back_other[1]):
            part.wait_recv()
            back.start()
    with mark("add"):
        for copy in back_other[0]:
            copy.wait_recv()
        add_far(0, 1)
    with mark("add"):
        back_own[1].wait_recv()
        add_far(1, 0)
    for copy in [back_own[1]] + back_other[0]:
        copy.wait_send()
    with mark("wgn0"):
        for copy in give_parts[0][1:]:
            copy.wait_recv()
    with mark("add"):
        add_near(0, other_cut, give_in)
    with mark("wgn"):
        give_parts[1][2].wait_recv()
    with mark("add"):
        add_middle(1, other_cut, give_in)
    for copy in give_parts[0][2:] + give_parts[1][2:]:
        copy.wait_send()

    def last_rows():
        with mark("wgn"):
            give_parts[1][3].wait_recv()
        add_end(1, other_cut, give_in)

    def last_peer_rows():
        with mark("wend"):
            for copy in back_other[1]:
                copy.wait_recv()
        add_far(1, 1)

    for copy in back_other[1]:
        copy.wait_send()
    order = (last_peer_rows, last_rows)

    @pl.when(steps[1].upper == 1)
    def _():
        for part in order:
            part()

    @pl.when(steps[1].upper == 0)
    def _():
        for part in order[::-1]:
            part()


def shards(objects, probes, amplitudes, prop_phase, scan_rows, scan_cols, probe_choice):
    side = probes.shape[-1]
    rim = side // 2
    count = lax.axis_size("region")
    band = objects[0]
    band_rows, columns = band.shape[1:]
    tables = dft_blocks(side)
    whole = (2, 2, side, side)
    half = (2, 2, 2, rim, side)
    slot = lambda shape: pltpu.VMEM(shape, jnp.bfloat16)
    tall = pltpu.VMEM((2, band_rows + 2 * rim + SUBLANES, columns), jnp.float32)
    HBM = pl.BlockSpec(memory_space=pltpu.HBM)
    scalars = pltpu.SMEM(scan_rows.shape, jnp.int32)
    laid = lambda rows: pltpu.VMEM((2, side // LANES + 2, rows, LANES), jnp.float32)
    out = pl.pallas_call(
        functools.partial(wave_kernel, side, count),
        out_shape=jax.ShapeDtypeStruct(band.shape, jnp.float32),
        in_specs=[(HBM, HBM)] + [HBM] * 6,
        out_specs=VMEM,
        scratch_shapes=[
            tall,
            pltpu.VMEM(probes.shape, probes.dtype),
            pltpu.VMEM((2,) + amplitudes.shape[:2] + (rim,), jnp.float32),
            pltpu.VMEM((2, side, rim), jnp.float32),
            pltpu.VMEM((2,) + prop_phase.shape, jnp.float32),
            pltpu.VMEM(tables.shape, tables.dtype),
            pltpu.VMEM((2, side, side), jnp.float32),
            slot(whole), slot(whole), slot(half), slot(half),
            pltpu.VMEM(whole, jnp.float32), slot(whole), slot(whole), slot(whole), slot(half),
            slot((2, rim, columns)), slot((2, rim, columns)),
            laid(side + side // 4), laid(side), laid(side - side // 4),
            (scalars,) * 2, ((scalars,) * 2,) * 2, scalars,
            pltpu.SemaphoreType.DMA((7,)),
            pltpu.SemaphoreType.DMA((15,)),
            pltpu.SemaphoreType.DMA((26,)),
        ],
        compiler_params=pltpu.CompilerParams(
            collective_id=0, has_side_effects=True, vmem_limit_bytes=32 * 1024 * 1024
        ),
    )(*jax.tree.map(
        lambda x: pltpu.with_memory_space_constraint(x, pltpu.HBM),
        ((scan_rows, scan_cols), probe_choice, band, probes, amplitudes, prop_phase, tables),
    ))
    return out[None]


def solution(mesh):
    return jax.shard_map(
        shards,
        mesh=mesh,
        in_specs=(
            P("cuts", None, "region", None),
            P(),
            P("region", None, None),
            P(),
            P("region"),
            P("region"),
            P("region"),
        ),
        out_specs=P("cuts", None, "region", None),
        check_vma=False,
    )
```

```python
import contextlib
import functools
import jax
import jax.numpy as jnp
import numpy as np
from jax import lax
from jax.experimental import pallas as pl
from jax.experimental.pallas import tpu as pltpu
from jax.sharding import PartitionSpec as P

modulus_floor = 0.25
LANES = 128
SUBLANES = 8
VMEM = pl.BlockSpec(memory_space=pltpu.VMEM)


def mark(name):
    return contextlib.nullcontext()


def dft_blocks(side):
    half = side // 2
    indices = np.arange(side)
    angles = (indices[:, None] * indices[None, :] % side) * (2.0 * np.pi / side)
    real = np.cos(angles) / np.sqrt(side)
    imag = np.sin(angles) / np.sqrt(side)
    tables = []
    for odd in range(2):
        cos, sin = real[:half, odd::2], imag[:half, odd::2]
        tables.append(np.block([[cos.T, sin.T], [-sin.T, cos.T]]))
    for odd in range(2):
        cos, sin = real[:half, odd::2], imag[:half, odd::2]
        tables.append(np.block([[cos, -sin], [sin, cos]]))
    return jnp.asarray(np.stack(tables), dtype=jnp.bfloat16)


def split_col(col, cols, side):
    base = jnp.minimum(lax.div(col, LANES), (cols - side) // LANES - 1) * LANES
    return base, col - base


def cut_window(ext, plane, row, col, height, side):
    base, shift = split_col(col, ext.shape[2], side)
    top = lax.div(row, SUBLANES) * SUBLANES
    tall = height + SUBLANES
    block = ext[plane, pl.ds(top, tall), pl.ds(base, side + LANES)]
    block = pltpu.roll(block, lax.rem(tall + top - row, tall), axis=0)[:height]
    back = lax.rem(LANES - shift + LANES, LANES)
    chunks = [
        pltpu.roll(block[:, j : j + LANES], back, axis=1) for j in range(0, side + LANES, LANES)
    ]
    lane = lax.broadcasted_iota(jnp.int32, (height, LANES), 1)
    keep = lane < LANES - shift
    return jnp.concatenate(
        [jnp.where(keep, chunks[j], chunks[j + 1]) for j in range(len(chunks) - 1)], axis=1
    )


def lay_window(padded, plane, row, col, field):
    height, side = field.shape
    rows = lax.rem(row + 8 * SUBLANES * side, SUBLANES)
    base, shift = col
    tall = height + SUBLANES
    field = jnp.concatenate([field, jnp.zeros((SUBLANES, side), field.dtype)], axis=0)
    field = pltpu.roll(field, rows, axis=0)
    ahead = lax.rem(shift, LANES)
    chunks = [pltpu.roll(field[:, j : j + LANES], ahead, axis=1) for j in range(0, side, LANES)]
    lane = lax.broadcasted_iota(jnp.int32, (tall, LANES), 1)
    keep = lane >= shift
    zero = jnp.zeros((tall, LANES), field.dtype)
    parts = [zero] + chunks + [zero]
    for j in range(len(chunks) + 1):
        padded[plane, j + 1, pl.ds(side // 4, tall)] = jnp.where(keep, parts[j + 1], parts[j])


def add_laid(total, padded, plane, row, col, first, height, side):
    base, _ = col
    shift = side // 4 + 8 * SUBLANES * side
    start = (lax.div(first + shift, SUBLANES) - lax.div(row + 8 * SUBLANES * side, SUBLANES)) * SUBLANES
    count = side // LANES + 1
    for j in range(total.shape[2] // LANES):
        block = j - lax.div(base, LANES)
        inside = jnp.logical_and(block >= 0, block < count)
        source = padded[plane, jnp.where(inside, block + 1, 0), pl.ds(start, height)]
        where = (plane, pl.ds(first, height), pl.ds(j * LANES, LANES))
        total[where] = total[where] + source


def dot(left, right):
    return jnp.dot(left, right, preferred_element_type=jnp.float32)


def narrow(left, right, axis):
    return jnp.concatenate([left, right], axis=axis).astype(jnp.bfloat16)


def forward(field, tables):
    half = field[0].shape[0] // 2
    low, high = [part[:half] for part in field], [part[half:] for part in field]
    even = dot(tables[0], narrow(low[0] + high[0], low[1] + high[1], 0))
    odd = dot(tables[1], narrow(low[0] - high[0], low[1] - high[1], 0))
    middle = [
        jnp.concatenate([even[:half], odd[:half]], axis=0),
        jnp.concatenate([even[half:], odd[half:]], axis=0),
    ]
    low, high = [part[:, :half] for part in middle], [part[:, half:] for part in middle]
    even = dot(narrow(low[0] + high[0], low[1] + high[1], 1), tables[2])
    odd = dot(narrow(low[0] - high[0], low[1] - high[1], 1), tables[3])
    return (
        jnp.concatenate([even[:, :half], odd[:, :half]], axis=1),
        jnp.concatenate([even[:, half:], odd[:, half:]], axis=1),
    )


def inverse(field, tables):
    half = field[0].shape[0] // 2
    even = dot(tables[2], narrow(field[0][:half], field[1][:half], 0))
    odd = dot(tables[3], narrow(field[0][half:], field[1][half:], 0))
    total, rest = even + odd, even - odd
    middle = [
        jnp.concatenate([total[:half], rest[:half]], axis=0),
        jnp.concatenate([total[half:], rest[half:]], axis=0),
    ]
    even = dot(narrow(middle[0][:, :half], middle[1][:, :half], 1), tables[0])
    odd = dot(narrow(middle[0][:, half:], middle[1][:, half:], 1), tables[1])
    total, rest = even + odd, even - odd
    return (
        jnp.concatenate([total[:, :half], rest[:, :half]], axis=1),
        jnp.concatenate([total[:, half:], rest[:, half:]], axis=1),
    )


def even_first(rows):
    array = jnp.concatenate(
        [jnp.concatenate([rows(first, k) for k in range(2)], axis=1) for first in range(2)], axis=0
    )
    side = array.shape[1]
    source = lax.broadcasted_iota(jnp.int32, (side, side), 0)
    target = lax.broadcasted_iota(jnp.int32, (side, side), 1)
    wanted = jnp.where(target < side // 2, 2 * target, 2 * target - side + 1)
    pick = jnp.where(source == wanted, 1.0, 0.0).astype(jnp.bfloat16)
    total = None
    for _ in range(3):
        part = array.astype(jnp.bfloat16)
        array = array - part.astype(jnp.float32)
        moved = dot(part, pick)
        total = moved if total is None else total + moved
    return total


def turn(phase):
    x = phase * 0.5
    y = x * x
    sin = np.float32(1.0 / 6227020800.0)
    for factor in (-39916800.0, 362880.0, -5040.0, 120.0, -6.0, 1.0):
        sin = sin * y + np.float32(1.0 / factor)
    sin = sin * x
    cos = np.float32(-1.0 / 87178291200.0)
    for factor in (479001600.0, -3628800.0, 40320.0, -720.0, 24.0, -2.0, 1.0):
        cos = cos * y + np.float32(1.0 / factor)
    return 1.0 - 2.0 * sin * sin, 2.0 * sin * cos


def multiply(left, right):
    return left[0] * right[0] - left[1] * right[1], left[0] * right[1] + left[1] * right[0]


def multiply_conjugate(left, right):
    return left[0] * right[0] + left[1] * right[1], left[0] * right[1] - left[1] * right[0]


def narrowed(field):
    return tuple(part.astype(jnp.bfloat16).astype(jnp.float32) for part in field)


def one_position(psi0, object0, object1, measured, wave, tables):
    psi1 = narrowed(
        inverse(multiply(wave, forward(multiply(psi0, object0), tables)), tables)
    )
    far = forward(multiply(psi1, object1), tables)
    modulus = jnp.sqrt(far[0] * far[0] + far[1] * far[1])
    factor = 1.0 - measured / jnp.maximum(modulus, modulus_floor)
    g1 = narrowed(inverse((far[0] * factor, far[1] * factor), tables))
    d1 = multiply_conjugate(psi1, g1)
    back = forward(multiply_conjugate(object1, g1), tables)
    g0 = narrowed(inverse(multiply_conjugate(wave, back), tables))
    return multiply_conjugate(psi0, g0), d1


def wide(ref, *index):
    return ref[index + (0,)].astype(jnp.float32), ref[index + (1,)].astype(jnp.float32)


def find(rows, upper, rank):
    seen = jnp.int32(0)
    chosen = jnp.int32(0)
    for position in range(rows.shape[0]):
        here = jnp.where(rows[position] < 0, 1, 0) == upper
        chosen = jnp.where(jnp.logical_and(here, seen == rank), position, chosen)
        seen = seen + jnp.where(here, 1, 0)
    return chosen


def corner(info, upper, rank, side, band_rows):
    position = find(info[0], upper, rank)
    least = jnp.where(upper == 1, -(side // 2), band_rows - side + side // 4)
    row = jnp.minimum(jnp.maximum(info[0][position], least), least + side // 4)
    return row, info[1][position]


class Step:
    def __init__(self, index, region, count, side, band_rows):
        self.index = index
        even = 1 - lax.rem(region, 2)
        self.upper = 1 - even if index == 0 else even
        before = lax.rem(region + count - 1, count)
        after = lax.rem(region + 1, count)
        self.peer = jnp.where(self.upper == 1, before, after)
        half = side // 2
        self.near_low = pl.multiple_of(self.upper * half, half)
        self.far_low = pl.multiple_of((1 - self.upper) * half, half)
        self.peer_upper = 1 - self.upper
        self.peer_offset = (2 * self.peer_upper - 1) * band_rows
        self.peer_far_low = self.near_low


def wave_kernel(
    side, count, scans, choice_any, band, probes_any, amps_any, phase_any, tables_any,
    total,
    ext, probes, amps, phase, wave, tables, measured,
    x_send, x_in, far_send, far_in, own, give, keep, give_in, far_back, detour, strip_send, strip_in,
    near_laid, far_laid, end_laid, here, around, choice,
    local_sem, send_sem, recv_sem,
):
    rim = side // 2
    band_rows = band.shape[1]
    c = lax.axis_index("cuts")
    region = lax.axis_index("region")
    other_cut = 1 - c
    steps = [Step(s, region, count, side, band_rows) for s in range(2)]
    cuts = [(p, k * rim) for p in range(2) for k in range(band_rows // rim)]
    loads = [(scans[0], here[0]), (scans[1], here[1])]
    loads += [
        (band.at[p, pl.ds(low, rim)], ext.at[p, pl.ds(rim + low, rim)]) for p, low in cuts
    ]
    early_loads = len(loads)
    loads += [
        (choice_any, choice), (tables_any, tables), (probes_any, probes),
        *((phase_any.at[:, pl.ds(k * rim, rim)], phase.at[k]) for k in range(2)),
        *((amps_any.at[:, :, pl.ds(k * rim, rim)], amps.at[k]) for k in range(2)),
    ]
    loads = [
        pltpu.make_async_copy(source, target, local_sem.at[k % early_loads if k < 2 * early_loads else k - early_loads])
        for k, (source, target) in enumerate(loads)
    ]
    for load in loads[:early_loads]:
        load.start()
    barrier = pltpu.get_barrier_semaphore()
    early = region == 0
    late = region == count - 1
    for peer in ((other_cut, region), (c, steps[0].peer)):
        pl.semaphore_signal(barrier, 1, device_id=peer, device_id_type=pl.DeviceIdType.MESH)

    @pl.when(jnp.logical_not(late))
    def _():
        pl.semaphore_signal(
            barrier, 1, device_id=(c, steps[1].peer), device_id_type=pl.DeviceIdType.MESH
        )

    with mark("bar"):
        pl.semaphore_wait(barrier, jnp.where(early, 2, 3))
    slots = iter(range(32))

    def remote(source, target, peer, send_slot, recv_slot=None):
        slot = next(slots) if recv_slot is None else recv_slot
        return pltpu.make_async_remote_copy(
            src_ref=source, dst_ref=target,
            send_sem=send_sem.at[send_slot], recv_sem=recv_sem.at[slot],
            device_id=peer, device_id_type=pl.DeviceIdType.MESH,
        )

    across = (other_cut, region)
    halves = [(c, step.peer) for step in steps]
    notes = [[remote(here[k], around[s][k], halves[s], 2 * s + k) for k in range(2)] for s in range(2)]
    near = [pl.ds(step.near_low, rim) for step in steps]
    far = [pl.ds(step.far_low, rim) for step in steps]
    x_near = [remote(x_send.at[s, :, near[s]], x_in.at[s, :, near[s]], across, 4 + 3 * s) for s in range(2)]
    x_far = [
        [remote(x_send.at[s, p, far[s]], x_in.at[s, p, far[s]], across, 5 + 3 * s + p) for p in range(2)]
        for s in range(2)
    ]
    halo = [[remote(far_send.at[0, j], far_in.at[0, j], halves[0], 10 + j) for j in range(2)]]
    halo.append([remote(far_send.at[1, j], far_in.at[1, j], halves[1], 12 + j, 10 + j + 2) for j in range(2)])
    strip = [remote(strip_send.at[p], strip_in.at[p], halves[1], 12 + p, 10 + p + 2) for p in range(2)]
    slots = iter(range(14, 32))
    quarter = side // 4
    rows = []
    for step in steps:
        order = [3 - k + step.upper * (2 * k - 3) for k in range(4)]
        rows.append([pl.ds(pl.multiple_of(k * quarter, quarter), quarter) for k in order])
    give_parts = [
        [
            remote(give.at[0, :, part], give_in.at[0, :, part], across, slot)
            for part, slot in ((far[0], 5), (rows[0][2], 4), (rows[0][3], 6))
        ],
        [
            remote(give.at[1, :, part], give_in.at[1, :, part], across, slot)
            for part, slot in zip(rows[1], (7, 8, 9, 14))
        ],
    ]
    back_other = [[remote(give_in.at[0, :, far[0]], far_back.at[0, 1], halves[0], 0)], []]
    for k in range(2):
        start = pl.multiple_of(jnp.where(steps[1].upper == 1, k, 1 - k) * quarter, quarter)
        back_other[1].append(
            remote(
                give_in.at[1, :, rows[1][k]],
                far_back.at[1, 1, :, pl.ds(start, quarter)],
                halves[1],
                1 + k,
            )
        )
    first_leg = remote(give.at[1, :, rows[1][0]], detour, halves[1], 7, 26)
    second_leg = remote(detour, far_back.at[1, 1, :, pl.ds(0, quarter)], across, 15, 22)
    back_own = [remote(keep.at[s, :, far[s]], far_back.at[s, 0], halves[s], 10 + s) for s in range(2)]
    for load in loads[:2]:
        load.wait()
    for note in notes[0]:
        note.start()

    @pl.when(jnp.logical_not(early))
    def _():
        for note in notes[1]:
            note.start()

    with mark("band"):
        for load in loads[2:early_loads]:
            load.wait()
    for load in loads[early_loads:]:
        load.start()

    ids = lax.broadcasted_iota(jnp.int32, (rim, side), 0)

    def cut_far(s, rank):
        step = steps[s]
        row, col = corner(around[s], step.peer_upper, rank, side, band_rows)
        top = row + step.peer_offset + step.peer_far_low + rim
        return [cut_window(ext, plane, top, col, rim, side) for plane in range(2)]

    def mixed(s, rank, j, plane):
        step = steps[s]
        row, col = corner(here, step.upper, rank, side, band_rows)
        held = cut_window(ext, plane, row + rim + step.far_low, col, rim, side)
        rows = ids + (row + step.far_low)
        outside = jnp.logical_or(rows < 0, rows >= band_rows)
        if s == 1:
            outside = jnp.logical_and(outside, jnp.logical_not(early))
        return jnp.where(outside, far_in[s, j, plane].astype(jnp.float32), held)

    def near_half(s, rank, plane):
        step = steps[s]
        row, col = corner(here, step.upper, rank, side, band_rows)
        return cut_window(ext, plane, row + rim + step.near_low, col, rim, side)

    def cut_near(s):
        for plane in range(2):
            x_send[s, plane, near[s]] = near_half(s, other_cut, plane).astype(jnp.bfloat16)

    def cut_halo(s, j):
        for plane, part in enumerate(cut_far(s, (other_cut, c)[j])):
            far_send[s, j, plane] = part.astype(jnp.bfloat16)

    def send_far(s, plane):
        with mark("far"):
            x_send[s, plane, far[s]] = mixed(s, other_cut, 0, plane).astype(jnp.bfloat16)
            x_far[s][plane].start()

    def send_strip_far(plane):
        with mark("wstrip"):
            strip[plane].wait_recv()
        rows = pl.ds(pl.multiple_of((1 - steps[1].upper) * (rim + band_rows), rim), rim)
        ext[plane, rows] = strip_in[plane].astype(jnp.float32)
        send_far(1, plane)

    def gather_own(s):
        for plane in range(2):
            own[s, plane, near[s]] = near_half(s, c, plane)
            own[s, plane, far[s]] = mixed(s, c, 1, plane)

    def send_strip(plane):
        rows = pl.ds(pl.multiple_of(rim + steps[1].peer_upper * (band_rows - rim), rim), rim)
        strip_send[plane] = ext[plane, rows].astype(jnp.bfloat16)
        strip[plane].start()

    def add_near(s, rank, source):
        step = steps[s]
        row, col = corner(here, step.upper, rank, side, band_rows)
        low = pl.multiple_of(step.upper * quarter, quarter)
        first = pl.multiple_of((1 - step.upper) * quarter, quarter)
        place = split_col(col, total.shape[2], side)
        for plane in range(2):
            part = source[s, plane, pl.ds(low, side - quarter)].astype(jnp.float32)
            lay_window(near_laid, plane, row + low, place, part)
            add_laid(total, near_laid, plane, row + low, place, first, side - quarter, side)

    def add_far(s, j, planes=(0, 1)):
        step = steps[s]
        row, col = corner(around[s], step.peer_upper, (c, other_cut)[j], side, band_rows)
        top = row + step.peer_offset + step.peer_far_low
        first = pl.multiple_of(step.peer_upper * rim, rim)
        place = split_col(col, total.shape[2], side)
        for plane in planes:
            part = far_back[s, j, plane].astype(jnp.float32)
            lay_window(far_laid, plane, top, place, part)
            add_laid(total, far_laid, plane, top, place, first, rim, side)

    def add_middle(s, rank, source):
        step = steps[s]
        row, col = corner(here, step.upper, rank, side, band_rows)
        first = pl.multiple_of((1 - step.upper) * rim, rim)
        place = split_col(col, total.shape[2], side)
        for plane in range(2):
            part = source[s, plane, pl.ds(quarter, rim)].astype(jnp.float32)
            lay_window(far_laid, plane, row + quarter, place, part)
            add_laid(total, far_laid, plane, row + quarter, place, first, rim, side)

    def add_end(s, rank, source, planes=(0, 1)):
        step = steps[s]
        row, col = corner(here, step.upper, rank, side, band_rows)
        low = pl.multiple_of(step.upper * 3 * quarter, quarter)
        place = split_col(col, total.shape[2], side)
        for plane in planes:
            part = source[s, plane, pl.ds(low, quarter)].astype(jnp.float32)
            lay_window(end_laid, plane, row + low, place, part)
            add_laid(total, end_laid, plane, row + low, place, quarter, rim, side)

    def position_of(s):
        position = find(here[0], steps[s].upper, c)
        psi0 = wide(probes, choice[position])
        with mark("wx"):
            for copy in [x_near[s]] + x_far[s]:
                copy.wait_recv()
        mine = tuple(own[s, plane] for plane in range(2))
        theirs = tuple(x_in[s, plane].astype(jnp.float32) for plane in range(2))
        object0 = tuple(jnp.where(first, x, y) for x, y in zip(mine, theirs))
        object1 = tuple(jnp.where(first, y, x) for x, y in zip(mine, theirs))
        with mark("pos"):
            d0, d1 = one_position(psi0, object0, object1, measured[s], (wave[0], wave[1]), tables)
        for plane in range(2):
            give[s, plane] = jnp.where(first, d1[plane], d0[plane]).astype(jnp.bfloat16)
            keep[s, plane] = jnp.where(first, d0[plane], d1[plane]).astype(jnp.bfloat16)

    first = c == 0
    with mark("near0"):
        cut_near(0)
        x_near[0].start()

    with mark("wnote"):
        for note in notes[0]:
            note.wait_recv()
    cut_halo(0, 0)
    halo[0][0].start()

    @pl.when(late)
    def _():
        send_strip(0)

    @pl.when(jnp.logical_not(jnp.logical_or(early, late)))
    def _():
        with mark("wnote"):
            for note in notes[1]:
                note.wait_recv()
        cut_halo(1, 0)
        halo[1][0].start()

    with mark("wh0"):
        halo[0][0].wait_recv()
    for plane in range(2):
        send_far(0, plane)
    cut_halo(0, 1)
    halo[0][1].start()
    with mark("prep"):
        cut_near(1)
        for load in loads[early_loads:]:
            load.wait()
        wave[0], wave[1] = turn(
            even_first(lambda first, k: phase[k, pl.ds(first, rim, stride=2), :])
        )

        @pl.when(late)
        def _():
            send_strip(1)

        halo[0][1].wait_recv()
        gather_own(0)
        for s in range(2):
            position = find(here[0], steps[s].upper, c)
            measured[s] = even_first(
                lambda first, k: amps[k, position, pl.ds(first, rim, stride=2), :]
            )
        near_laid[...] = jnp.zeros_like(near_laid)
        far_laid[...] = jnp.zeros_like(far_laid)
        end_laid[...] = jnp.zeros_like(end_laid)
        total[...] = jnp.zeros_like(total)

    @pl.when(early)
    def _():
        with mark("wnote"):
            for note in notes[1]:
                note.wait_recv()
        cut_halo(1, 0)
        halo[1][0].start()
        for note in notes[1]:
            note.start()

    with mark("wsA"):
        x_near[0].wait_send()
        x_far[0][0].wait_send()
    x_near[1].start()

    @pl.when(jnp.logical_not(early))
    def _():
        with mark("wh1"):
            halo[1][0].wait_recv()
        for plane in range(2):
            send_far(1, plane)

    @pl.when(jnp.logical_not(late))
    def _():
        cut_halo(1, 1)
        halo[1][1].start()

    for copy in notes[0] + notes[1] + halo[0]:
        copy.wait_send()
    position_of(0)
    back_own[0].start()

    @pl.when(early)
    def _():
        for plane in range(2):
            send_strip_far(plane)

    @pl.when(early)
    def _():
        gather_own(1)

    @pl.when(jnp.logical_not(early))
    def _():
        give_parts[0][1].start()

    with mark("wsB"):
        for copy in [x_far[0][1], x_near[1]] + x_far[1]:
            copy.wait_send()
    give_parts[0][0].start()

    @pl.when(early)
    def _():
        for copy in give_parts[0][1:]:
            copy.start()

    @pl.when(jnp.logical_not(early))
    def _():
        with mark("wh1"):
            halo[1][1].wait_recv()
        gather_own(1)

    with mark("add"):
        add_near(0, c, keep)
    position_of(1)
    @pl.when(early)
    def _():
        first_leg.start()

    @pl.when(jnp.logical_not(early))
    def _():
        give_parts[1][0].start()

    give_parts[1][1].start()

    @pl.when(early)
    def _():
        for copy in give_parts[1][2:]:
            copy.start()

    @pl.when(region == 1)
    def _():
        for copy in give_parts[0][2:] + give_parts[1][2:]:
            copy.start()

    back_own[1].start()
    with mark("wgf0"):
        for part, back in zip(give_parts[0], back_other[0]):
            part.wait_recv()
            back.start()
    with mark("add"):
        back_own[0].wait_recv()
        add_far(0, 0)
        add_near(1, c, keep)

    @pl.when(late)
    def _():
        for note in notes[1]:
            note.wait_recv()

    with mark("wsC"):
        for copy in give_parts[0][:2] + give_parts[1][:2]:
            copy.wait_send()

    @pl.when(region > 1)
    def _():
        for copy in give_parts[0][2:] + give_parts[1][2:]:
            copy.start()

    @pl.when(late)
    def _():
        for copy in strip:
            copy.wait_send()

    @pl.when(jnp.logical_not(late))
    def _():
        for copy in halo[1]:
            copy.wait_send()

    back_own[0].wait_send()
    with mark("wgf1"):

        @pl.when(jnp.logical_not(early))
        def _():
            give_parts[1][0].wait_recv()
            back_other[1][0].start()

        give_parts[1][1].wait_recv()
        back_other[1][1].start()

    with mark("add"):
        for copy in back_other[0]:
            copy.wait_recv()
        add_far(0, 1)
    with mark("add"):
        back_own[1].wait_recv()
        add_far(1, 0)
    for copy in [back_own[1]] + back_other[0]:
        copy.wait_send()
    with mark("wgn0"):
        for copy in give_parts[0][1:]:
            copy.wait_recv()
    with mark("add"):
        add_near(0, other_cut, give_in)
    @pl.when(late)
    def _():
        first_leg.wait_recv()
        second_leg.start()

    with mark("wgn"):
        give_parts[1][2].wait_recv()
    with mark("add"):
        add_middle(1, other_cut, give_in)
    def last_rows():
        with mark("wgn"):
            give_parts[1][3].wait_recv()
        add_end(1, other_cut, give_in)

    def last_peer_rows():
        with mark("wend"):
            for copy in back_other[1]:
                copy.wait_recv()
        add_far(1, 1)

    order = (last_peer_rows, last_rows)

    peer_first = jnp.logical_and(steps[1].upper == 1, jnp.logical_not(early))

    @pl.when(peer_first)
    def _():
        for part in order:
            part()

    @pl.when(jnp.logical_not(peer_first))
    def _():
        for part in order[::-1]:
            part()

    for copy in give_parts[0][2:] + give_parts[1][2:] + back_other[1][1:]:
        copy.wait_send()

    @pl.when(jnp.logical_not(early))
    def _():
        back_other[1][0].wait_send()

    @pl.when(late)
    def _():
        second_leg.wait_send()


def shards(objects, probes, amplitudes, prop_phase, scan_rows, scan_cols, probe_choice):
    side = probes.shape[-1]
    rim = side // 2
    count = lax.axis_size("region")
    band = objects[0]
    band_rows, columns = band.shape[1:]
    tables = dft_blocks(side)
    whole = (2, 2, side, side)
    half = (2, 2, 2, rim, side)
    slot = lambda shape: pltpu.VMEM(shape, jnp.bfloat16)
    tall = pltpu.VMEM((2, band_rows + 2 * rim + SUBLANES, columns), jnp.float32)
    HBM = pl.BlockSpec(memory_space=pltpu.HBM)
    scalars = pltpu.SMEM(scan_rows.shape, jnp.int32)
    laid = lambda rows: pltpu.VMEM((2, side // LANES + 2, rows, LANES), jnp.float32)
    out = pl.pallas_call(
        functools.partial(wave_kernel, side, count),
        out_shape=jax.ShapeDtypeStruct(band.shape, jnp.float32),
        in_specs=[(HBM, HBM)] + [HBM] * 6,
        out_specs=VMEM,
        scratch_shapes=[
            tall,
            pltpu.VMEM(probes.shape, probes.dtype),
            pltpu.VMEM((2,) + amplitudes.shape[:2] + (rim,), jnp.float32),
            pltpu.VMEM((2, side, rim), jnp.float32),
            pltpu.VMEM((2,) + prop_phase.shape, jnp.float32),
            pltpu.VMEM(tables.shape, tables.dtype),
            pltpu.VMEM((2, side, side), jnp.float32),
            slot(whole), slot(whole), slot(half), slot(half),
            pltpu.VMEM(whole, jnp.float32), slot(whole), slot(whole), slot(whole), slot(half),
            slot((2, side // 4, side)), slot((2, rim, columns)), slot((2, rim, columns)),
            laid(side + side // 4), laid(side), laid(side - side // 4),
            (scalars,) * 2, ((scalars,) * 2,) * 2, scalars,
            pltpu.SemaphoreType.DMA((7,)),
            pltpu.SemaphoreType.DMA((16,)),
            pltpu.SemaphoreType.DMA((27,)),
        ],
        compiler_params=pltpu.CompilerParams(
            collective_id=0, has_side_effects=True, vmem_limit_bytes=32 * 1024 * 1024
        ),
    )(*jax.tree.map(
        lambda x: pltpu.with_memory_space_constraint(x, pltpu.HBM),
        ((scan_rows, scan_cols), probe_choice, band, probes, amplitudes, prop_phase, tables),
    ))
    return out[None]


def solution(mesh):
    return jax.shard_map(
        shards,
        mesh=mesh,
        in_specs=(
            P("cuts", None, "region", None),
            P(),
            P("region", None, None),
            P(),
            P("region"),
            P("region"),
            P("region"),
        ),
        out_specs=P("cuts", None, "region", None),
        check_vma=False,
    )
```

```python
import contextlib
import functools
import jax
import jax.numpy as jnp
import numpy as np
from jax import lax
from jax.experimental import pallas as pl
from jax.experimental.pallas import tpu as pltpu
from jax.sharding import PartitionSpec as P

modulus_floor = 0.25
LANES = 128
SUBLANES = 8
VMEM = pl.BlockSpec(memory_space=pltpu.VMEM)


def mark(name):
    return contextlib.nullcontext()


def dft_blocks(side):
    half = side // 2
    indices = np.arange(side)
    angles = (indices[:, None] * indices[None, :] % side) * (2.0 * np.pi / side)
    real = np.cos(angles) / np.sqrt(side)
    imag = np.sin(angles) / np.sqrt(side)
    tables = []
    for odd in range(2):
        cos, sin = real[:half, odd::2], imag[:half, odd::2]
        tables.append(np.block([[cos.T, sin.T], [-sin.T, cos.T]]))
    for odd in range(2):
        cos, sin = real[:half, odd::2], imag[:half, odd::2]
        tables.append(np.block([[cos, -sin], [sin, cos]]))
    return jnp.asarray(np.stack(tables), dtype=jnp.bfloat16)


def split_col(col, cols, side):
    base = jnp.minimum(lax.div(col, LANES), (cols - side) // LANES - 1) * LANES
    return base, col - base


def cut_window(ext, plane, row, col, height, side):
    base, shift = split_col(col, ext.shape[2], side)
    top = lax.div(row, SUBLANES) * SUBLANES
    tall = height + SUBLANES
    block = ext[plane, pl.ds(top, tall), pl.ds(base, side + LANES)]
    block = pltpu.roll(block, lax.rem(tall + top - row, tall), axis=0)[:height]
    back = lax.rem(LANES - shift + LANES, LANES)
    chunks = [
        pltpu.roll(block[:, j : j + LANES], back, axis=1) for j in range(0, side + LANES, LANES)
    ]
    lane = lax.broadcasted_iota(jnp.int32, (height, LANES), 1)
    keep = lane < LANES - shift
    return jnp.concatenate(
        [jnp.where(keep, chunks[j], chunks[j + 1]) for j in range(len(chunks) - 1)], axis=1
    )


def lay_window(padded, plane, row, col, field):
    height, side = field.shape
    rows = lax.rem(row + 8 * SUBLANES * side, SUBLANES)
    base, shift = col
    tall = height + SUBLANES
    field = jnp.concatenate([field, jnp.zeros((SUBLANES, side), field.dtype)], axis=0)
    field = pltpu.roll(field, rows, axis=0)
    ahead = lax.rem(shift, LANES)
    chunks = [pltpu.roll(field[:, j : j + LANES], ahead, axis=1) for j in range(0, side, LANES)]
    lane = lax.broadcasted_iota(jnp.int32, (tall, LANES), 1)
    keep = lane >= shift
    zero = jnp.zeros((tall, LANES), field.dtype)
    parts = [zero] + chunks + [zero]
    for j in range(len(chunks) + 1):
        padded[plane, j + 1, pl.ds(side // 4, tall)] = jnp.where(keep, parts[j + 1], parts[j])


def add_laid(total, padded, plane, row, col, first, height, side):
    base, _ = col
    shift = side // 4 + 8 * SUBLANES * side
    start = (lax.div(first + shift, SUBLANES) - lax.div(row + 8 * SUBLANES * side, SUBLANES)) * SUBLANES
    count = side // LANES + 1
    for j in range(total.shape[2] // LANES):
        block = j - lax.div(base, LANES)
        inside = jnp.logical_and(block >= 0, block < count)
        source = padded[plane, jnp.where(inside, block + 1, 0), pl.ds(start, height)]
        where = (plane, pl.ds(first, height), pl.ds(j * LANES, LANES))
        total[where] = total[where] + source


def dot(left, right):
    return jnp.dot(left, right, preferred_element_type=jnp.float32)


def narrow(left, right, axis):
    return jnp.concatenate([left, right], axis=axis).astype(jnp.bfloat16)


def forward(field, tables):
    half = field[0].shape[0] // 2
    low, high = [part[:half] for part in field], [part[half:] for part in field]
    even = dot(tables[0], narrow(low[0] + high[0], low[1] + high[1], 0))
    odd = dot(tables[1], narrow(low[0] - high[0], low[1] - high[1], 0))
    middle = [
        jnp.concatenate([even[:half], odd[:half]], axis=0),
        jnp.concatenate([even[half:], odd[half:]], axis=0),
    ]
    low, high = [part[:, :half] for part in middle], [part[:, half:] for part in middle]
    even = dot(narrow(low[0] + high[0], low[1] + high[1], 1), tables[2])
    odd = dot(narrow(low[0] - high[0], low[1] - high[1], 1), tables[3])
    return (
        jnp.concatenate([even[:, :half], odd[:, :half]], axis=1),
        jnp.concatenate([even[:, half:], odd[:, half:]], axis=1),
    )


def inverse(field, tables):
    half = field[0].shape[0] // 2
    even = dot(tables[2], narrow(field[0][:half], field[1][:half], 0))
    odd = dot(tables[3], narrow(field[0][half:], field[1][half:], 0))
    total, rest = even + odd, even - odd
    middle = [
        jnp.concatenate([total[:half], rest[:half]], axis=0),
        jnp.concatenate([total[half:], rest[half:]], axis=0),
    ]
    even = dot(narrow(middle[0][:, :half], middle[1][:, :half], 1), tables[0])
    odd = dot(narrow(middle[0][:, half:], middle[1][:, half:], 1), tables[1])
    total, rest = even + odd, even - odd
    return (
        jnp.concatenate([total[:, :half], rest[:, :half]], axis=1),
        jnp.concatenate([total[:, half:], rest[:, half:]], axis=1),
    )


def even_first(rows):
    array = jnp.concatenate(
        [jnp.concatenate([rows(first, k) for k in range(2)], axis=1) for first in range(2)], axis=0
    )
    side = array.shape[1]
    source = lax.broadcasted_iota(jnp.int32, (side, side), 0)
    target = lax.broadcasted_iota(jnp.int32, (side, side), 1)
    wanted = jnp.where(target < side // 2, 2 * target, 2 * target - side + 1)
    pick = jnp.where(source == wanted, 1.0, 0.0).astype(jnp.bfloat16)
    total = None
    for _ in range(3):
        part = array.astype(jnp.bfloat16)
        array = array - part.astype(jnp.float32)
        moved = dot(part, pick)
        total = moved if total is None else total + moved
    return total


def turn(phase):
    x = phase * 0.5
    y = x * x
    sin = np.float32(1.0 / 6227020800.0)
    for factor in (-39916800.0, 362880.0, -5040.0, 120.0, -6.0, 1.0):
        sin = sin * y + np.float32(1.0 / factor)
    sin = sin * x
    cos = np.float32(-1.0 / 87178291200.0)
    for factor in (479001600.0, -3628800.0, 40320.0, -720.0, 24.0, -2.0, 1.0):
        cos = cos * y + np.float32(1.0 / factor)
    return 1.0 - 2.0 * sin * sin, 2.0 * sin * cos


def multiply(left, right):
    return left[0] * right[0] - left[1] * right[1], left[0] * right[1] + left[1] * right[0]


def multiply_conjugate(left, right):
    return left[0] * right[0] + left[1] * right[1], left[0] * right[1] - left[1] * right[0]


def narrowed(field):
    return tuple(part.astype(jnp.bfloat16).astype(jnp.float32) for part in field)


def one_position(psi0, object0, object1, measured, wave, tables):
    psi1 = narrowed(
        inverse(multiply(wave, forward(multiply(psi0, object0), tables)), tables)
    )
    far = forward(multiply(psi1, object1), tables)
    modulus = jnp.sqrt(far[0] * far[0] + far[1] * far[1])
    factor = 1.0 - measured / jnp.maximum(modulus, modulus_floor)
    g1 = narrowed(inverse((far[0] * factor, far[1] * factor), tables))
    d1 = multiply_conjugate(psi1, g1)
    back = forward(multiply_conjugate(object1, g1), tables)
    g0 = narrowed(inverse(multiply_conjugate(wave, back), tables))
    return multiply_conjugate(psi0, g0), d1


def wide(ref, *index):
    return ref[index + (0,)].astype(jnp.float32), ref[index + (1,)].astype(jnp.float32)


def find(rows, upper, rank):
    seen = jnp.int32(0)
    chosen = jnp.int32(0)
    for position in range(rows.shape[0]):
        here = jnp.where(rows[position] < 0, 1, 0) == upper
        chosen = jnp.where(jnp.logical_and(here, seen == rank), position, chosen)
        seen = seen + jnp.where(here, 1, 0)
    return chosen


def corner(info, upper, rank, side, band_rows):
    position = find(info[0], upper, rank)
    least = jnp.where(upper == 1, -(side // 2), band_rows - side + side // 4)
    row = jnp.minimum(jnp.maximum(info[0][position], least), least + side // 4)
    return row, info[1][position]


class Step:
    def __init__(self, index, region, count, side, band_rows):
        self.index = index
        even = 1 - lax.rem(region, 2)
        self.upper = 1 - even if index == 0 else even
        before = lax.rem(region + count - 1, count)
        after = lax.rem(region + 1, count)
        self.peer = jnp.where(self.upper == 1, before, after)
        half = side // 2
        self.near_low = pl.multiple_of(self.upper * half, half)
        self.far_low = pl.multiple_of((1 - self.upper) * half, half)
        self.peer_upper = 1 - self.upper
        self.peer_offset = (2 * self.peer_upper - 1) * band_rows
        self.peer_far_low = self.near_low


def wave_kernel(
    side, count, scans, choice_any, band, probes_any, amps_any, phase_any, tables_any,
    total,
    ext, probes, amps, phase, wave, tables, measured,
    x_send, x_in, far_send, far_in, own, give, keep, give_in, far_back, detour, strip_send, strip_in,
    near_laid, far_laid, end_laid, here, around, choice,
    local_sem, send_sem, recv_sem,
):
    rim = side // 2
    band_rows = band.shape[1]
    c = lax.axis_index("cuts")
    region = lax.axis_index("region")
    other_cut = 1 - c
    steps = [Step(s, region, count, side, band_rows) for s in range(2)]
    cuts = [(p, k * rim) for p in range(2) for k in range(band_rows // rim)]
    loads = [(scans[0], here[0]), (scans[1], here[1])]
    loads += [
        (band.at[p, pl.ds(low, rim)], ext.at[p, pl.ds(rim + low, rim)]) for p, low in cuts
    ]
    early_loads = len(loads)
    loads += [
        (choice_any, choice), (tables_any, tables), (probes_any, probes),
        *((phase_any.at[:, pl.ds(k * rim, rim)], phase.at[k]) for k in range(2)),
        *((amps_any.at[:, :, pl.ds(k * rim, rim)], amps.at[k]) for k in range(2)),
    ]
    loads = [
        pltpu.make_async_copy(source, target, local_sem.at[k % early_loads if k < 2 * early_loads else k - early_loads])
        for k, (source, target) in enumerate(loads)
    ]
    for load in loads[:early_loads]:
        load.start()
    barrier = pltpu.get_barrier_semaphore()
    early = region == 0
    late = region == count - 1
    for peer in ((other_cut, region), (c, steps[0].peer)):
        pl.semaphore_signal(barrier, 1, device_id=peer, device_id_type=pl.DeviceIdType.MESH)

    @pl.when(jnp.logical_not(late))
    def _():
        pl.semaphore_signal(
            barrier, 1, device_id=(c, steps[1].peer), device_id_type=pl.DeviceIdType.MESH
        )

    with mark("bar"):
        pl.semaphore_wait(barrier, jnp.where(early, 2, 3))
    slots = iter(range(32))

    def remote(source, target, peer, send_slot, recv_slot=None):
        slot = next(slots) if recv_slot is None else recv_slot
        return pltpu.make_async_remote_copy(
            src_ref=source, dst_ref=target,
            send_sem=send_sem.at[send_slot], recv_sem=recv_sem.at[slot],
            device_id=peer, device_id_type=pl.DeviceIdType.MESH,
        )

    across = (other_cut, region)
    halves = [(c, step.peer) for step in steps]
    notes = [[remote(here[k], around[s][k], halves[s], 2 * s + k) for k in range(2)] for s in range(2)]
    near = [pl.ds(step.near_low, rim) for step in steps]
    far = [pl.ds(step.far_low, rim) for step in steps]
    x_near = [remote(x_send.at[s, :, near[s]], x_in.at[s, :, near[s]], across, 4 + 3 * s) for s in range(2)]
    x_far = [
        [remote(x_send.at[s, p, far[s]], x_in.at[s, p, far[s]], across, 5 + 3 * s + p) for p in range(2)]
        for s in range(2)
    ]
    halo = [[remote(far_send.at[0, j], far_in.at[0, j], halves[0], 10 + j) for j in range(2)]]
    halo.append([remote(far_send.at[1, j], far_in.at[1, j], halves[1], 12 + j, 10 + j + 2) for j in range(2)])
    strip = [remote(strip_send.at[p], strip_in.at[p], halves[1], 12 + p, 10 + p + 2) for p in range(2)]
    slots = iter(range(14, 32))
    quarter = side // 4
    rows = []
    for step in steps:
        order = [3 - k + step.upper * (2 * k - 3) for k in range(4)]
        rows.append([pl.ds(pl.multiple_of(k * quarter, quarter), quarter) for k in order])
    give_parts = [
        [
            remote(give.at[0, :, part], give_in.at[0, :, part], across, slot)
            for part, slot in ((far[0], 5), (rows[0][2], 4), (rows[0][3], 6))
        ],
        [
            remote(give.at[1, :, part], give_in.at[1, :, part], across, slot)
            for part, slot in zip(rows[1], (7, 8, 9, 14))
        ],
    ]
    back_other = [[remote(give_in.at[0, :, far[0]], far_back.at[0, 1], halves[0], 0)], []]
    for k in range(2):
        start = pl.multiple_of(jnp.where(steps[1].upper == 1, k, 1 - k) * quarter, quarter)
        back_other[1].append(
            remote(
                give_in.at[1, :, rows[1][k]],
                far_back.at[1, 1, :, pl.ds(start, quarter)],
                halves[1],
                1 + k,
            )
        )
    begin = pl.multiple_of(steps[1].upper * quarter, quarter)
    first_leg = remote(give.at[1, :, rows[1][0]], detour, halves[1], 7, 26)
    second_leg = remote(detour, far_back.at[1, 1, :, pl.ds(begin, quarter)], across, 15, 22)
    back_own = [remote(keep.at[s, :, far[s]], far_back.at[s, 0], halves[s], 10 + s) for s in range(2)]
    for load in loads[:2]:
        load.wait()
    for note in notes[0]:
        note.start()

    @pl.when(jnp.logical_not(early))
    def _():
        for note in notes[1]:
            note.start()

    with mark("band"):
        for load in loads[2:early_loads]:
            load.wait()
    for load in loads[early_loads:]:
        load.start()

    ids = lax.broadcasted_iota(jnp.int32, (rim, side), 0)

    def cut_far(s, rank):
        step = steps[s]
        row, col = corner(around[s], step.peer_upper, rank, side, band_rows)
        top = row + step.peer_offset + step.peer_far_low + rim
        return [cut_window(ext, plane, top, col, rim, side) for plane in range(2)]

    def mixed(s, rank, j, plane):
        step = steps[s]
        row, col = corner(here, step.upper, rank, side, band_rows)
        held = cut_window(ext, plane, row + rim + step.far_low, col, rim, side)
        rows = ids + (row + step.far_low)
        outside = jnp.logical_or(rows < 0, rows >= band_rows)
        if s == 1:
            outside = jnp.logical_and(outside, jnp.logical_not(early))
        return jnp.where(outside, far_in[s, j, plane].astype(jnp.float32), held)

    def near_half(s, rank, plane):
        step = steps[s]
        row, col = corner(here, step.upper, rank, side, band_rows)
        return cut_window(ext, plane, row + rim + step.near_low, col, rim, side)

    def cut_near(s):
        for plane in range(2):
            x_send[s, plane, near[s]] = near_half(s, other_cut, plane).astype(jnp.bfloat16)

    def cut_halo(s, j):
        for plane, part in enumerate(cut_far(s, (other_cut, c)[j])):
            far_send[s, j, plane] = part.astype(jnp.bfloat16)

    def send_far(s, plane):
        with mark("far"):
            x_send[s, plane, far[s]] = mixed(s, other_cut, 0, plane).astype(jnp.bfloat16)
            x_far[s][plane].start()

    def send_strip_far(plane):
        with mark("wstrip"):
            strip[plane].wait_recv()
        rows = pl.ds(pl.multiple_of((1 - steps[1].upper) * (rim + band_rows), rim), rim)
        ext[plane, rows] = strip_in[plane].astype(jnp.float32)
        send_far(1, plane)

    def gather_own(s):
        for plane in range(2):
            own[s, plane, near[s]] = near_half(s, c, plane)
            own[s, plane, far[s]] = mixed(s, c, 1, plane)

    def send_strip(plane):
        rows = pl.ds(pl.multiple_of(rim + steps[1].peer_upper * (band_rows - rim), rim), rim)
        strip_send[plane] = ext[plane, rows].astype(jnp.bfloat16)
        strip[plane].start()

    def add_near(s, rank, source):
        step = steps[s]
        row, col = corner(here, step.upper, rank, side, band_rows)
        low = pl.multiple_of(step.upper * quarter, quarter)
        first = pl.multiple_of((1 - step.upper) * quarter, quarter)
        place = split_col(col, total.shape[2], side)
        for plane in range(2):
            part = source[s, plane, pl.ds(low, side - quarter)].astype(jnp.float32)
            lay_window(near_laid, plane, row + low, place, part)
            add_laid(total, near_laid, plane, row + low, place, first, side - quarter, side)

    def add_far(s, j, planes=(0, 1)):
        step = steps[s]
        row, col = corner(around[s], step.peer_upper, (c, other_cut)[j], side, band_rows)
        top = row + step.peer_offset + step.peer_far_low
        first = pl.multiple_of(step.peer_upper * rim, rim)
        place = split_col(col, total.shape[2], side)
        for plane in planes:
            part = far_back[s, j, plane].astype(jnp.float32)
            lay_window(far_laid, plane, top, place, part)
            add_laid(total, far_laid, plane, top, place, first, rim, side)

    def add_middle(s, rank, source):
        step = steps[s]
        row, col = corner(here, step.upper, rank, side, band_rows)
        first = pl.multiple_of((1 - step.upper) * rim, rim)
        place = split_col(col, total.shape[2], side)
        for plane in range(2):
            part = source[s, plane, pl.ds(quarter, rim)].astype(jnp.float32)
            lay_window(far_laid, plane, row + quarter, place, part)
            add_laid(total, far_laid, plane, row + quarter, place, first, rim, side)

    def add_end(s, rank, source, planes=(0, 1)):
        step = steps[s]
        row, col = corner(here, step.upper, rank, side, band_rows)
        low = pl.multiple_of(step.upper * 3 * quarter, quarter)
        place = split_col(col, total.shape[2], side)
        for plane in planes:
            part = source[s, plane, pl.ds(low, quarter)].astype(jnp.float32)
            lay_window(end_laid, plane, row + low, place, part)
            add_laid(total, end_laid, plane, row + low, place, quarter, rim, side)

    def position_of(s):
        position = find(here[0], steps[s].upper, c)
        psi0 = wide(probes, choice[position])
        with mark("wx"):
            for copy in [x_near[s]] + x_far[s]:
                copy.wait_recv()
        mine = tuple(own[s, plane] for plane in range(2))
        theirs = tuple(x_in[s, plane].astype(jnp.float32) for plane in range(2))
        object0 = tuple(jnp.where(first, x, y) for x, y in zip(mine, theirs))
        object1 = tuple(jnp.where(first, y, x) for x, y in zip(mine, theirs))
        with mark("pos"):
            d0, d1 = one_position(psi0, object0, object1, measured[s], (wave[0], wave[1]), tables)
        for plane in range(2):
            give[s, plane] = jnp.where(first, d1[plane], d0[plane]).astype(jnp.bfloat16)
            keep[s, plane] = jnp.where(first, d0[plane], d1[plane]).astype(jnp.bfloat16)

    first = c == 0
    with mark("near0"):
        cut_near(0)
        x_near[0].start()

    with mark("wnote"):
        for note in notes[0]:
            note.wait_recv()
    cut_halo(0, 0)
    halo[0][0].start()

    @pl.when(late)
    def _():
        send_strip(0)

    @pl.when(jnp.logical_not(jnp.logical_or(early, late)))
    def _():
        with mark("wnote"):
            for note in notes[1]:
                note.wait_recv()
        cut_halo(1, 0)
        halo[1][0].start()

    with mark("wh0"):
        halo[0][0].wait_recv()
    for plane in range(2):
        send_far(0, plane)
    cut_halo(0, 1)
    halo[0][1].start()
    with mark("prep"):
        cut_near(1)
        for load in loads[early_loads:]:
            load.wait()
        wave[0], wave[1] = turn(
            even_first(lambda first, k: phase[k, pl.ds(first, rim, stride=2), :])
        )

        @pl.when(late)
        def _():
            send_strip(1)

        halo[0][1].wait_recv()
        gather_own(0)
        for s in range(2):
            position = find(here[0], steps[s].upper, c)
            measured[s] = even_first(
                lambda first, k: amps[k, position, pl.ds(first, rim, stride=2), :]
            )
        near_laid[...] = jnp.zeros_like(near_laid)
        far_laid[...] = jnp.zeros_like(far_laid)
        end_laid[...] = jnp.zeros_like(end_laid)
        total[...] = jnp.zeros_like(total)

    @pl.when(early)
    def _():
        with mark("wnote"):
            for note in notes[1]:
                note.wait_recv()
        cut_halo(1, 0)
        halo[1][0].start()
        for note in notes[1]:
            note.start()

    with mark("wsA"):
        x_near[0].wait_send()
        x_far[0][0].wait_send()
    x_near[1].start()

    @pl.when(jnp.logical_not(early))
    def _():
        with mark("wh1"):
            halo[1][0].wait_recv()
        for plane in range(2):
            send_far(1, plane)

    @pl.when(jnp.logical_not(late))
    def _():
        cut_halo(1, 1)
        halo[1][1].start()

    for copy in notes[0] + notes[1] + halo[0]:
        copy.wait_send()
    position_of(0)
    back_own[0].start()

    @pl.when(early)
    def _():
        for plane in range(2):
            send_strip_far(plane)

    @pl.when(early)
    def _():
        gather_own(1)

    @pl.when(jnp.logical_not(early))
    def _():
        give_parts[0][1].start()

    with mark("wsB"):
        for copy in [x_far[0][1], x_near[1]] + x_far[1]:
            copy.wait_send()

    @pl.when(jnp.logical_not(late))
    def _():
        give_parts[0][0].start()

    @pl.when(early)
    def _():
        for copy in give_parts[0][1:]:
            copy.start()

    @pl.when(jnp.logical_not(early))
    def _():
        with mark("wh1"):
            halo[1][1].wait_recv()
        gather_own(1)

    with mark("add"):
        add_near(0, c, keep)
    position_of(1)
    @pl.when(region < 2)
    def _():
        first_leg.start()

    @pl.when(region >= 2)
    def _():
        give_parts[1][0].start()

    give_parts[1][1].start()

    @pl.when(early)
    def _():
        for copy in give_parts[1][2:]:
            copy.start()

    @pl.when(region == 1)
    def _():
        for copy in give_parts[0][2:] + give_parts[1][2:]:
            copy.start()

    back_own[1].start()
    def pass_first():
        with mark("wgf0"):
            give_parts[0][0].wait_recv()
        back_other[0][0].start()

    @pl.when(jnp.logical_not(late))
    def _():
        pass_first()

    with mark("add"):
        back_own[0].wait_recv()
        add_far(0, 0)
        add_near(1, c, keep)

    @pl.when(late)
    def _():
        for note in notes[1]:
            note.wait_recv()

    with mark("wsC"):
        for copy in give_parts[0][1:2] + give_parts[1][:2]:
            copy.wait_send()

    @pl.when(late)
    def _():
        give_parts[0][0].start()


    @pl.when(region > 1)
    def _():
        for copy in give_parts[0][2:] + give_parts[1][2:]:
            copy.start()

    @pl.when(late)
    def _():
        for copy in strip:
            copy.wait_send()

    @pl.when(jnp.logical_not(late))
    def _():
        for copy in halo[1]:
            copy.wait_send()

    back_own[0].wait_send()
    with mark("wgf1"):

        @pl.when(region >= 2)
        def _():
            give_parts[1][0].wait_recv()
            back_other[1][0].start()

        give_parts[1][1].wait_recv()
        back_other[1][1].start()

    passes_on = jnp.logical_or(late, region == 2)

    @pl.when(region == 2)
    def _():
        first_leg.wait_recv()
        second_leg.start()

    @pl.when(late)
    def _():
        pass_first()

    with mark("add"):
        for copy in back_other[0]:
            copy.wait_recv()
        add_far(0, 1)
    with mark("add"):
        back_own[1].wait_recv()
        add_far(1, 0)
    for copy in [back_own[1]] + back_other[0]:
        copy.wait_send()
    with mark("wgn0"):
        for copy in give_parts[0][1:]:
            copy.wait_recv()
    with mark("add"):
        add_near(0, other_cut, give_in)
    @pl.when(late)
    def _():
        first_leg.wait_recv()
        second_leg.start()

    with mark("wgn"):
        give_parts[1][2].wait_recv()
    with mark("add"):
        add_middle(1, other_cut, give_in)
    def last_rows():
        with mark("wgn"):
            give_parts[1][3].wait_recv()
        add_end(1, other_cut, give_in)

    def last_peer_rows():
        with mark("wend"):
            for copy in back_other[1]:
                copy.wait_recv()
        add_far(1, 1)

    order = (last_peer_rows, last_rows)

    peer_first = jnp.logical_and(steps[1].upper == 1, jnp.logical_not(early))

    @pl.when(peer_first)
    def _():
        for part in order:
            part()

    @pl.when(jnp.logical_not(peer_first))
    def _():
        for part in order[::-1]:
            part()

    for copy in give_parts[0][:1] + give_parts[0][2:] + give_parts[1][2:] + back_other[1][1:]:
        copy.wait_send()

    @pl.when(region >= 2)
    def _():
        back_other[1][0].wait_send()

    @pl.when(passes_on)
    def _():
        second_leg.wait_send()


def shards(objects, probes, amplitudes, prop_phase, scan_rows, scan_cols, probe_choice):
    side = probes.shape[-1]
    rim = side // 2
    count = lax.axis_size("region")
    band = objects[0]
    band_rows, columns = band.shape[1:]
    tables = dft_blocks(side)
    whole = (2, 2, side, side)
    half = (2, 2, 2, rim, side)
    slot = lambda shape: pltpu.VMEM(shape, jnp.bfloat16)
    tall = pltpu.VMEM((2, band_rows + 2 * rim + SUBLANES, columns), jnp.float32)
    HBM = pl.BlockSpec(memory_space=pltpu.HBM)
    scalars = pltpu.SMEM(scan_rows.shape, jnp.int32)
    laid = lambda rows: pltpu.VMEM((2, side // LANES + 2, rows, LANES), jnp.float32)
    out = pl.pallas_call(
        functools.partial(wave_kernel, side, count),
        out_shape=jax.ShapeDtypeStruct(band.shape, jnp.float32),
        in_specs=[(HBM, HBM)] + [HBM] * 6,
        out_specs=VMEM,
        scratch_shapes=[
            tall,
            pltpu.VMEM(probes.shape, probes.dtype),
            pltpu.VMEM((2,) + amplitudes.shape[:2] + (rim,), jnp.float32),
            pltpu.VMEM((2, side, rim), jnp.float32),
            pltpu.VMEM((2,) + prop_phase.shape, jnp.float32),
            pltpu.VMEM(tables.shape, tables.dtype),
            pltpu.VMEM((2, side, side), jnp.float32),
            slot(whole), slot(whole), slot(half), slot(half),
            pltpu.VMEM(whole, jnp.float32), slot(whole), slot(whole), slot(whole), slot(half),
            slot((2, side // 4, side)), slot((2, rim, columns)), slot((2, rim, columns)),
            laid(side + side // 4), laid(side), laid(side - side // 4),
            (scalars,) * 2, ((scalars,) * 2,) * 2, scalars,
            pltpu.SemaphoreType.DMA((7,)),
            pltpu.SemaphoreType.DMA((16,)),
            pltpu.SemaphoreType.DMA((27,)),
        ],
        compiler_params=pltpu.CompilerParams(
            collective_id=0, has_side_effects=True, vmem_limit_bytes=32 * 1024 * 1024
        ),
    )(*jax.tree.map(
        lambda x: pltpu.with_memory_space_constraint(x, pltpu.HBM),
        ((scan_rows, scan_cols), probe_choice, band, probes, amplitudes, prop_phase, tables),
    ))
    return out[None]


def solution(mesh):
    return jax.shard_map(
        shards,
        mesh=mesh,
        in_specs=(
            P("cuts", None, "region", None),
            P(),
            P("region", None, None),
            P(),
            P("region"),
            P("region"),
            P("region"),
        ),
        out_specs=P("cuts", None, "region", None),
        check_vma=False,
    )
```

```python
import contextlib
import functools
import jax
import jax.numpy as jnp
import numpy as np
from jax import lax
from jax.experimental import pallas as pl
from jax.experimental.pallas import tpu as pltpu
from jax.sharding import PartitionSpec as P

modulus_floor = 0.25
LANES = 128
SUBLANES = 8
VMEM = pl.BlockSpec(memory_space=pltpu.VMEM)


def mark(name):
    return contextlib.nullcontext()


def dft_blocks(side):
    half = side // 2
    indices = np.arange(side)
    angles = (indices[:, None] * indices[None, :] % side) * (2.0 * np.pi / side)
    real = np.cos(angles) / np.sqrt(side)
    imag = np.sin(angles) / np.sqrt(side)
    tables = []
    for odd in range(2):
        cos, sin = real[:half, odd::2], imag[:half, odd::2]
        tables.append(np.block([[cos.T, sin.T], [-sin.T, cos.T]]))
    for odd in range(2):
        cos, sin = real[:half, odd::2], imag[:half, odd::2]
        tables.append(np.block([[cos, -sin], [sin, cos]]))
    return jnp.asarray(np.stack(tables), dtype=jnp.bfloat16)


def split_col(col, cols, side):
    base = jnp.minimum(lax.div(col, LANES), (cols - side) // LANES - 1) * LANES
    return base, col - base


def cut_window(ext, plane, row, col, height, side):
    base, shift = split_col(col, ext.shape[2], side)
    top = lax.div(row, SUBLANES) * SUBLANES
    tall = height + SUBLANES
    block = ext[plane, pl.ds(top, tall), pl.ds(base, side + LANES)]
    block = pltpu.roll(block, lax.rem(tall + top - row, tall), axis=0)[:height]
    back = lax.rem(LANES - shift + LANES, LANES)
    chunks = [
        pltpu.roll(block[:, j : j + LANES], back, axis=1) for j in range(0, side + LANES, LANES)
    ]
    lane = lax.broadcasted_iota(jnp.int32, (height, LANES), 1)
    keep = lane < LANES - shift
    return jnp.concatenate(
        [jnp.where(keep, chunks[j], chunks[j + 1]) for j in range(len(chunks) - 1)], axis=1
    )


def lay_window(padded, plane, row, col, field):
    height, side = field.shape
    rows = lax.rem(row + 8 * SUBLANES * side, SUBLANES)
    base, shift = col
    tall = height + SUBLANES
    field = jnp.concatenate([field, jnp.zeros((SUBLANES, side), field.dtype)], axis=0)
    field = pltpu.roll(field, rows, axis=0)
    ahead = lax.rem(shift, LANES)
    chunks = [pltpu.roll(field[:, j : j + LANES], ahead, axis=1) for j in range(0, side, LANES)]
    lane = lax.broadcasted_iota(jnp.int32, (tall, LANES), 1)
    keep = lane >= shift
    zero = jnp.zeros((tall, LANES), field.dtype)
    parts = [zero] + chunks + [zero]
    for j in range(len(chunks) + 1):
        padded[plane, j + 1, pl.ds(side // 4, tall)] = jnp.where(keep, parts[j + 1], parts[j])


def add_laid(total, padded, plane, row, col, first, height, side):
    base, _ = col
    shift = side // 4 + 8 * SUBLANES * side
    start = (lax.div(first + shift, SUBLANES) - lax.div(row + 8 * SUBLANES * side, SUBLANES)) * SUBLANES
    count = side // LANES + 1
    for j in range(total.shape[2] // LANES):
        block = j - lax.div(base, LANES)
        inside = jnp.logical_and(block >= 0, block < count)
        source = padded[plane, jnp.where(inside, block + 1, 0), pl.ds(start, height)]
        where = (plane, pl.ds(first, height), pl.ds(j * LANES, LANES))
        total[where] = total[where] + source


def dot(left, right):
    return jnp.dot(left, right, preferred_element_type=jnp.float32)


def narrow(left, right, axis):
    return jnp.concatenate([left, right], axis=axis).astype(jnp.bfloat16)


def forward(field, tables):
    half = field[0].shape[0] // 2
    low, high = [part[:half] for part in field], [part[half:] for part in field]
    even = dot(tables[0], narrow(low[0] + high[0], low[1] + high[1], 0))
    odd = dot(tables[1], narrow(low[0] - high[0], low[1] - high[1], 0))
    middle = [
        jnp.concatenate([even[:half], odd[:half]], axis=0),
        jnp.concatenate([even[half:], odd[half:]], axis=0),
    ]
    low, high = [part[:, :half] for part in middle], [part[:, half:] for part in middle]
    even = dot(narrow(low[0] + high[0], low[1] + high[1], 1), tables[2])
    odd = dot(narrow(low[0] - high[0], low[1] - high[1], 1), tables[3])
    return (
        jnp.concatenate([even[:, :half], odd[:, :half]], axis=1),
        jnp.concatenate([even[:, half:], odd[:, half:]], axis=1),
    )


def inverse(field, tables):
    half = field[0].shape[0] // 2
    even = dot(tables[2], narrow(field[0][:half], field[1][:half], 0))
    odd = dot(tables[3], narrow(field[0][half:], field[1][half:], 0))
    total, rest = even + odd, even - odd
    middle = [
        jnp.concatenate([total[:half], rest[:half]], axis=0),
        jnp.concatenate([total[half:], rest[half:]], axis=0),
    ]
    even = dot(narrow(middle[0][:, :half], middle[1][:, :half], 1), tables[0])
    odd = dot(narrow(middle[0][:, half:], middle[1][:, half:], 1), tables[1])
    total, rest = even + odd, even - odd
    return (
        jnp.concatenate([total[:, :half], rest[:, :half]], axis=1),
        jnp.concatenate([total[:, half:], rest[:, half:]], axis=1),
    )


def even_first(rows):
    array = jnp.concatenate(
        [jnp.concatenate([rows(first, k) for k in range(2)], axis=1) for first in range(2)], axis=0
    )
    side = array.shape[1]
    source = lax.broadcasted_iota(jnp.int32, (side, side), 0)
    target = lax.broadcasted_iota(jnp.int32, (side, side), 1)
    wanted = jnp.where(target < side // 2, 2 * target, 2 * target - side + 1)
    pick = jnp.where(source == wanted, 1.0, 0.0).astype(jnp.bfloat16)
    total = None
    for _ in range(3):
        part = array.astype(jnp.bfloat16)
        array = array - part.astype(jnp.float32)
        moved = dot(part, pick)
        total = moved if total is None else total + moved
    return total


def turn(phase):
    x = phase * 0.5
    y = x * x
    sin = np.float32(1.0 / 6227020800.0)
    for factor in (-39916800.0, 362880.0, -5040.0, 120.0, -6.0, 1.0):
        sin = sin * y + np.float32(1.0 / factor)
    sin = sin * x
    cos = np.float32(-1.0 / 87178291200.0)
    for factor in (479001600.0, -3628800.0, 40320.0, -720.0, 24.0, -2.0, 1.0):
        cos = cos * y + np.float32(1.0 / factor)
    return 1.0 - 2.0 * sin * sin, 2.0 * sin * cos


def multiply(left, right):
    return left[0] * right[0] - left[1] * right[1], left[0] * right[1] + left[1] * right[0]


def multiply_conjugate(left, right):
    return left[0] * right[0] + left[1] * right[1], left[0] * right[1] - left[1] * right[0]


def narrowed(field):
    return tuple(part.astype(jnp.bfloat16).astype(jnp.float32) for part in field)


def one_position(psi0, object0, object1, measured, wave, tables):
    psi1 = narrowed(
        inverse(multiply(wave, forward(multiply(psi0, object0), tables)), tables)
    )
    far = forward(multiply(psi1, object1), tables)
    modulus = jnp.sqrt(far[0] * far[0] + far[1] * far[1])
    factor = 1.0 - measured / jnp.maximum(modulus, modulus_floor)
    g1 = narrowed(inverse((far[0] * factor, far[1] * factor), tables))
    d1 = multiply_conjugate(psi1, g1)
    back = forward(multiply_conjugate(object1, g1), tables)
    g0 = narrowed(inverse(multiply_conjugate(wave, back), tables))
    return multiply_conjugate(psi0, g0), d1


def wide(ref, *index):
    return ref[index + (0,)].astype(jnp.float32), ref[index + (1,)].astype(jnp.float32)


def find(rows, upper, rank):
    seen = jnp.int32(0)
    chosen = jnp.int32(0)
    for position in range(rows.shape[0]):
        here = jnp.where(rows[position] < 0, 1, 0) == upper
        chosen = jnp.where(jnp.logical_and(here, seen == rank), position, chosen)
        seen = seen + jnp.where(here, 1, 0)
    return chosen


def corner(info, upper, rank, side, band_rows):
    position = find(info[0], upper, rank)
    least = jnp.where(upper == 1, -(side // 2), band_rows - side + side // 4)
    row = jnp.minimum(jnp.maximum(info[0][position], least), least + side // 4)
    return row, info[1][position]


class Step:
    def __init__(self, index, region, count, side, band_rows):
        self.index = index
        even = 1 - lax.rem(region, 2)
        self.upper = 1 - even if index == 0 else even
        before = lax.rem(region + count - 1, count)
        after = lax.rem(region + 1, count)
        self.peer = jnp.where(self.upper == 1, before, after)
        half = side // 2
        self.near_low = pl.multiple_of(self.upper * half, half)
        self.far_low = pl.multiple_of((1 - self.upper) * half, half)
        self.peer_upper = 1 - self.upper
        self.peer_offset = (2 * self.peer_upper - 1) * band_rows
        self.peer_far_low = self.near_low


def wave_kernel(
    side, count, scans, choice_any, band, probes_any, amps_any, phase_any, tables_any,
    total,
    ext, probes, amps, phase, wave, tables, measured,
    x_send, x_in, far_send, far_in, own, give, keep, give_in, far_back, detour, strip_send, strip_in,
    near_laid, far_laid, end_laid, here, around, choice,
    local_sem, send_sem, recv_sem,
):
    rim = side // 2
    band_rows = band.shape[1]
    c = lax.axis_index("cuts")
    region = lax.axis_index("region")
    other_cut = 1 - c
    steps = [Step(s, region, count, side, band_rows) for s in range(2)]
    cuts = [(p, k * rim) for p in range(2) for k in range(band_rows // rim)]
    loads = [(scans[0], here[0]), (scans[1], here[1])]
    loads += [
        (band.at[p, pl.ds(low, rim)], ext.at[p, pl.ds(rim + low, rim)]) for p, low in cuts
    ]
    early_loads = len(loads)
    loads += [
        (choice_any, choice), (tables_any, tables), (probes_any, probes),
        *((phase_any.at[:, pl.ds(k * rim, rim)], phase.at[k]) for k in range(2)),
        *((amps_any.at[:, :, pl.ds(k * rim, rim)], amps.at[k]) for k in range(2)),
    ]
    loads = [
        pltpu.make_async_copy(source, target, local_sem.at[k % early_loads if k < 2 * early_loads else k - early_loads])
        for k, (source, target) in enumerate(loads)
    ]
    for load in loads[:early_loads]:
        load.start()
    barrier = pltpu.get_barrier_semaphore()
    early = region == 0
    late = region == count - 1
    for peer in ((other_cut, region), (c, steps[0].peer)):
        pl.semaphore_signal(barrier, 1, device_id=peer, device_id_type=pl.DeviceIdType.MESH)

    @pl.when(jnp.logical_not(late))
    def _():
        pl.semaphore_signal(
            barrier, 1, device_id=(c, steps[1].peer), device_id_type=pl.DeviceIdType.MESH
        )

    with mark("bar"):
        pl.semaphore_wait(barrier, jnp.where(early, 2, 3))
    slots = iter(range(32))

    def remote(source, target, peer, send_slot, recv_slot=None):
        slot = next(slots) if recv_slot is None else recv_slot
        return pltpu.make_async_remote_copy(
            src_ref=source, dst_ref=target,
            send_sem=send_sem.at[send_slot], recv_sem=recv_sem.at[slot],
            device_id=peer, device_id_type=pl.DeviceIdType.MESH,
        )

    across = (other_cut, region)
    halves = [(c, step.peer) for step in steps]
    notes = [[remote(here[k], around[s][k], halves[s], 2 * s + k) for k in range(2)] for s in range(2)]
    near = [pl.ds(step.near_low, rim) for step in steps]
    far = [pl.ds(step.far_low, rim) for step in steps]
    x_near = [remote(x_send.at[s, :, near[s]], x_in.at[s, :, near[s]], across, 4 + 3 * s) for s in range(2)]
    x_far = [
        [remote(x_send.at[s, p, far[s]], x_in.at[s, p, far[s]], across, 5 + 3 * s + p) for p in range(2)]
        for s in range(2)
    ]
    halo = [[remote(far_send.at[0, j], far_in.at[0, j], halves[0], 10 + j) for j in range(2)]]
    halo.append([remote(far_send.at[1, j], far_in.at[1, j], halves[1], 12 + j, 10 + j + 2) for j in range(2)])
    strip = [remote(strip_send.at[p], strip_in.at[p], halves[1], 12 + p, 10 + p + 2) for p in range(2)]
    slots = iter(range(14, 32))
    quarter = side // 4
    rows = []
    for step in steps:
        order = [3 - k + step.upper * (2 * k - 3) for k in range(4)]
        rows.append([pl.ds(pl.multiple_of(k * quarter, quarter), quarter) for k in order])
    give_parts = [
        [
            remote(give.at[0, :, part], give_in.at[0, :, part], across, slot)
            for part, slot in ((far[0], 5), (rows[0][2], 4), (rows[0][3], 6))
        ],
        [
            remote(give.at[1, :, part], give_in.at[1, :, part], across, slot)
            for part, slot in zip(rows[1], (7, 8, 9, 14))
        ],
    ]
    back_other = [[remote(give_in.at[0, :, far[0]], far_back.at[0, 1], halves[0], 0)], []]
    for k in range(2):
        start = pl.multiple_of(jnp.where(steps[1].upper == 1, k, 1 - k) * quarter, quarter)
        back_other[1].append(
            remote(
                give_in.at[1, :, rows[1][k]],
                far_back.at[1, 1, :, pl.ds(start, quarter)],
                halves[1],
                1 + k,
            )
        )
    begin = pl.multiple_of(steps[1].upper * quarter, quarter)
    first_leg = remote(give.at[1, :, rows[1][0]], detour, halves[1], 7, 26)
    second_leg = remote(detour, far_back.at[1, 1, :, pl.ds(begin, quarter)], across, 15, 22)
    back_own = [remote(keep.at[s, :, far[s]], far_back.at[s, 0], halves[s], 10 + s) for s in range(2)]
    for load in loads[:2]:
        load.wait()
    for note in notes[0]:
        note.start()

    @pl.when(jnp.logical_not(early))
    def _():
        for note in notes[1]:
            note.start()

    with mark("band"):
        for load in loads[2:early_loads]:
            load.wait()
    for load in loads[early_loads:]:
        load.start()

    ids = lax.broadcasted_iota(jnp.int32, (rim, side), 0)

    def cut_far(s, rank):
        step = steps[s]
        row, col = corner(around[s], step.peer_upper, rank, side, band_rows)
        top = row + step.peer_offset + step.peer_far_low + rim
        return [cut_window(ext, plane, top, col, rim, side) for plane in range(2)]

    def mixed(s, rank, j, plane):
        step = steps[s]
        row, col = corner(here, step.upper, rank, side, band_rows)
        held = cut_window(ext, plane, row + rim + step.far_low, col, rim, side)
        rows = ids + (row + step.far_low)
        outside = jnp.logical_or(rows < 0, rows >= band_rows)
        if s == 1:
            outside = jnp.logical_and(outside, jnp.logical_not(early))
        return jnp.where(outside, far_in[s, j, plane].astype(jnp.float32), held)

    def near_half(s, rank, plane):
        step = steps[s]
        row, col = corner(here, step.upper, rank, side, band_rows)
        return cut_window(ext, plane, row + rim + step.near_low, col, rim, side)

    def cut_near(s):
        for plane in range(2):
            x_send[s, plane, near[s]] = near_half(s, other_cut, plane).astype(jnp.bfloat16)

    def cut_halo(s, j):
        for plane, part in enumerate(cut_far(s, (other_cut, c)[j])):
            far_send[s, j, plane] = part.astype(jnp.bfloat16)

    def send_far(s, plane):
        with mark("far"):
            x_send[s, plane, far[s]] = mixed(s, other_cut, 0, plane).astype(jnp.bfloat16)
            x_far[s][plane].start()

    def send_strip_far(plane):
        with mark("wstrip"):
            strip[plane].wait_recv()
        rows = pl.ds(pl.multiple_of((1 - steps[1].upper) * (rim + band_rows), rim), rim)
        ext[plane, rows] = strip_in[plane].astype(jnp.float32)
        send_far(1, plane)

    def gather_own(s):
        for plane in range(2):
            own[s, plane, near[s]] = near_half(s, c, plane)
            own[s, plane, far[s]] = mixed(s, c, 1, plane)

    def send_strip(plane):
        rows = pl.ds(pl.multiple_of(rim + steps[1].peer_upper * (band_rows - rim), rim), rim)
        strip_send[plane] = ext[plane, rows].astype(jnp.bfloat16)
        strip[plane].start()

    def add_near(s, rank, source):
        step = steps[s]
        row, col = corner(here, step.upper, rank, side, band_rows)
        low = pl.multiple_of(step.upper * quarter, quarter)
        first = pl.multiple_of((1 - step.upper) * quarter, quarter)
        place = split_col(col, total.shape[2], side)
        for plane in range(2):
            part = source[s, plane, pl.ds(low, side - quarter)].astype(jnp.float32)
            lay_window(near_laid, plane, row + low, place, part)
            add_laid(total, near_laid, plane, row + low, place, first, side - quarter, side)

    def add_far(s, j, planes=(0, 1)):
        step = steps[s]
        row, col = corner(around[s], step.peer_upper, (c, other_cut)[j], side, band_rows)
        top = row + step.peer_offset + step.peer_far_low
        first = pl.multiple_of(step.peer_upper * rim, rim)
        place = split_col(col, total.shape[2], side)
        for plane in planes:
            part = far_back[s, j, plane].astype(jnp.float32)
            lay_window(far_laid, plane, top, place, part)
            add_laid(total, far_laid, plane, top, place, first, rim, side)

    def add_middle(s, rank, source):
        step = steps[s]
        row, col = corner(here, step.upper, rank, side, band_rows)
        first = pl.multiple_of((1 - step.upper) * rim, rim)
        place = split_col(col, total.shape[2], side)
        for plane in range(2):
            part = source[s, plane, pl.ds(quarter, rim)].astype(jnp.float32)
            lay_window(far_laid, plane, row + quarter, place, part)
            add_laid(total, far_laid, plane, row + quarter, place, first, rim, side)

    def add_end(s, rank, source, planes=(0, 1)):
        step = steps[s]
        row, col = corner(here, step.upper, rank, side, band_rows)
        low = pl.multiple_of(step.upper * 3 * quarter, quarter)
        place = split_col(col, total.shape[2], side)
        for plane in planes:
            part = source[s, plane, pl.ds(low, quarter)].astype(jnp.float32)
            lay_window(end_laid, plane, row + low, place, part)
            add_laid(total, end_laid, plane, row + low, place, quarter, rim, side)

    def position_of(s):
        position = find(here[0], steps[s].upper, c)
        psi0 = wide(probes, choice[position])
        with mark("wx"):
            for copy in [x_near[s]] + x_far[s]:
                copy.wait_recv()
        mine = tuple(own[s, plane] for plane in range(2))
        theirs = tuple(x_in[s, plane].astype(jnp.float32) for plane in range(2))
        object0 = tuple(jnp.where(first, x, y) for x, y in zip(mine, theirs))
        object1 = tuple(jnp.where(first, y, x) for x, y in zip(mine, theirs))
        with mark("pos"):
            d0, d1 = one_position(psi0, object0, object1, measured[s], (wave[0], wave[1]), tables)
        for plane in range(2):
            give[s, plane] = jnp.where(first, d1[plane], d0[plane]).astype(jnp.bfloat16)
            keep[s, plane] = jnp.where(first, d0[plane], d1[plane]).astype(jnp.bfloat16)

    first = c == 0
    with mark("near0"):
        cut_near(0)
        x_near[0].start()

    with mark("wnote"):
        for note in notes[0]:
            note.wait_recv()
    cut_halo(0, 0)
    halo[0][0].start()

    @pl.when(late)
    def _():
        send_strip(0)

    @pl.when(jnp.logical_not(jnp.logical_or(early, late)))
    def _():
        with mark("wnote"):
            for note in notes[1]:
                note.wait_recv()
        cut_halo(1, 0)
        halo[1][0].start()

    with mark("wh0"):
        halo[0][0].wait_recv()
    for plane in range(2):
        send_far(0, plane)
    cut_halo(0, 1)
    halo[0][1].start()
    with mark("prep"):
        cut_near(1)
        for load in loads[early_loads:]:
            load.wait()
        wave[0], wave[1] = turn(
            even_first(lambda first, k: phase[k, pl.ds(first, rim, stride=2), :])
        )

        @pl.when(late)
        def _():
            send_strip(1)

        halo[0][1].wait_recv()
        gather_own(0)
        for s in range(2):
            position = find(here[0], steps[s].upper, c)
            measured[s] = even_first(
                lambda first, k: amps[k, position, pl.ds(first, rim, stride=2), :]
            )
        near_laid[...] = jnp.zeros_like(near_laid)
        far_laid[...] = jnp.zeros_like(far_laid)
        end_laid[...] = jnp.zeros_like(end_laid)
        total[...] = jnp.zeros_like(total)

    @pl.when(early)
    def _():
        with mark("wnote"):
            for note in notes[1]:
                note.wait_recv()
        cut_halo(1, 0)
        halo[1][0].start()
        for note in notes[1]:
            note.start()

    with mark("wsA"):
        x_near[0].wait_send()
        x_far[0][0].wait_send()
    x_near[1].start()

    @pl.when(jnp.logical_not(early))
    def _():
        with mark("wh1"):
            halo[1][0].wait_recv()
        for plane in range(2):
            send_far(1, plane)

    @pl.when(jnp.logical_not(late))
    def _():
        cut_halo(1, 1)
        halo[1][1].start()

    for copy in notes[0] + notes[1] + halo[0]:
        copy.wait_send()
    position_of(0)
    back_own[0].start()

    @pl.when(early)
    def _():
        for plane in range(2):
            send_strip_far(plane)

    @pl.when(early)
    def _():
        gather_own(1)

    @pl.when(jnp.logical_not(early))
    def _():
        give_parts[0][1].start()

    with mark("wsB"):
        for copy in [x_far[0][1], x_near[1]] + x_far[1]:
            copy.wait_send()

    @pl.when(jnp.logical_not(late))
    def _():
        give_parts[0][0].start()

    @pl.when(early)
    def _():
        for copy in give_parts[0][1:]:
            copy.start()

    @pl.when(jnp.logical_not(early))
    def _():
        with mark("wh1"):
            halo[1][1].wait_recv()
        gather_own(1)

    with mark("add"):
        add_near(0, c, keep)
    position_of(1)
    @pl.when(region < 2)
    def _():
        first_leg.start()

    yields = region == count - 2

    @pl.when(jnp.logical_and(region >= 2, jnp.logical_not(yields)))
    def _():
        give_parts[1][0].start()

    @pl.when(jnp.logical_not(yields))
    def _():
        give_parts[1][1].start()

    @pl.when(early)
    def _():
        for copy in give_parts[1][2:]:
            copy.start()

    @pl.when(region == 1)
    def _():
        for copy in give_parts[0][2:] + give_parts[1][2:]:
            copy.start()

    back_own[1].start()
    def pass_first():
        with mark("wgf0"):
            give_parts[0][0].wait_recv()
        back_other[0][0].start()

    @pl.when(jnp.logical_not(late))
    def _():
        pass_first()

    with mark("add"):
        back_own[0].wait_recv()
        add_far(0, 0)
        add_near(1, c, keep)

    @pl.when(yields)
    def _():
        for copy in give_parts[1][:2]:
            copy.start()

    @pl.when(late)
    def _():
        for note in notes[1]:
            note.wait_recv()

    with mark("wsC"):
        for copy in give_parts[0][1:2] + give_parts[1][:2]:
            copy.wait_send()

    @pl.when(late)
    def _():
        give_parts[0][0].start()


    @pl.when(region > 1)
    def _():
        for copy in give_parts[0][2:] + give_parts[1][2:]:
            copy.start()

    @pl.when(late)
    def _():
        for copy in strip:
            copy.wait_send()

    @pl.when(jnp.logical_not(late))
    def _():
        for copy in halo[1]:
            copy.wait_send()

    back_own[0].wait_send()
    with mark("wgf1"):

        @pl.when(region >= 2)
        def _():
            give_parts[1][0].wait_recv()
            back_other[1][0].start()

        give_parts[1][1].wait_recv()
        back_other[1][1].start()

    passes_on = jnp.logical_or(late, region == 2)

    @pl.when(region == 2)
    def _():
        first_leg.wait_recv()
        second_leg.start()

    @pl.when(late)
    def _():
        pass_first()

    with mark("add"):
        for copy in back_other[0]:
            copy.wait_recv()
        add_far(0, 1)
    with mark("add"):
        back_own[1].wait_recv()
        add_far(1, 0)
    for copy in [back_own[1]] + back_other[0]:
        copy.wait_send()
    with mark("wgn0"):
        for copy in give_parts[0][1:]:
            copy.wait_recv()
    with mark("add"):
        add_near(0, other_cut, give_in)
    @pl.when(late)
    def _():
        first_leg.wait_recv()
        second_leg.start()

    with mark("wgn"):
        give_parts[1][2].wait_recv()
    with mark("add"):
        add_middle(1, other_cut, give_in)
    def last_rows():
        with mark("wgn"):
            give_parts[1][3].wait_recv()
        add_end(1, other_cut, give_in)

    def last_peer_rows():
        with mark("wend"):
            for copy in back_other[1]:
                copy.wait_recv()
        add_far(1, 1)

    order = (last_peer_rows, last_rows)

    peer_first = jnp.logical_and(steps[1].upper == 1, jnp.logical_not(early))

    @pl.when(peer_first)
    def _():
        for part in order:
            part()

    @pl.when(jnp.logical_not(peer_first))
    def _():
        for part in order[::-1]:
            part()

    for copy in give_parts[0][:1] + give_parts[0][2:] + give_parts[1][2:] + back_other[1][1:]:
        copy.wait_send()

    @pl.when(region >= 2)
    def _():
        back_other[1][0].wait_send()

    @pl.when(passes_on)
    def _():
        second_leg.wait_send()


def shards(objects, probes, amplitudes, prop_phase, scan_rows, scan_cols, probe_choice):
    side = probes.shape[-1]
    rim = side // 2
    count = lax.axis_size("region")
    band = objects[0]
    band_rows, columns = band.shape[1:]
    tables = dft_blocks(side)
    whole = (2, 2, side, side)
    half = (2, 2, 2, rim, side)
    slot = lambda shape: pltpu.VMEM(shape, jnp.bfloat16)
    tall = pltpu.VMEM((2, band_rows + 2 * rim + SUBLANES, columns), jnp.float32)
    HBM = pl.BlockSpec(memory_space=pltpu.HBM)
    scalars = pltpu.SMEM(scan_rows.shape, jnp.int32)
    laid = lambda rows: pltpu.VMEM((2, side // LANES + 2, rows, LANES), jnp.float32)
    out = pl.pallas_call(
        functools.partial(wave_kernel, side, count),
        out_shape=jax.ShapeDtypeStruct(band.shape, jnp.float32),
        in_specs=[(HBM, HBM)] + [HBM] * 6,
        out_specs=VMEM,
        scratch_shapes=[
            tall,
            pltpu.VMEM(probes.shape, probes.dtype),
            pltpu.VMEM((2,) + amplitudes.shape[:2] + (rim,), jnp.float32),
            pltpu.VMEM((2, side, rim), jnp.float32),
            pltpu.VMEM((2,) + prop_phase.shape, jnp.float32),
            pltpu.VMEM(tables.shape, tables.dtype),
            pltpu.VMEM((2, side, side), jnp.float32),
            slot(whole), slot(whole), slot(half), slot(half),
            pltpu.VMEM(whole, jnp.float32), slot(whole), slot(whole), slot(whole), slot(half),
            slot((2, side // 4, side)), slot((2, rim, columns)), slot((2, rim, columns)),
            laid(side + side // 4), laid(side), laid(side - side // 4),
            (scalars,) * 2, ((scalars,) * 2,) * 2, scalars,
            pltpu.SemaphoreType.DMA((7,)),
            pltpu.SemaphoreType.DMA((16,)),
            pltpu.SemaphoreType.DMA((27,)),
        ],
        compiler_params=pltpu.CompilerParams(
            collective_id=0, has_side_effects=True, vmem_limit_bytes=32 * 1024 * 1024
        ),
    )(*jax.tree.map(
        lambda x: pltpu.with_memory_space_constraint(x, pltpu.HBM),
        ((scan_rows, scan_cols), probe_choice, band, probes, amplitudes, prop_phase, tables),
    ))
    return out[None]


def solution(mesh):
    return jax.shard_map(
        shards,
        mesh=mesh,
        in_specs=(
            P("cuts", None, "region", None),
            P(),
            P("region", None, None),
            P(),
            P("region"),
            P("region"),
            P("region"),
        ),
        out_specs=P("cuts", None, "region", None),
        check_vma=False,
    )
```
